32 devices in a mesh: group: 4 (over y, x), ctx: 8 (over z, core).
Axes of the slice: x: 2, y: 2, z: 4, core: 2. Of those that a mesh axis runs over, the one named last changes fastest.
Arguments:
- tokens: bfloat16 [4, 2048, 1024], P('group', 'ctx'), may hold values from -6 to 6
- cotangent: bfloat16 [4, 2048, 1024], P('group', 'ctx'), may hold values from -6 to 6
- block_table: int32 [4, 16], P('group'), may hold values from 0 to 15, each once within a row
- norm1_gain: bfloat16 [1024], P('ctx'), may hold values from 0.5 to 1.5
- w_query: bfloat16 [1024, 1024], P('ctx'), may hold values from -0.1875 to 0.1875
- w_key: bfloat16 [1024, 1024], P('ctx'), may hold values from -0.1875 to 0.1875
- w_value: bfloat16 [1024, 1024], P('ctx'), may hold values from -0.1875 to 0.1875
- w_out: bfloat16 [1024, 1024], P('ctx'), may hold values from -1.5 to 1.5
- norm2_gain: bfloat16 [1024], P('ctx'), may hold values from 0.5 to 1.5
- w_gate: bfloat16 [1024, 2816], P('ctx'), may hold values from -0.1875 to 0.1875
- w_up: bfloat16 [1024, 2816], P('ctx'), may hold values from -0.1875 to 0.1875
- w_down: bfloat16 [2816, 1024], P('ctx'), may hold values from -0.15625 to 0.15625
Outputs:
- output: bfloat16 [4, 2048, 1024], P('group', 'ctx')
- tokens_grad: bfloat16 [4, 2048, 1024], P('group', 'ctx')
- grad_norm1_gain: float32 [1024], P('ctx')
- grad_w_query: float32 [1024, 1024], P('ctx')
- grad_w_key: float32 [1024, 1024], P('ctx')
- grad_w_value: float32 [1024, 1024], P('ctx')
- grad_w_out: float32 [1024, 1024], P('ctx')
- grad_norm2_gain: float32 [1024], P('ctx')
- grad_w_gate: float32 [1024, 2816], P('ctx')
- grad_w_up: float32 [1024, 2816], P('ctx')
- grad_w_down: float32 [2816, 1024], P('ctx')
The draws below stay inside these ranges and needn't reach their ends.
Inputs may be any that keep to these rules, and one draw needn't show every extreme that they name: Each row of block_table names every block of the family once.
All inputs are finite; a program needn't handle non-finite values.
Results may differ from the reference program's by a relative error of at most 0.023.
Values may be sent and summed in bfloat16 or wider, within the bound.
A program may use at most 256 MiB of HBM per device.

```python
import jax
import jax.numpy as jnp
from jax import lax

D = 1024
HEADS = 16
HEAD = 64
FF = 2816
BLK = 128
KEYBLK = 512
CONT = 256
GROUPS = 4
TOKS = 2048
PROMPT = 1024
NBLK = 16


def block_scale(stream_key, extent, cuts, least, high):
    def one(dim, blocks):
        steps = jax.random.uniform(jax.random.fold_in(jax.random.fold_in(stream_key, 6), dim), (blocks,), jnp.float32, least / len(cuts), high / len(cuts))
        return jnp.repeat(jnp.exp(steps), extent[dim] // blocks).reshape((-1,) + (1,) * (len(extent) - dim - 1))

    level = one(*cuts[0])
    for cut in cuts[1:]:
        level = level * one(*cut)
    return level


def gaussian(rng, dims, deviation, bound, cuts=(), held_as=jnp.bfloat16):
    drawn = jax.random.normal(rng, dims, jnp.float32) * deviation
    if len(cuts) > 0:
        drawn = block_scale(rng, dims, cuts, -0.22, 0.18) * drawn
    return jnp.clip(drawn, min=-bound, max=bound).astype(held_as)


def setup_inputs(seed: int = 0) -> dict:
    seeds = jax.random.split(jax.random.key(seed), 13)
    tokens = gaussian(seeds[0], (GROUPS, TOKS, D), 1.0, 6.0, ((0, 4), (1, 8)))
    cotangent = gaussian(seeds[1], (GROUPS, TOKS, D), 1.0, 6.0, ((0, 4), (1, 8)))
    block_table = jax.vmap(lambda own: jax.random.permutation(own, NBLK))(jax.random.split(seeds[2], GROUPS)).reshape((GROUPS, NBLK)).astype(jnp.int32)
    norm1_gain = jnp.clip(1.0 + 0.1 * jax.random.normal(seeds[3], (D,), jnp.float32), 0.5, 1.5).astype(jnp.bfloat16)
    w_query = gaussian(seeds[4], (D, D), D ** -0.5, 0.1875, ((0, 8),))
    w_key = gaussian(seeds[5], (D, D), D ** -0.5, 0.1875, ((0, 8),))
    w_value = gaussian(seeds[6], (D, D), D ** -0.5, 0.1875, ((0, 8),))
    w_out = gaussian(seeds[7], (D, D), (D // 64) ** -0.5, 1.5, ((0, 8),))
    norm2_gain = jnp.clip(1.0 + 0.1 * jax.random.normal(seeds[8], (D,), jnp.float32), 0.5, 1.5).astype(jnp.bfloat16)
    w_gate = gaussian(seeds[9], (D, FF), D ** -0.5, 0.1875, ((0, 8),))
    w_up = gaussian(seeds[10], (D, FF), D ** -0.5, 0.1875, ((0, 8),))
    w_down = gaussian(seeds[11], (FF, D), (FF // 2) ** -0.5, 0.15625, ((0, 8),))
    return {"tokens": tokens, "cotangent": cotangent, "block_table": block_table, "norm1_gain": norm1_gain, "w_query": w_query, "w_key": w_key, "w_value": w_value, "w_out": w_out, "norm2_gain": norm2_gain, "w_gate": w_gate, "w_up": w_up, "w_down": w_down}


EPS = 1e-06
SCALE = 0.125
HIGH = lax.Precision.HIGHEST

@jax.custom_vjp
def low(v):
    return lax.optimization_barrier(v.astype(jnp.bfloat16)).astype(jnp.float32)

@jax.custom_vjp
def low_back(v):
    return v

def low_keep(v):
    return (low(v), None)

def low_pass(kept, grad):
    return (grad,)

def back_keep(v):
    return (v, None)

def back_low(kept, grad):
    return (low(grad),)
low.defvjp(low_keep, low_pass)
low_back.defvjp(back_keep, back_low)

def rms_scale(hidden, gain):
    return hidden * lax.rsqrt(lax.optimization_barrier(jnp.mean(hidden * hidden, axis=-1, keepdims=True)) + EPS) * gain

def gated(gate, upper):
    return jax.nn.gelu(gate, approximate=True) * upper

def matmul(left, right):
    return jnp.dot(left, right, precision=HIGH)

def family_index(table):
    offsets = jnp.arange(BLK, dtype=jnp.int32)
    return (table.astype(jnp.int32)[:, None] * BLK + offsets[None, :]).reshape(-1).astype(jnp.int32)

def segment_of(index):
    return jnp.where(index < PROMPT, 0, 1 + (index - PROMPT) // CONT)

def allowed(query_index, key_index):
    query_seg = segment_of(query_index)
    key_seg = segment_of(key_index)
    same = (query_seg[:, None] == key_seg[None, :]) & (key_index[None, :] <= query_index[:, None])
    prompt = (key_seg[None, :] == 0) & (query_seg[:, None] > 0)
    return same | prompt

def layer(inputs, gain1, w_query, w_key, w_value, w_out, gain2, w_gate, w_up, w_down, index):
    row_count = inputs.shape[0]
    normed = low(rms_scale(inputs, gain1))
    queries = low(low_back(matmul(normed, w_query)))
    keys = low(low_back(matmul(normed, w_key)))
    values = low(low_back(matmul(normed, w_value)))
    key_heads = keys.reshape(row_count, HEADS, HEAD)
    value_heads = values.reshape(row_count, HEADS, HEAD)

    def block(pair):
        query_block, query_index = pair
        score = low_back(jnp.einsum('qhd,khd->hqk', query_block, key_heads, precision=HIGH) * SCALE)
        keep = allowed(query_index, index)
        weight = jax.nn.softmax(jnp.where(keep[None], score, -1e+30), axis=-1)
        return jnp.einsum('hqk,khd->qhd', low(weight), value_heads, precision=HIGH)
    blocks = row_count // KEYBLK
    attended = lax.map(jax.checkpoint(block), (queries.reshape(blocks, KEYBLK, HEADS, HEAD), index.reshape(blocks, KEYBLK)))
    attended = low(low_back(attended.reshape(row_count, HEADS * HEAD)))
    hidden = inputs + low_back(matmul(attended, w_out))
    normed2 = low(rms_scale(hidden, gain2))
    gate = low_back(matmul(normed2, w_gate))
    upper = low_back(matmul(normed2, w_up))
    mixed = low(gated(gate, upper))
    return hidden + low_back(matmul(mixed, w_down))

def reference(tokens, cotangent, block_table, norm1_gain, w_query, w_key, w_value, w_out, norm2_gain, w_gate, w_up, w_down):
    weights = tuple((item.astype(jnp.float32) for item in (norm1_gain, w_query, w_key, w_value, w_out, norm2_gain, w_gate, w_up, w_down)))

    def family(totals, item):
        inputs, grad_out, table = item
        index = family_index(table)

        def forward(source, gain1, wq_full, wk_full, wv_full, wo_full, gain2, wg_full, wu_full, wd_full):
            return layer(source, gain1, wq_full, wk_full, wv_full, wo_full, gain2, wg_full, wu_full, wd_full, index)
        result, pull = jax.vjp(forward, inputs.astype(jnp.float32), *weights)
        grads = pull(grad_out.astype(jnp.float32))
        totals = tuple((total + grad for total, grad in zip(totals, grads[1:])))
        return (totals, (result.astype(jnp.bfloat16), grads[0].astype(jnp.bfloat16)))
    zeros = tuple((jnp.zeros(item.shape, jnp.float32) for item in weights))
    totals, (output, tokens_grad) = lax.scan(family, zeros, (tokens, cotangent, block_table))
    return (output, tokens_grad, totals[0], totals[1], totals[2], totals[3], totals[4], totals[5], totals[6], totals[7], totals[8])
```

```python
import jax
import jax.numpy as jnp
from jax import lax
from jax.experimental import pallas as pl
from jax.experimental.pallas import tpu as pltpu
from jax.sharding import Mesh
from jax.sharding import PartitionSpec as P

HEADS = 16
HEAD = 64
BLK = 128
KEYBLK = 512
PROMPT_MAX = 2048
CONT = 256


EPS = 1e-06
SCALE = 0.125


def rms_scale(hidden, gain):
    return hidden * lax.rsqrt(jnp.mean(hidden * hidden, axis=-1, keepdims=True) + EPS) * gain


def gated(gate, upper):
    return jax.nn.gelu(gate, approximate=True) * upper


def matmul(left, right):
    return jnp.dot(left, right, preferred_element_type=jnp.float32)


def inner(left, right):
    return lax.dot_general(
        left, right, (((0,), (0,)), ((), ())), preferred_element_type=jnp.float32
    )


def outer(left, right):
    return lax.dot_general(
        left, right, (((1,), (1,)), ((), ())), preferred_element_type=jnp.float32
    )


def family_index(table):
    offsets = jnp.arange(BLK, dtype=jnp.int32)
    return (table[:, None] * BLK + offsets[None, :]).reshape(-1)


def segment_of(index, prompt_len):
    return jnp.where(index < prompt_len, 0, 1 + (index - prompt_len) // CONT)


def allowed(query_index, key_index, prompt_len):
    query_seg = segment_of(query_index, prompt_len)
    key_seg = segment_of(key_index, prompt_len)
    same = (query_seg[:, None] == key_seg[None, :]) & (key_index[None, :] <= query_index[:, None])
    prompt = (key_seg[None, :] == 0) & (query_seg[:, None] > 0)
    return same | prompt


def head_split(block):
    return block.reshape(block.shape[0], HEADS, HEAD)


def scores_of(query_heads, key_block, query_index, key_index, prompt_len):
    score = (
        jnp.einsum(
            "qhd,khd->hqk", query_heads, head_split(key_block), preferred_element_type=jnp.float32
        )
        * SCALE
    )
    return (score, allowed(query_index, key_index, prompt_len))


def attend_stats(queries, keys, query_index, key_index, prompt_len):
    query_heads = head_split(queries)

    def step(carry, number):
        best, total = carry
        start = number * KEYBLK
        key_block = lax.dynamic_slice_in_dim(keys, start, KEYBLK, 0)
        block_index = lax.dynamic_slice_in_dim(key_index, start, KEYBLK, 0)
        score, keep = scores_of(query_heads, key_block, query_index, block_index, prompt_len)
        score = jnp.where(keep[None], score, -1e30)
        larger = jnp.maximum(best, jnp.max(score, axis=-1))
        terms = jnp.where(keep[None], jnp.exp(score - larger[:, :, None]), 0.0)
        total = total * jnp.exp(best - larger) + jnp.sum(terms, axis=-1)
        return ((larger, total), None)

    start_best = jnp.full((HEADS, queries.shape[0]), -1e30, jnp.float32)
    (best, total), ignored = lax.scan(
        step, (start_best, jnp.zeros_like(start_best)), jnp.arange(keys.shape[0] // KEYBLK)
    )
    return best + jnp.log(total)


def attend_values(queries, keys, values, lse, query_index, key_index, prompt_len):
    query_heads = head_split(queries)

    def step(acc, number):
        start = number * KEYBLK
        key_block = lax.dynamic_slice_in_dim(keys, start, KEYBLK, 0)
        value_block = lax.dynamic_slice_in_dim(values, start, KEYBLK, 0)
        block_index = lax.dynamic_slice_in_dim(key_index, start, KEYBLK, 0)
        score, keep = scores_of(query_heads, key_block, query_index, block_index, prompt_len)
        prob = jnp.where(keep[None], jnp.exp(score - lse[:, :, None]), 0.0).astype(jnp.bfloat16)
        return (
            acc
            + jnp.einsum(
                "hqk,khd->qhd", prob, head_split(value_block), preferred_element_type=jnp.float32
            ),
            None,
        )

    start_acc = jnp.zeros((queries.shape[0], HEADS, HEAD), jnp.float32)
    acc, ignored = lax.scan(step, start_acc, jnp.arange(keys.shape[0] // KEYBLK))
    return acc.reshape(queries.shape[0], HEADS * HEAD)


def block_grads(query_heads, grad_heads, key_block, value_block, lse, delta, keep):
    key_heads = head_split(key_block)
    value_heads = head_split(value_block)
    score = (
        jnp.einsum("qhd,khd->hqk", query_heads, key_heads, preferred_element_type=jnp.float32)
        * SCALE
    )
    prob = jnp.where(keep[None], jnp.exp(score - lse[:, :, None]), 0.0)
    dvalue = jnp.einsum(
        "hqk,qhd->khd", prob.astype(jnp.bfloat16), grad_heads, preferred_element_type=jnp.float32
    )
    dprob = jnp.einsum("qhd,khd->hqk", grad_heads, value_heads, preferred_element_type=jnp.float32)
    dscore = (prob * (dprob - delta[:, :, None])).astype(jnp.bfloat16)
    dquery = (
        jnp.einsum("hqk,khd->qhd", dscore, key_heads, preferred_element_type=jnp.float32) * SCALE
    )
    dkey = (
        jnp.einsum("hqk,qhd->khd", dscore, query_heads, preferred_element_type=jnp.float32) * SCALE
    )
    return (dquery, dkey, dvalue)


def local(
    tokens,
    cotangent,
    block_table,
    norm1_gain,
    w_query,
    w_key,
    w_value,
    w_out,
    norm2_gain,
    w_gate,
    w_up,
    w_down,
):
    row_count = tokens.shape[1]
    width = tokens.shape[2]
    every_index = family_index(block_table[0])
    prompt_len = min(PROMPT_MAX, every_index.shape[0] // 2)
    own_index = lax.dynamic_slice_in_dim(
        every_index, lax.axis_index("ctx") * row_count, row_count, 0
    )
    gain1, wq_full, wk_full, wv_full, wo_full = (
        lax.all_gather(norm1_gain, "ctx", axis=0, tiled=True),
        lax.all_gather(w_query, "ctx", axis=0, tiled=True),
        lax.all_gather(w_key, "ctx", axis=0, tiled=True),
        lax.all_gather(w_value, "ctx", axis=0, tiled=True),
        lax.all_gather(w_out, "ctx", axis=0, tiled=True),
    )
    inputs = tokens[0].astype(jnp.float32)
    normed1, norm1_pull = jax.vjp(rms_scale, inputs, gain1.astype(jnp.float32))
    first_low = normed1.astype(jnp.bfloat16)
    queries = matmul(first_low, wq_full).astype(jnp.bfloat16)
    keys_own = matmul(first_low, wk_full).astype(jnp.bfloat16)
    values_own = matmul(first_low, wv_full).astype(jnp.bfloat16)
    keys_all, values_all = (
        lax.all_gather(keys_own, "ctx", axis=0, tiled=True),
        lax.all_gather(values_own, "ctx", axis=0, tiled=True),
    )
    lse = attend_stats(queries, keys_all, own_index, every_index, prompt_len)
    attended_wide = attend_values(
        queries, keys_all, values_all, lse, own_index, every_index, prompt_len
    )
    attended = attended_wide.astype(jnp.bfloat16)
    hidden = inputs + matmul(attended, wo_full)
    gain2, wg_full, wu_full, wd_full = (
        lax.all_gather(norm2_gain, "ctx", axis=0, tiled=True),
        lax.all_gather(w_gate, "ctx", axis=0, tiled=True),
        lax.all_gather(w_up, "ctx", axis=0, tiled=True),
        lax.all_gather(w_down, "ctx", axis=0, tiled=True),
    )
    normed2, norm2_pull = jax.vjp(rms_scale, hidden, gain2.astype(jnp.float32))
    second_low = normed2.astype(jnp.bfloat16)
    gate = matmul(second_low, wg_full)
    upper = matmul(second_low, wu_full)
    mixed_wide, gate_pull = jax.vjp(gated, gate, upper)
    mixed = mixed_wide.astype(jnp.bfloat16)
    result = hidden + matmul(mixed, wd_full)
    output = result.astype(jnp.bfloat16)[None]
    grad_low = cotangent[0]
    grad_down = inner(mixed, grad_low)
    dmixed = outer(grad_low, wd_full)
    dgate, dupper = gate_pull(dmixed)
    dgate_low = dgate.astype(jnp.bfloat16)
    dupper_low = dupper.astype(jnp.bfloat16)
    grad_gate = inner(second_low, dgate_low)
    grad_up = inner(second_low, dupper_low)
    dnormed2 = outer(dgate_low, wg_full) + outer(dupper_low, wu_full)
    dhidden_norm, grad_gain2 = norm2_pull(dnormed2)
    dhidden = grad_low.astype(jnp.float32) + dhidden_norm
    attn_low = dhidden.astype(jnp.bfloat16)
    grad_out_w = inner(attended, attn_low)
    dattended = outer(attn_low, wo_full).astype(jnp.bfloat16)
    delta = jnp.sum(
        (dattended.astype(jnp.float32) * attended_wide).reshape(row_count, HEADS, HEAD), axis=-1
    ).T
    query_heads = head_split(queries)
    grad_heads = head_split(dattended)

    def key_step(carry, number):
        start = number * KEYBLK
        key_block = lax.dynamic_slice_in_dim(keys_all, start, KEYBLK, 0)
        value_block = lax.dynamic_slice_in_dim(values_all, start, KEYBLK, 0)
        block_index = lax.dynamic_slice_in_dim(every_index, start, KEYBLK, 0)
        keep = allowed(own_index, block_index, prompt_len)
        dquery, dkey, dvalue = block_grads(
            query_heads, grad_heads, key_block, value_block, lse, delta, keep
        )
        joined = jnp.concatenate(
            [dkey.reshape(KEYBLK, width), dvalue.reshape(KEYBLK, width)], axis=1
        )
        return (carry + dquery, joined)

    start_query = jnp.zeros((row_count, HEADS, HEAD), jnp.float32)
    query_sum, key_terms = lax.scan(
        key_step, start_query, jnp.arange(every_index.shape[0] // KEYBLK)
    )
    summed = lax.psum_scatter(
        key_terms.reshape(every_index.shape[0], 2 * width).astype(jnp.bfloat16),
        "ctx",
        scatter_dimension=0,
        tiled=True,
    ).astype(jnp.float32)
    query_grad = query_sum.reshape(row_count, width)
    key_grad = summed[:, :width]
    value_grad = summed[:, width:]
    query_low = query_grad.astype(jnp.bfloat16)
    key_low = key_grad.astype(jnp.bfloat16)
    value_low = value_grad.astype(jnp.bfloat16)
    grad_query = inner(first_low, query_low)
    grad_key = inner(first_low, key_low)
    grad_value = inner(first_low, value_low)
    dnormed1 = outer(query_low, wq_full) + outer(key_low, wk_full) + outer(value_low, wv_full)
    dinput_norm, grad_gain1 = norm1_pull(dnormed1)
    tokens_grad = (dhidden + dinput_norm).astype(jnp.bfloat16)[None]
    shards = (
        lax.psum_scatter(
            grad_gain1.astype(jnp.bfloat16), "ctx", scatter_dimension=0, tiled=True
        ).astype(jnp.float32),
        lax.psum_scatter(
            grad_query.astype(jnp.bfloat16), "ctx", scatter_dimension=0, tiled=True
        ).astype(jnp.float32),
        lax.psum_scatter(
            grad_key.astype(jnp.bfloat16), "ctx", scatter_dimension=0, tiled=True
        ).astype(jnp.float32),
        lax.psum_scatter(
            grad_value.astype(jnp.bfloat16), "ctx", scatter_dimension=0, tiled=True
        ).astype(jnp.float32),
        lax.psum_scatter(
            grad_out_w.astype(jnp.bfloat16), "ctx", scatter_dimension=0, tiled=True
        ).astype(jnp.float32),
        lax.psum_scatter(
            grad_gain2.astype(jnp.bfloat16), "ctx", scatter_dimension=0, tiled=True
        ).astype(jnp.float32),
        lax.psum_scatter(
            grad_gate.astype(jnp.bfloat16), "ctx", scatter_dimension=0, tiled=True
        ).astype(jnp.float32),
        lax.psum_scatter(
            grad_up.astype(jnp.bfloat16), "ctx", scatter_dimension=0, tiled=True
        ).astype(jnp.float32),
        lax.psum_scatter(
            grad_down.astype(jnp.bfloat16), "ctx", scatter_dimension=0, tiled=True
        ).astype(jnp.float32),
    )
    shards = (
        lax.psum(shards[0].astype(jnp.bfloat16), "group").astype(jnp.float32),
        lax.psum(shards[1].astype(jnp.bfloat16), "group").astype(jnp.float32),
        lax.psum(shards[2].astype(jnp.bfloat16), "group").astype(jnp.float32),
        lax.psum(shards[3].astype(jnp.bfloat16), "group").astype(jnp.float32),
        lax.psum(shards[4].astype(jnp.bfloat16), "group").astype(jnp.float32),
        lax.psum(shards[5].astype(jnp.bfloat16), "group").astype(jnp.float32),
        lax.psum(shards[6].astype(jnp.bfloat16), "group").astype(jnp.float32),
        lax.psum(shards[7].astype(jnp.bfloat16), "group").astype(jnp.float32),
        lax.psum(shards[8].astype(jnp.bfloat16), "group").astype(jnp.float32),
    )
    return (
        output,
        tokens_grad,
        shards[0],
        shards[1],
        shards[2],
        shards[3],
        shards[4],
        shards[5],
        shards[6],
        shards[7],
        shards[8],
    )


PLANE = 4
CORES = 2
TP = ("group", "core")
F32 = jnp.float32
BF16 = jnp.bfloat16


def dot_nt(left, right):
    return lax.dot_general(left, right, (((1,), (1,)), ((), ())), preferred_element_type=F32)


def place_rows(table_ref, blocks, chunk):
    for stored in range(blocks):
        line, core, half = stored // 4, (stored // 2) % 2, stored % 2
        start = table_ref[stored] * BLK
        for part in range(2):
            plane = 2 * half + part
            row = ((plane * CORES + core) * PLANE + line) * chunk
            yield row, pl.multiple_of(start + part * chunk, chunk)


def head_mask(rows, head):
    lane = lax.broadcasted_iota(jnp.int32, (rows, 2 * HEAD), 1)
    return (lane >= head * HEAD) & (lane < (head + 1) * HEAD)


def causal_mask():
    key = lax.broadcasted_iota(jnp.int32, (CONT, CONT), 0)
    query = lax.broadcasted_iota(jnp.int32, (CONT, CONT), 1)
    return key <= query


def attend_kernel(table_ref, qkv_ref, att_ref, lse_ref, ot_ref, qs, ks, vs, vt, att):
    total = qkv_ref.shape[0]
    chunk = BLK // 2
    width = 2 * HEAD
    for row, place in place_rows(table_ref, total // BLK, chunk):
        for number, ref in enumerate((qs, ks, vs)):
            block = qkv_ref[row : row + chunk, number * width : (number + 1) * width]
            ref[pl.ds(place, chunk), :] = block * jnp.bfloat16(SCALE) if number == 0 else block

    @pl.loop(0, total // CONT)
    def _(number):
        start = pl.multiple_of(number * CONT, CONT)
        vt[:, pl.ds(start, CONT)] = vs[pl.ds(start, CONT), :].astype(F32).T.astype(BF16)

    def one(start, before):
        query = qs[pl.ds(start, CONT), :]
        outs = []
        for head in range(2):
            masked = jnp.where(head_mask(CONT, head), query, jnp.zeros_like(query))
            own = dot_nt(ks[pl.ds(start, CONT), :], masked)
            own = jnp.where(causal_mask(), own, -1e30)
            best = jnp.max(own, axis=0, keepdims=True)
            if before:
                past = dot_nt(ks[0:before, :], masked)
                best = jnp.maximum(best, jnp.max(past, axis=0, keepdims=True))
            terms = jnp.exp(own - best)
            total_terms = jnp.sum(terms, axis=0, keepdims=True)
            rows = slice(head * HEAD, (head + 1) * HEAD)
            out = matmul(vt[rows, pl.ds(start, CONT)], terms.astype(BF16))
            if before:
                terms = jnp.exp(past - best)
                total_terms = total_terms + jnp.sum(terms, axis=0, keepdims=True)
                out = out + matmul(vt[rows, 0:before], terms.astype(BF16))
            outs.append(out / total_terms)
            lse_ref[head : head + 1, pl.ds(start, CONT)] = best + jnp.log(total_terms)
        joined = jnp.concatenate(outs, axis=0)
        ot_ref[:, pl.ds(start, CONT)] = joined.astype(BF16)
        att[pl.ds(start, CONT), :] = joined.T.astype(BF16)

    prompt = total // 2
    for number in range(prompt // CONT):
        one(number * CONT, number * CONT)

    @pl.loop(prompt // CONT, total // CONT)
    def _(number):
        one(pl.multiple_of(number * CONT, CONT), prompt)

    for row, place in place_rows(table_ref, total // BLK, chunk):
        att_ref[row : row + chunk, :] = att[pl.ds(place, chunk), :]


def attend_grad_kernel(
    table_ref, qkv_ref, datt_ref, lse_ref, ot_ref, out_ref, qs, ks, vs, gs, kt, dqs, dks, dvs
):
    total = qkv_ref.shape[0]
    chunk = BLK // 2
    width = 2 * HEAD
    for row, place in place_rows(table_ref, total // BLK, chunk):
        for number, ref in enumerate((qs, ks, vs)):
            block = qkv_ref[row : row + chunk, number * width : (number + 1) * width]
            ref[pl.ds(place, chunk), :] = block * jnp.bfloat16(SCALE) if number == 0 else block
        gs[pl.ds(place, chunk), :] = datt_ref[row : row + chunk, :]

    @pl.loop(0, total // CONT)
    def _(number):
        start = pl.multiple_of(number * CONT, CONT)
        kt[:, pl.ds(start, CONT)] = ks[pl.ds(start, CONT), :].astype(F32).T.astype(BF16)

    dks[...] = jnp.zeros_like(dks)
    dvs[...] = jnp.zeros_like(dvs)

    def one(start, before):
        query = qs[pl.ds(start, CONT), :]
        grad = gs[pl.ds(start, CONT), :]
        product = grad.astype(F32).T * ot_ref[:, pl.ds(start, CONT)].astype(F32)
        outs = []
        for head in range(2):
            rows = slice(head * HEAD, (head + 1) * HEAD)
            delta = jnp.sum(product[rows], axis=0, keepdims=True)
            lse = lse_ref[head : head + 1, pl.ds(start, CONT)]
            keep = head_mask(CONT, head)
            query_head = jnp.where(keep, query, jnp.zeros_like(query))
            grad_head = jnp.where(keep, grad, jnp.zeros_like(grad))
            parts = [(pl.ds(start, CONT), True)]
            if before:
                parts.append((pl.ds(0, before), False))
            dq = None
            for keys, diagonal in parts:
                prob = jnp.exp(dot_nt(ks[keys, :], query_head) - lse)
                if diagonal:
                    prob = jnp.where(causal_mask(), prob, 0.0)
                dprob = dot_nt(vs[keys, :], grad_head)
                dscore = (prob * (dprob - delta)).astype(BF16)
                dvs[keys, :] += matmul(prob.astype(BF16), grad_head)
                dks[keys, :] += matmul(dscore, query_head)
                term = matmul(kt[rows, keys], dscore)
                dq = term if dq is None else dq + term
            outs.append(dq)
        joined = jnp.concatenate(outs, axis=0) * SCALE
        dqs[pl.ds(start, CONT), :] = joined.T.astype(BF16)

    prompt = total // 2
    for number in range(prompt // CONT):
        one(number * CONT, number * CONT)

    @pl.loop(prompt // CONT, total // CONT)
    def _(number):
        one(pl.multiple_of(number * CONT, CONT), prompt)

    for row, place in place_rows(table_ref, total // BLK, chunk):
        out_ref[row : row + chunk, 0:width] = dqs[pl.ds(place, chunk), :]
        out_ref[row : row + chunk, width : 2 * width] = dks[pl.ds(place, chunk), :].astype(BF16)
        out_ref[row : row + chunk, 2 * width :] = dvs[pl.ds(place, chunk), :].astype(BF16)


def vmem(count):
    return [pl.BlockSpec(memory_space=pltpu.VMEM)] * count


def attend(table, qkv):
    total, width = qkv.shape[0], 2 * HEAD
    return pl.pallas_call(
        attend_kernel,
        out_shape=(
            jax.ShapeDtypeStruct((total, width), BF16),
            jax.ShapeDtypeStruct((2, total), F32),
            jax.ShapeDtypeStruct((width, total), BF16),
        ),
        in_specs=[pl.BlockSpec(memory_space=pltpu.SMEM)] + vmem(1),
        out_specs=tuple(vmem(3)),
        scratch_shapes=[pltpu.VMEM((total, width), BF16)] * 3
        + [pltpu.VMEM((width, total), BF16), pltpu.VMEM((total, width), BF16)],
        compiler_params=pltpu.CompilerParams(vmem_limit_bytes=40 << 20),
        name="attend",
    )(table, qkv)


def attend_grad(table, qkv, datt, lse, ot):
    total, width = qkv.shape[0], 2 * HEAD
    return pl.pallas_call(
        attend_grad_kernel,
        out_shape=jax.ShapeDtypeStruct((total, 3 * width), BF16),
        in_specs=[pl.BlockSpec(memory_space=pltpu.SMEM)] + vmem(4),
        out_specs=vmem(1)[0],
        scratch_shapes=[pltpu.VMEM((total, width), BF16)] * 4
        + [pltpu.VMEM((width, total), BF16), pltpu.VMEM((total, width), BF16)]
        + [pltpu.VMEM((total, width), F32)] * 2,
        compiler_params=pltpu.CompilerParams(vmem_limit_bytes=50 << 20),
        name="attend_grad",
    )(table, qkv, datt, lse, ot)


MESH = pl.DeviceIdType.MESH
COPIES = 128


def spots():
    chip, line, core = lax.axis_index("group"), lax.axis_index("z"), lax.axis_index("core")
    side = chip + 1 - 2 * lax.rem(chip, 2)
    over = lax.rem(chip + 2, PLANE)
    far = PLANE - 1 - chip
    return chip, line, core, side, over, far


def plane_partners():
    chip, line, core, side, over, far = spots()
    return [(q, line, core) for q in (far, side, over)]


def line_partners():
    chip, line, core, side, over, far = spots()
    lines = [lax.rem(line + d, PLANE) for d in range(1, PLANE)]
    same = [(chip, z, core) for z in lines]
    return same + [(chip, z, 1 - core) for z in lines] + [(chip, line, 1 - core)]


class Copies:
    def __init__(self, sems):
        self.sems, self.count, self.started = sems, 0, []

    def number(self):
        self.count += 1
        return self.count - 1

    def enter(self):
        barrier = pltpu.get_barrier_semaphore()
        partners = plane_partners() + line_partners()
        for partner in partners:
            pl.semaphore_signal(barrier, inc=1, device_id=partner, device_id_type=MESH)
        pl.semaphore_wait(barrier, len(partners))

    def send(self, source, target, partner):
        number = self.number()
        copy = pltpu.make_async_remote_copy(
            src_ref=source,
            dst_ref=target,
            send_sem=self.sems.at[0, number],
            recv_sem=self.sems.at[1, number],
            device_id=partner,
            device_id_type=MESH,
        )
        copy.start()
        self.started.append(copy)
        return copy

    def keep(self, source, target):
        copy = pltpu.make_async_copy(source, target, self.sems.at[0, self.number()])
        copy.start()
        return copy

    def finish(self):
        for copy in self.started:
            copy.wait_send()


def arrived(copies):
    for copy in copies:
        copy.wait_recv()


def finished(copies):
    for copy in copies:
        copy.wait()


def gather_stream(copies, own_ref, out_ref, twin=True):
    chip, line, core, side, over, far = spots()
    half = own_ref.shape[0] // 2
    to_far, to_side, to_over = plane_partners()
    to_twin = (chip, line, 1 - core)

    def slot_of(q):
        return CORES * q + core if twin else q

    def part(slot, number):
        return out_ref.at[slot, pl.ds(number * half, half)]

    def own(number):
        return own_ref.at[pl.ds(number * half, half)]

    def on(slot, number, partner):
        return copies.send(part(slot, number), part(slot, number), partner)

    def share(slot, number):
        return [on(slot, number, to_twin)] if twin else []

    mine, slot_side, slot_over, slot_far = map(slot_of, (chip, side, over, far))
    sides, overs = [None, None], [None, None]
    overs[0] = copies.send(own(0), part(mine, 0), to_over)
    sides[1] = copies.send(own(1), part(mine, 1), to_side)
    sides[0] = copies.send(own(0), part(mine, 0), to_side)
    overs[1] = copies.send(own(1), part(mine, 1), to_over)
    twins = [copies.send(own(h), part(mine, h), to_twin) for h in range(2)] if twin else []
    local = copies.keep(own_ref, out_ref.at[mine])
    yield
    overs[0].wait_recv()
    far0 = on(slot_over, 0, to_side)
    twins += share(slot_over, 0)
    sides[1].wait_recv()
    far1 = on(slot_side, 1, to_over)
    twins += share(slot_side, 1)
    yield
    sides[0].wait_recv()
    twins += share(slot_side, 0)
    overs[1].wait_recv()
    twins += share(slot_over, 1)
    yield
    far0.wait_recv()
    twins += share(slot_far, 0)
    far1.wait_recv()
    twins += share(slot_far, 1)
    arrived(twins)
    local.wait()
    yield


def scatter_stream(copies, part_ref, out_ref, scratch):
    twin, mine, from_side, from_over, go = scratch
    chip, line, core, side, over, far = spots()
    rows = out_ref.shape[0]
    half = rows // 2
    to_far, to_side, to_over = plane_partners()
    to_twin = (chip, line, 1 - core)
    twins, locals_ = [], []
    for n, q in enumerate((far, side, over, chip)):
        slot = CORES * q + (1 - core)
        twins.append([])
        for h in range(2):
            half_rows = pl.ds(h * half, half)
            twins[n].append(copies.send(part_ref.at[slot, half_rows], twin.at[n, half_rows], to_twin))
        locals_.append(copies.keep(part_ref.at[CORES * q + core], mine.at[n]))
    yield

    def pair(n, h):
        part = slice(h * half, (h + 1) * half)
        twins[n][h].wait_recv()
        return mine[n, part].astype(F32) + twin[n, part].astype(F32)

    def put(n, h, value):
        part = slice(h * half, (h + 1) * half)
        go[n, part] = value.astype(BF16)
        return go.at[n, pl.ds(h * half, half)]

    locals_[0].wait()
    far0 = copies.send(put(0, 0, pair(0, 0)), from_side.at[0], to_side)
    far1 = copies.send(put(0, 1, pair(0, 1)), from_over.at[0], to_over)
    locals_[1].wait()
    side0 = copies.send(put(1, 0, pair(1, 0)), from_side.at[1], to_side)
    locals_[2].wait()
    over1 = copies.send(put(2, 1, pair(2, 1)), from_over.at[2], to_over)
    yield
    value = pair(2, 0)
    far0.wait_recv()
    over0 = copies.send(put(2, 0, value + from_side[0].astype(F32)), from_over.at[1], to_over)
    value = pair(1, 1)
    far1.wait_recv()
    side1 = copies.send(put(1, 1, value + from_over[0].astype(F32)), from_side.at[2], to_side)
    yield
    locals_[3].wait()
    first, second = pair(3, 0), pair(3, 1)
    side0.wait_recv()
    first = first + from_side[1].astype(F32)
    over1.wait_recv()
    second = second + from_over[2].astype(F32)
    over0.wait_recv()
    out_ref[0:half] = first + from_over[1].astype(F32)
    side1.wait_recv()
    out_ref[half:rows] = second + from_side[2].astype(F32)
    yield


def scatter_scratch(rows, width):
    return [
        pltpu.VMEM((PLANE, rows, width), BF16),
        pltpu.VMEM((PLANE, rows, width), BF16),
        pltpu.VMEM((3, rows // 2, width), BF16),
        pltpu.VMEM((3, rows // 2, width), BF16),
        pltpu.VMEM((3, rows, width), BF16),
    ]


def inward_stream(copies, own_ref, mid, out_ref):
    chip, line, core, side, over, far = spots()
    chunk = own_ref.shape[0] // PLANE

    def rows(q):
        return own_ref.at[pl.ds(q * chunk, chunk)]

    sent = [copies.send(rows(q[0]), mid.at[chip], q) for q in plane_partners()]
    local = copies.keep(rows(chip), mid.at[chip])
    yield
    local.wait()
    arrived(sent)
    moved = [copies.send(mid.at[q[1]], out_ref.at[line], q) for q in line_partners()[: PLANE - 1]]
    local = copies.keep(mid.at[line], out_ref.at[line])
    yield
    arrived(moved)
    local.wait()
    yield


def outward_stream(copies, own_ref, mid, out_ref):
    chip, line, core, side, over, far = spots()
    chunk = own_ref.shape[1]
    moved = [copies.send(own_ref.at[q[1]], mid.at[line], q) for q in line_partners()[: PLANE - 1]]
    local = copies.keep(own_ref.at[line], mid.at[line])
    yield
    local.wait()
    arrived(moved)
    target = out_ref.at[pl.ds(chip * chunk, chunk)]
    sent = [copies.send(mid.at[q[0]], target, q) for q in plane_partners()]
    local = copies.keep(mid.at[chip], target)
    yield
    arrived(sent)
    local.wait()
    yield


def columns_stream(copies, piece_ref, out_ref):
    chip, line, core, side, over, far = spots()
    mine = out_ref.at[CORES * line + core]
    sent = [copies.send(piece_ref.at[q[2]], mine, q) for q in line_partners()]
    local = copies.keep(piece_ref.at[core], mine)
    yield
    arrived(sent)
    local.wait()
    yield


def rows_stream(copies, shard_ref, mid, out_ref):
    chip, line, core, side, over, far = spots()
    width = shard_ref.shape[1] // PLANE
    quarter = pl.ds(pl.multiple_of(chip * width, width), width)
    sent = [copies.send(shard_ref.at[:, quarter], mid.at[line], q) for q in line_partners()[: PLANE - 1]]
    local = copies.keep(shard_ref.at[:, quarter], mid.at[line])
    yield
    local.wait()
    arrived(sent)
    sent = [copies.send(mid.at[q[0]], out_ref.at[:, quarter], q) for q in plane_partners()]
    local = copies.keep(mid.at[chip], out_ref.at[:, quarter])
    yield
    arrived(sent)
    local.wait()
    yield


def unit_rows(value):
    inverse = lax.rsqrt(jnp.mean(value * value, axis=-1, keepdims=True) + EPS)
    return value * inverse, inverse


def start_kernel(
    tok_ref, cot_ref, small_ref, qkv_ref, wo_ref,
    n1_ref, x_ref, cotp_ref, line_ref, plane_ref, wqkv_ref, wout_ref,
    mid_x, mid_c, mid_w, normed, lines, sems,
):
    copies = Copies(sems)
    chip, line, core, side, over, far = spots()
    copies.enter()
    tokens = inward_stream(copies, tok_ref, mid_x, x_ref)
    next(tokens)
    mine = CORES * line + core
    small = [copies.send(small_ref, lines.at[mine], q) for q in line_partners()]
    small += [copies.send(small_ref, plane_ref.at[chip], q) for q in plane_partners()]
    local = [copies.keep(small_ref, lines.at[mine]), copies.keep(small_ref, plane_ref.at[chip])]
    next(tokens)
    cots = inward_stream(copies, cot_ref, mid_c, cotp_ref)
    next(cots)
    arrived(small)
    finished(local)
    line_ref[...] = lines[...]
    next(tokens)
    weights = columns_stream(copies, qkv_ref, wqkv_ref)
    next(weights)
    rows = rows_stream(copies, wo_ref, mid_w, wout_ref)
    next(rows)
    chunk = x_ref.shape[1]
    ranks = lines.shape[0]
    gain = jnp.concatenate([lines[s, 0:1, :] for s in range(ranks)], axis=1)
    for n in range(PLANE):
        unit, ignored = unit_rows(x_ref[n].astype(F32))
        normed[n * chunk : (n + 1) * chunk] = (unit * gain).astype(BF16)
    gather = gather_stream(copies, normed, n1_ref)
    next(gather)
    next(gather)
    next(cots)
    next(gather)
    next(gather)
    next(rows)
    next(weights)
    next(rows)
    next(cots)
    copies.finish()


def comm_call(kernel, name, number, out_shape, in_specs, out_specs, scratch, vmem_mib=32):
    return pl.pallas_call(
        kernel,
        out_shape=out_shape,
        in_specs=in_specs,
        out_specs=out_specs,
        scratch_shapes=scratch + [pltpu.SemaphoreType.DMA((2, COPIES))],
        compiler_params=pltpu.CompilerParams(
            collective_id=number, has_side_effects=True, vmem_limit_bytes=vmem_mib << 20
        ),
        name=name,
    )


ANY = pl.BlockSpec(memory_space=pl.ANY)
IN_VMEM = pl.BlockSpec(memory_space=pltpu.VMEM)


def start(tokens, cotangent, small, qkv, w_out):
    rows, width = tokens.shape
    ranks = PLANE * CORES
    chunks = (PLANE, rows // PLANE, width)
    shapes = (
        jax.ShapeDtypeStruct((ranks, rows, width), BF16),
        jax.ShapeDtypeStruct(chunks, BF16),
        jax.ShapeDtypeStruct(chunks, BF16),
        jax.ShapeDtypeStruct((ranks,) + small.shape, F32),
        jax.ShapeDtypeStruct((PLANE,) + small.shape, F32),
        jax.ShapeDtypeStruct((ranks,) + qkv.shape[1:], BF16),
        jax.ShapeDtypeStruct(w_out.shape, BF16),
    )
    return comm_call(
        start_kernel, "start", 1, shapes, [ANY] * 5,
        (ANY, IN_VMEM, ANY, IN_VMEM, ANY, ANY, ANY),
        [pltpu.VMEM(chunks, BF16)] * 2
        + [pltpu.VMEM((PLANE, w_out.shape[0], width // PLANE), BF16)]
        + [pltpu.VMEM((rows, width), BF16), pltpu.VMEM((ranks,) + small.shape, F32)],
    )(tokens, cotangent, small, qkv, w_out)


def gains_of(line_ref, row):
    return jnp.concatenate([line_ref[s, row : row + 1, :] for s in range(line_ref.shape[0])], axis=1)


def middle_kernel(
    part_ref, x_ref, line_ref, gu_ref, wd_ref,
    n2_ref, h1_ref, wgu_ref, wdown_ref,
    *rest,
):
    scratch, (summed, normed, mid_w, sems) = rest[:5], rest[5:]
    copies = Copies(sems)
    copies.enter()
    scatter = scatter_stream(copies, part_ref, summed, scratch)
    next(scatter)
    weights = columns_stream(copies, gu_ref, wgu_ref)
    rows = rows_stream(copies, wd_ref, mid_w, wdown_ref)
    next(rows)
    next(weights)
    next(scatter)
    next(scatter)
    next(scatter)
    gain = gains_of(line_ref, 1)
    chunk = x_ref.shape[1]
    for n in range(PLANE):
        part = slice(n * chunk, (n + 1) * chunk)
        hidden = x_ref[n].astype(F32) + summed[part]
        h1_ref[part] = hidden
        unit, ignored = unit_rows(hidden)
        normed[part] = (unit * gain).astype(BF16)
    gather = gather_stream(copies, normed, n2_ref)
    next(gather)
    next(gather)
    next(gather)
    next(rows)
    next(gather)
    next(rows)
    next(weights)
    copies.finish()


def middle(partial, x, lines, gate_up, w_down):
    ranks = PLANE * CORES
    rows, width = PLANE * x.shape[1], x.shape[2]
    shapes = (
        jax.ShapeDtypeStruct((ranks, rows, width), BF16),
        jax.ShapeDtypeStruct((rows, width), F32),
        jax.ShapeDtypeStruct((ranks,) + gate_up.shape[1:], BF16),
        jax.ShapeDtypeStruct(w_down.shape, BF16),
    )
    return comm_call(
        middle_kernel, "middle", 2, shapes, [ANY, IN_VMEM, IN_VMEM, ANY, ANY],
        (ANY, IN_VMEM, ANY, ANY),
        scatter_scratch(rows, width)
        + [pltpu.VMEM((rows, width), F32), pltpu.VMEM((rows, width), BF16)]
        + [pltpu.VMEM((PLANE, w_down.shape[0], width // PLANE), BF16)],
    )(partial.reshape(ranks, rows, width), x, lines, gate_up, w_down)


def column_grads_stream(copies, grad_ref, recv, sum_ref):
    chip, line, core, side, over, far = spots()
    sent = [
        copies.send(grad_ref.at[CORES * q[1] + q[2]], recv.at[core, line], q)
        for q in line_partners()
    ]
    local = copies.keep(grad_ref.at[CORES * line + core], recv.at[core, line])
    yield
    arrived(sent)
    local.wait()
    for number in range(CORES):
        total = recv[number, 0].astype(F32)
        for family in range(1, PLANE):
            total = total + recv[number, family].astype(F32)
        sum_ref[number] = total.astype(BF16)
    yield


def row_grads_stream(copies, grad_ref, mid, recv, summed, out_ref):
    chip, line, core, side, over, far = spots()
    width = out_ref.shape[1] // PLANE

    def quarter(q):
        return pl.ds(pl.multiple_of(q * width, width), width)

    sent = [copies.send(grad_ref.at[:, quarter(q[0])], mid.at[chip], q) for q in plane_partners()]
    local = copies.keep(grad_ref.at[:, quarter(chip)], mid.at[chip])
    yield
    local.wait()
    arrived(sent)
    sent = [copies.send(mid.at[q[1]], recv.at[line], q) for q in line_partners()[: PLANE - 1]]
    local = copies.keep(mid.at[line], recv.at[line])
    yield
    arrived(sent)
    local.wait()
    total = recv[0].astype(F32)
    for family in range(1, PLANE):
        total = total + recv[family].astype(F32)
    summed[...] = total.astype(BF16)
    sent = [copies.send(summed, out_ref.at[:, quarter(chip)], q) for q in plane_partners()]
    local = copies.keep(summed, out_ref.at[:, quarter(chip)])
    yield
    arrived(sent)
    local.wait()
    yield


def gain_grads_stream(copies, own, recv, summed, plane, out_ref):
    chip, line, core, side, over, far = spots()
    mine = CORES * line + core
    sent = [copies.send(own.at[CORES * q[1] + q[2]], recv.at[mine], q) for q in line_partners()]
    local = copies.keep(own.at[mine], recv.at[mine])
    yield
    arrived(sent)
    local.wait()
    summed[...] = jnp.sum(recv[...], axis=0)
    sent = [copies.send(summed, plane.at[chip], q) for q in plane_partners()]
    local = copies.keep(summed, plane.at[chip])
    yield
    arrived(sent)
    local.wait()
    out_ref[...] = jnp.sum(plane[...], axis=0)
    yield


def norm_back(grad, value, gain):
    unit, inverse = unit_rows(value)
    scaled = grad * gain
    back = inverse * (scaled - unit * jnp.mean(scaled * unit, axis=-1, keepdims=True))
    return back, jnp.sum(grad * unit, axis=0, keepdims=True)


def back_kernel(
    part_ref, h1_ref, cot_ref, line_ref, gu_ref,
    ga_ref, dh1_ref, gain_ref, gusum_ref,
    *rest,
):
    scratch, (summed, low, recv, sems) = rest[:5], rest[5:]
    copies = Copies(sems)
    copies.enter()
    scatter = scatter_stream(copies, part_ref, summed, scratch)
    next(scatter)
    columns = column_grads_stream(copies, gu_ref, recv, gusum_ref)
    next(columns)
    next(scatter)
    next(scatter)
    next(scatter)
    gain = gains_of(line_ref, 1)
    chunk = cot_ref.shape[1]
    gain_ref[...] = jnp.zeros_like(gain_ref)
    for n in range(PLANE):
        part = slice(n * chunk, (n + 1) * chunk)
        back, by_gain = norm_back(summed[part], h1_ref[part], gain)
        grad = cot_ref[n].astype(F32) + back
        gain_ref[0:1] += by_gain
        dh1_ref[part] = grad
        low[part] = grad.astype(BF16)
    gather = gather_stream(copies, low, ga_ref)
    next(gather)
    next(gather)
    next(gather)
    next(gather)
    next(columns)
    copies.finish()


def back(partial, h1, cot, lines, gate_up_grad):
    ranks = PLANE * CORES
    rows, width = h1.shape
    shapes = (
        jax.ShapeDtypeStruct((ranks, rows, width), BF16),
        jax.ShapeDtypeStruct((rows, width), F32),
        jax.ShapeDtypeStruct((8, width), F32),
        jax.ShapeDtypeStruct((CORES,) + gate_up_grad.shape[1:], BF16),
    )
    return comm_call(
        back_kernel, "back", 3, shapes, [ANY, IN_VMEM, IN_VMEM, IN_VMEM, ANY],
        (ANY, IN_VMEM, IN_VMEM, IN_VMEM),
        scatter_scratch(rows, width)
        + [pltpu.VMEM((rows, width), F32), pltpu.VMEM((rows, width), BF16)]
        + [pltpu.VMEM((CORES, PLANE) + gate_up_grad.shape[1:], BF16)],
    )(partial, h1, cot, lines, gate_up_grad)


def last_kernel(
    part_ref, mixed_ref, x_ref, h1_ref, dh1_ref, line_ref, gain_ref,
    gusum_ref, qkv_ref, wo_ref, wd_ref,
    out_ref, grad_ref, gains_ref, gu_all, qkv_all, wo_all, wd_all,
    *rest,
):
    scratch, other, rest = rest[:5], rest[5:10], rest[10:]
    summed, mixed, low, mid_a, mid_b, recv_qkv, qkvsum, rest = *rest[:7], rest[7:]
    mid_wo, recv_wo, sum_wo, mid_wd, recv_wd, sum_wd, own, recv_gain, sum_gain, plane, sems = rest
    copies = Copies(sems)
    copies.enter()
    scatter = scatter_stream(copies, part_ref, summed, scratch)
    next(scatter)
    qkv = column_grads_stream(copies, qkv_ref, recv_qkv, qkvsum)
    next(qkv)
    next(scatter)
    second = scatter_stream(copies, mixed_ref, mixed, other)
    next(second)
    next(scatter)
    wd = row_grads_stream(copies, wd_ref, mid_wd, recv_wd, sum_wd, wd_all)
    next(wd)
    wo = row_grads_stream(copies, wo_ref, mid_wo, recv_wo, sum_wo, wo_all)
    next(wo)
    next(scatter)
    gain = gains_of(line_ref, 0)
    chunk, width = x_ref.shape[1], x_ref.shape[2]
    total = jnp.zeros((1, width), F32)
    for n in range(PLANE):
        part = slice(n * chunk, (n + 1) * chunk)
        back, by_gain = norm_back(summed[part], x_ref[n].astype(F32), gain)
        total = total + by_gain
        low[n] = (dh1_ref[part] + back).astype(BF16)
    tokens = outward_stream(copies, low, mid_a, grad_ref)
    next(tokens)
    shard = line_ref.shape[2]
    own[...] = jnp.zeros_like(own)
    for s in range(PLANE * CORES):
        part = slice(s * shard, (s + 1) * shard)
        own[s, 0:1] = total[:, part]
        own[s, 1:2] = gain_ref[0:1, part]
    gains = gain_grads_stream(copies, own, recv_gain, sum_gain, plane, gains_ref)
    next(gains)
    next(second)
    next(wd)
    next(wo)
    next(second)
    next(qkv)
    gather_qkv = gather_stream(copies, qkvsum, qkv_all, twin=False)
    next(gather_qkv)
    gather_gu = gather_stream(copies, gusum_ref, gu_all, twin=False)
    next(gather_gu)
    next(second)
    for n in range(PLANE):
        part = slice(n * chunk, (n + 1) * chunk)
        low_out = (h1_ref[part] + mixed[part]).astype(BF16)
        mid_b[1, n] = low_out
    output = outward_stream(copies, mid_b.at[1], mid_b.at[0], out_ref)
    next(output)
    next(gains)
    next(tokens)
    next(gather_qkv)
    next(wd)
    next(wo)
    next(gather_gu)
    next(output)
    for stream in (gather_qkv, gather_qkv, gather_gu, gather_gu, tokens, gains, wd, wo, output):
        next(stream)
    copies.finish()


def last(partial, mixed, x, h1, dh1, lines, gain2, gate_up_sum, qkv_grad, out_grad, down_grad):
    ranks = PLANE * CORES
    rows, width = h1.shape
    quarter = width // PLANE
    small = lines.shape[1:]
    shapes = (
        jax.ShapeDtypeStruct((rows, width), BF16),
        jax.ShapeDtypeStruct((rows, width), BF16),
        jax.ShapeDtypeStruct(small, F32),
        jax.ShapeDtypeStruct((PLANE,) + gate_up_sum.shape, BF16),
        jax.ShapeDtypeStruct((PLANE, CORES) + qkv_grad.shape[1:], BF16),
        jax.ShapeDtypeStruct(out_grad.shape, BF16),
        jax.ShapeDtypeStruct(down_grad.shape, BF16),
    )
    scratch = scatter_scratch(rows, width) * 2
    scratch += [pltpu.VMEM((rows, width), F32)] * 2
    scratch += [pltpu.VMEM(x.shape, BF16)] * 2 + [pltpu.VMEM((2,) + x.shape, BF16)]
    scratch += [pltpu.VMEM((CORES, PLANE) + qkv_grad.shape[1:], BF16)]
    scratch += [pltpu.VMEM((CORES,) + qkv_grad.shape[1:], BF16)]
    for grad in (out_grad, down_grad):
        scratch += [pltpu.VMEM((PLANE, grad.shape[0], quarter), BF16)] * 2
        scratch += [pltpu.VMEM((grad.shape[0], quarter), BF16)]
    scratch += [pltpu.VMEM(lines.shape, F32)] * 2 + [pltpu.VMEM(small, F32), pltpu.VMEM((PLANE,) + small, F32)]
    return comm_call(
        last_kernel, "last", 4, shapes,
        [ANY, ANY] + [IN_VMEM] * 5 + [ANY] * 4,
        (ANY, ANY, IN_VMEM, ANY, ANY, ANY, ANY),
        scratch, 48,
    )(partial, mixed, x, h1, dh1, lines, gain2, gate_up_sum, qkv_grad, out_grad, down_grad)


def feed_kernel(n2_ref, cot_ref, wgu_ref, wd_ref, mix_ref, dn2_ref, ggu_ref, gd_ref, wgu_t, wd_t, wd_p, ggu, gd):
    step = pl.program_id(0)
    hidden, lanes = wd_ref.shape[0], wd_p.shape[0]

    @pl.when(step == 0)
    def _():
        wd_p[...] = jnp.zeros_like(wd_p)
        wd_p[0:hidden] = wd_ref[...]
        for s in range(wgu_ref.shape[0]):
            shard = wgu_ref.shape[1]
            wgu_t[:, s * shard : (s + 1) * shard] = wgu_ref[s].T
        wd_t[...] = wd_p[...].T
        ggu[...] = jnp.zeros_like(ggu)
        gd[...] = jnp.zeros_like(gd)

    block, cot = n2_ref[0], cot_ref[0]
    gate_up = matmul(block, wgu_ref[...].reshape(-1, 2 * lanes))
    gate, upper = gate_up[:, :lanes], gate_up[:, lanes:]
    cubic = 0.7978845608028654 * (gate + 0.044715 * gate * gate * gate)
    bend = jnp.tanh(cubic)
    half = 0.5 * (1.0 + bend)
    active = gate * half
    slope = half + (0.5 * 0.7978845608028654) * gate * (1.0 - bend * bend) * (
        1.0 + 3 * 0.044715 * gate * gate
    )
    mixed = (active * upper).astype(BF16)
    mix_ref[0] = matmul(mixed, wd_p[...]).astype(BF16)
    du = matmul(cot, wd_t[...])
    dab = jnp.concatenate([(du * upper * slope).astype(BF16), (du * active).astype(BF16)], axis=1)
    dn2_ref[0] = matmul(dab, wgu_t[...]).astype(BF16)
    ggu[...] += inner(block, dab)
    gd[...] += inner(mixed, cot)

    @pl.when(step == pl.num_programs(0) - 1)
    def _():
        shard = ggu_ref.shape[1]
        for s in range(ggu_ref.shape[0]):
            ggu_ref[s] = ggu[s * shard : (s + 1) * shard].astype(BF16)
        gd_ref[...] = gd[0:hidden].astype(BF16)


def feed(n2, cot, w_gu, w_d):
    ranks, rows, width = n2.shape
    lanes = w_gu.shape[2] // 2
    block = pl.BlockSpec((1, rows, width), lambda i: (i, 0, 0))
    whole3 = pl.BlockSpec(w_gu.shape, lambda i: (0, 0, 0))
    whole2 = pl.BlockSpec(w_d.shape, lambda i: (0, 0))
    tokens = jax.ShapeDtypeStruct(n2.shape, BF16)
    return pl.pallas_call(
        feed_kernel,
        grid=(ranks,),
        out_shape=(
            tokens, tokens,
            jax.ShapeDtypeStruct(w_gu.shape, BF16),
            jax.ShapeDtypeStruct(w_d.shape, BF16),
        ),
        in_specs=[block, block, whole3, whole2],
        out_specs=(block, block, whole3, whole2),
        scratch_shapes=[
            pltpu.VMEM((2 * lanes, width), BF16),
            pltpu.VMEM((width, lanes), BF16),
            pltpu.VMEM((lanes, width), BF16),
            pltpu.VMEM((width, 2 * lanes), F32),
            pltpu.VMEM((lanes, width), F32),
        ],
        compiler_params=pltpu.CompilerParams(
            dimension_semantics=("arbitrary",), vmem_limit_bytes=48 << 20
        ),
        name="feed",
    )(n2, cot, w_gu, w_d)


def attend_back_kernel(n1_ref, dqkv_ref, att_ref, ga_ref, wqkv_ref, dn1_ref, gqkv_ref, gwo_ref, w_t, gqkv, gwo):
    step = pl.program_id(0)

    @pl.when(step == 0)
    def _():
        for s in range(wqkv_ref.shape[0]):
            shard = wqkv_ref.shape[1]
            w_t[:, s * shard : (s + 1) * shard] = wqkv_ref[s].T
        gqkv[...] = jnp.zeros_like(gqkv)
        gwo[...] = jnp.zeros_like(gwo)

    dqkv = dqkv_ref[...]
    dn1_ref[0] = matmul(dqkv, w_t[...]).astype(BF16)
    gqkv[...] += inner(n1_ref[0], dqkv)
    gwo[...] += inner(att_ref[...], ga_ref[0])

    @pl.when(step == pl.num_programs(0) - 1)
    def _():
        shard = gqkv_ref.shape[1]
        for s in range(gqkv_ref.shape[0]):
            gqkv_ref[s] = gqkv[s * shard : (s + 1) * shard].astype(BF16)
        gwo_ref[...] = gwo[...].astype(BF16)


def attend_back(n1, dqkv, att, ga, w_qkv):
    ranks, rows, width = n1.shape
    heads, cols = att.shape[1], dqkv.shape[1]
    block = pl.BlockSpec((1, rows, width), lambda i: (i, 0, 0))
    whole3 = pl.BlockSpec(w_qkv.shape, lambda i: (0, 0, 0))
    return pl.pallas_call(
        attend_back_kernel,
        grid=(ranks,),
        out_shape=(
            jax.ShapeDtypeStruct(n1.shape, BF16),
            jax.ShapeDtypeStruct(w_qkv.shape, BF16),
            jax.ShapeDtypeStruct((heads, width), BF16),
        ),
        in_specs=[
            block,
            pl.BlockSpec((rows, cols), lambda i: (i, 0)),
            pl.BlockSpec((rows, heads), lambda i: (i, 0)),
            block,
            whole3,
        ],
        out_specs=(block, whole3, pl.BlockSpec((heads, width), lambda i: (0, 0))),
        scratch_shapes=[
            pltpu.VMEM((cols, width), BF16),
            pltpu.VMEM((width, cols), F32),
            pltpu.VMEM((heads, width), F32),
        ],
        compiler_params=pltpu.CompilerParams(
            dimension_semantics=("arbitrary",), vmem_limit_bytes=40 << 20
        ),
        name="attend_back",
    )(n1, dqkv, att, ga, w_qkv)


def padded(piece, size):
    return jnp.pad(piece, ((0, 0), (0, size - piece.shape[1])))


def plane_local(
    tokens,
    cotangent,
    block_table,
    norm1_gain,
    w_query,
    w_key,
    w_value,
    w_out,
    norm2_gain,
    w_gate,
    w_up,
    w_down,
):
    chip, line, core = lax.axis_index("group"), lax.axis_index("z"), lax.axis_index("core")
    rows, width = tokens.shape[1:]
    heads = width // (PLANE * CORES)
    hidden = w_gate.shape[1] // (PLANE * CORES)
    lanes = -(-hidden // 128) * 128

    def column(w, size, number):
        return lax.dynamic_slice_in_dim(w, (chip * CORES + number) * size, size, 1)

    def pieces(weights, size, wide):
        return jnp.stack([
            jnp.concatenate([padded(column(w, size, number), wide) for w in weights], axis=1)
            for number in range(CORES)
        ])

    table_row = jnp.pad(block_table.astype(F32), ((0, 0), (0, heads - block_table.shape[1])))
    small = jnp.concatenate([norm1_gain[None].astype(F32), norm2_gain[None].astype(F32), table_row])
    small = jnp.pad(small, ((0, 5), (0, 0)))
    n1, x, cot, gains_all, plane_small, w_qkv, w_o = start(
        tokens[0], cotangent[0], small, pieces((w_query, w_key, w_value), heads, heads), w_out
    )
    table = lax.dynamic_index_in_dim(plane_small, line, 0, keepdims=False)
    table = table[2, : block_table.shape[1]].astype(jnp.int32)
    cot_all = lax.all_gather(cot.reshape(rows, width), TP, axis=0, tiled=False)

    qkv = matmul(n1.reshape(-1, width), w_qkv.reshape(width, -1)).astype(BF16)
    att, lse, ot = attend(table, qkv)
    n2, h1, w_gu, w_d = middle(
        matmul(att, w_o).astype(BF16), x, gains_all, pieces((w_gate, w_up), hidden, lanes), w_down
    )
    mixed, dn2, g_gu, g_down = feed(n2, cot_all, w_gu, w_d)
    ga, dh1, gain2, gu_sum = back(dn2, h1, cot, gains_all, g_gu)
    datt = outer(ga.reshape(-1, width), w_o).astype(BF16)
    dqkv = attend_grad(table, qkv, datt, lse, ot)
    dn1, g_qkv, g_out = attend_back(n1, dqkv, att, ga, w_qkv)
    output, tokens_grad, gain_grads, g_gu, g_qkv, g_out, g_down = last(
        dn1, mixed, x, h1, dh1, gains_all, gain2, gu_sum, g_qkv, g_out, g_down
    )

    def whole(grad, begin, size):
        piece = grad[..., begin : begin + size].reshape(-1, grad.shape[2], size)
        return piece.swapaxes(0, 1).reshape(grad.shape[2], -1).astype(F32)

    return (
        output[None],
        tokens_grad[None],
        gain_grads[0],
        whole(g_qkv, 0, heads),
        whole(g_qkv, heads, heads),
        whole(g_qkv, 2 * heads, heads),
        g_out.astype(F32),
        gain_grads[1],
        whole(g_gu, 0, hidden),
        whole(g_gu, lanes, hidden),
        g_down.astype(F32),
    )


def plane_solution(mesh):
    split = Mesh(mesh.devices.reshape(PLANE, PLANE, CORES), ("group", "z", "core"))
    ctx = ("z", "core")
    token, weight = P("group", ctx, None), P(ctx, None)
    in_specs = (token, token, P("group", None), P(ctx)) + (weight,) * 4 + (P(ctx),) + (weight,) * 3
    out_specs = (token, token, P(ctx)) + (weight,) * 4 + (P(ctx),) + (weight,) * 3
    return jax.shard_map(
        plane_local, mesh=split, in_specs=in_specs, out_specs=out_specs, check_vma=False
    )


def family_solution(mesh):
    in_specs = (
        P("group", "ctx", None),
        P("group", "ctx", None),
        P("group", None),
        P("ctx"),
        P("ctx", None),
        P("ctx", None),
        P("ctx", None),
        P("ctx", None),
        P("ctx"),
        P("ctx", None),
        P("ctx", None),
        P("ctx", None),
    )
    out_specs = (
        P("group", "ctx", None),
        P("group", "ctx", None),
        P("ctx"),
        P("ctx", None),
        P("ctx", None),
        P("ctx", None),
        P("ctx", None),
        P("ctx"),
        P("ctx", None),
        P("ctx", None),
        P("ctx", None),
    )
    return jax.shard_map(local, mesh=mesh, in_specs=in_specs, out_specs=out_specs, check_vma=False)


def solution(mesh):
    groups, ranks = mesh.shape["group"], mesh.shape["ctx"]
    if groups == PLANE and ranks == 2 * PLANE:
        return plane_solution(mesh)
    return family_solution(mesh)
```

```python
import jax
import jax.numpy as jnp
from jax import lax
from jax.experimental import pallas as pl
from jax.experimental.pallas import tpu as pltpu
from jax.sharding import Mesh
from jax.sharding import PartitionSpec as P

HEADS = 16
HEAD = 64
BLK = 128
KEYBLK = 512
PROMPT_MAX = 2048
CONT = 256


EPS = 1e-06
SCALE = 0.125


def rms_scale(hidden, gain):
    return hidden * lax.rsqrt(jnp.mean(hidden * hidden, axis=-1, keepdims=True) + EPS) * gain


def gated(gate, upper):
    return jax.nn.gelu(gate, approximate=True) * upper


def matmul(left, right):
    return jnp.dot(left, right, preferred_element_type=jnp.float32)


def inner(left, right):
    return lax.dot_general(
        left, right, (((0,), (0,)), ((), ())), preferred_element_type=jnp.float32
    )


def outer(left, right):
    return lax.dot_general(
        left, right, (((1,), (1,)), ((), ())), preferred_element_type=jnp.float32
    )


def family_index(table):
    offsets = jnp.arange(BLK, dtype=jnp.int32)
    return (table[:, None] * BLK + offsets[None, :]).reshape(-1)


def segment_of(index, prompt_len):
    return jnp.where(index < prompt_len, 0, 1 + (index - prompt_len) // CONT)


def allowed(query_index, key_index, prompt_len):
    query_seg = segment_of(query_index, prompt_len)
    key_seg = segment_of(key_index, prompt_len)
    same = (query_seg[:, None] == key_seg[None, :]) & (key_index[None, :] <= query_index[:, None])
    prompt = (key_seg[None, :] == 0) & (query_seg[:, None] > 0)
    return same | prompt


def head_split(block):
    return block.reshape(block.shape[0], HEADS, HEAD)


def scores_of(query_heads, key_block, query_index, key_index, prompt_len):
    score = (
        jnp.einsum(
            "qhd,khd->hqk", query_heads, head_split(key_block), preferred_element_type=jnp.float32
        )
        * SCALE
    )
    return (score, allowed(query_index, key_index, prompt_len))


def attend_stats(queries, keys, query_index, key_index, prompt_len):
    query_heads = head_split(queries)

    def step(carry, number):
        best, total = carry
        start = number * KEYBLK
        key_block = lax.dynamic_slice_in_dim(keys, start, KEYBLK, 0)
        block_index = lax.dynamic_slice_in_dim(key_index, start, KEYBLK, 0)
        score, keep = scores_of(query_heads, key_block, query_index, block_index, prompt_len)
        score = jnp.where(keep[None], score, -1e30)
        larger = jnp.maximum(best, jnp.max(score, axis=-1))
        terms = jnp.where(keep[None], jnp.exp(score - larger[:, :, None]), 0.0)
        total = total * jnp.exp(best - larger) + jnp.sum(terms, axis=-1)
        return ((larger, total), None)

    start_best = jnp.full((HEADS, queries.shape[0]), -1e30, jnp.float32)
    (best, total), ignored = lax.scan(
        step, (start_best, jnp.zeros_like(start_best)), jnp.arange(keys.shape[0] // KEYBLK)
    )
    return best + jnp.log(total)


def attend_values(queries, keys, values, lse, query_index, key_index, prompt_len):
    query_heads = head_split(queries)

    def step(acc, number):
        start = number * KEYBLK
        key_block = lax.dynamic_slice_in_dim(keys, start, KEYBLK, 0)
        value_block = lax.dynamic_slice_in_dim(values, start, KEYBLK, 0)
        block_index = lax.dynamic_slice_in_dim(key_index, start, KEYBLK, 0)
        score, keep = scores_of(query_heads, key_block, query_index, block_index, prompt_len)
        prob = jnp.where(keep[None], jnp.exp(score - lse[:, :, None]), 0.0).astype(jnp.bfloat16)
        return (
            acc
            + jnp.einsum(
                "hqk,khd->qhd", prob, head_split(value_block), preferred_element_type=jnp.float32
            ),
            None,
        )

    start_acc = jnp.zeros((queries.shape[0], HEADS, HEAD), jnp.float32)
    acc, ignored = lax.scan(step, start_acc, jnp.arange(keys.shape[0] // KEYBLK))
    return acc.reshape(queries.shape[0], HEADS * HEAD)


def block_grads(query_heads, grad_heads, key_block, value_block, lse, delta, keep):
    key_heads = head_split(key_block)
    value_heads = head_split(value_block)
    score = (
        jnp.einsum("qhd,khd->hqk", query_heads, key_heads, preferred_element_type=jnp.float32)
        * SCALE
    )
    prob = jnp.where(keep[None], jnp.exp(score - lse[:, :, None]), 0.0)
    dvalue = jnp.einsum(
        "hqk,qhd->khd", prob.astype(jnp.bfloat16), grad_heads, preferred_element_type=jnp.float32
    )
    dprob = jnp.einsum("qhd,khd->hqk", grad_heads, value_heads, preferred_element_type=jnp.float32)
    dscore = (prob * (dprob - delta[:, :, None])).astype(jnp.bfloat16)
    dquery = (
        jnp.einsum("hqk,khd->qhd", dscore, key_heads, preferred_element_type=jnp.float32) * SCALE
    )
    dkey = (
        jnp.einsum("hqk,qhd->khd", dscore, query_heads, preferred_element_type=jnp.float32) * SCALE
    )
    return (dquery, dkey, dvalue)


def local(
    tokens,
    cotangent,
    block_table,
    norm1_gain,
    w_query,
    w_key,
    w_value,
    w_out,
    norm2_gain,
    w_gate,
    w_up,
    w_down,
):
    row_count = tokens.shape[1]
    width = tokens.shape[2]
    every_index = family_index(block_table[0])
    prompt_len = min(PROMPT_MAX, every_index.shape[0] // 2)
    own_index = lax.dynamic_slice_in_dim(
        every_index, lax.axis_index("ctx") * row_count, row_count, 0
    )
    gain1, wq_full, wk_full, wv_full, wo_full = (
        lax.all_gather(norm1_gain, "ctx", axis=0, tiled=True),
        lax.all_gather(w_query, "ctx", axis=0, tiled=True),
        lax.all_gather(w_key, "ctx", axis=0, tiled=True),
        lax.all_gather(w_value, "ctx", axis=0, tiled=True),
        lax.all_gather(w_out, "ctx", axis=0, tiled=True),
    )
    inputs = tokens[0].astype(jnp.float32)
    normed1, norm1_pull = jax.vjp(rms_scale, inputs, gain1.astype(jnp.float32))
    first_low = normed1.astype(jnp.bfloat16)
    queries = matmul(first_low, wq_full).astype(jnp.bfloat16)
    keys_own = matmul(first_low, wk_full).astype(jnp.bfloat16)
    values_own = matmul(first_low, wv_full).astype(jnp.bfloat16)
    keys_all, values_all = (
        lax.all_gather(keys_own, "ctx", axis=0, tiled=True),
        lax.all_gather(values_own, "ctx", axis=0, tiled=True),
    )
    lse = attend_stats(queries, keys_all, own_index, every_index, prompt_len)
    attended_wide = attend_values(
        queries, keys_all, values_all, lse, own_index, every_index, prompt_len
    )
    attended = attended_wide.astype(jnp.bfloat16)
    hidden = inputs + matmul(attended, wo_full)
    gain2, wg_full, wu_full, wd_full = (
        lax.all_gather(norm2_gain, "ctx", axis=0, tiled=True),
        lax.all_gather(w_gate, "ctx", axis=0, tiled=True),
        lax.all_gather(w_up, "ctx", axis=0, tiled=True),
        lax.all_gather(w_down, "ctx", axis=0, tiled=True),
    )
    normed2, norm2_pull = jax.vjp(rms_scale, hidden, gain2.astype(jnp.float32))
    second_low = normed2.astype(jnp.bfloat16)
    gate = matmul(second_low, wg_full)
    upper = matmul(second_low, wu_full)
    mixed_wide, gate_pull = jax.vjp(gated, gate, upper)
    mixed = mixed_wide.astype(jnp.bfloat16)
    result = hidden + matmul(mixed, wd_full)
    output = result.astype(jnp.bfloat16)[None]
    grad_low = cotangent[0]
    grad_down = inner(mixed, grad_low)
    dmixed = outer(grad_low, wd_full)
    dgate, dupper = gate_pull(dmixed)
    dgate_low = dgate.astype(jnp.bfloat16)
    dupper_low = dupper.astype(jnp.bfloat16)
    grad_gate = inner(second_low, dgate_low)
    grad_up = inner(second_low, dupper_low)
    dnormed2 = outer(dgate_low, wg_full) + outer(dupper_low, wu_full)
    dhidden_norm, grad_gain2 = norm2_pull(dnormed2)
    dhidden = grad_low.astype(jnp.float32) + dhidden_norm
    attn_low = dhidden.astype(jnp.bfloat16)
    grad_out_w = inner(attended, attn_low)
    dattended = outer(attn_low, wo_full).astype(jnp.bfloat16)
    delta = jnp.sum(
        (dattended.astype(jnp.float32) * attended_wide).reshape(row_count, HEADS, HEAD), axis=-1
    ).T
    query_heads = head_split(queries)
    grad_heads = head_split(dattended)

    def key_step(carry, number):
        start = number * KEYBLK
        key_block = lax.dynamic_slice_in_dim(keys_all, start, KEYBLK, 0)
        value_block = lax.dynamic_slice_in_dim(values_all, start, KEYBLK, 0)
        block_index = lax.dynamic_slice_in_dim(every_index, start, KEYBLK, 0)
        keep = allowed(own_index, block_index, prompt_len)
        dquery, dkey, dvalue = block_grads(
            query_heads, grad_heads, key_block, value_block, lse, delta, keep
        )
        joined = jnp.concatenate(
            [dkey.reshape(KEYBLK, width), dvalue.reshape(KEYBLK, width)], axis=1
        )
        return (carry + dquery, joined)

    start_query = jnp.zeros((row_count, HEADS, HEAD), jnp.float32)
    query_sum, key_terms = lax.scan(
        key_step, start_query, jnp.arange(every_index.shape[0] // KEYBLK)
    )
    summed = lax.psum_scatter(
        key_terms.reshape(every_index.shape[0], 2 * width).astype(jnp.bfloat16),
        "ctx",
        scatter_dimension=0,
        tiled=True,
    ).astype(jnp.float32)
    query_grad = query_sum.reshape(row_count, width)
    key_grad = summed[:, :width]
    value_grad = summed[:, width:]
    query_low = query_grad.astype(jnp.bfloat16)
    key_low = key_grad.astype(jnp.bfloat16)
    value_low = value_grad.astype(jnp.bfloat16)
    grad_query = inner(first_low, query_low)
    grad_key = inner(first_low, key_low)
    grad_value = inner(first_low, value_low)
    dnormed1 = outer(query_low, wq_full) + outer(key_low, wk_full) + outer(value_low, wv_full)
    dinput_norm, grad_gain1 = norm1_pull(dnormed1)
    tokens_grad = (dhidden + dinput_norm).astype(jnp.bfloat16)[None]
    shards = (
        lax.psum_scatter(
            grad_gain1.astype(jnp.bfloat16), "ctx", scatter_dimension=0, tiled=True
        ).astype(jnp.float32),
        lax.psum_scatter(
            grad_query.astype(jnp.bfloat16), "ctx", scatter_dimension=0, tiled=True
        ).astype(jnp.float32),
        lax.psum_scatter(
            grad_key.astype(jnp.bfloat16), "ctx", scatter_dimension=0, tiled=True
        ).astype(jnp.float32),
        lax.psum_scatter(
            grad_value.astype(jnp.bfloat16), "ctx", scatter_dimension=0, tiled=True
        ).astype(jnp.float32),
        lax.psum_scatter(
            grad_out_w.astype(jnp.bfloat16), "ctx", scatter_dimension=0, tiled=True
        ).astype(jnp.float32),
        lax.psum_scatter(
            grad_gain2.astype(jnp.bfloat16), "ctx", scatter_dimension=0, tiled=True
        ).astype(jnp.float32),
        lax.psum_scatter(
            grad_gate.astype(jnp.bfloat16), "ctx", scatter_dimension=0, tiled=True
        ).astype(jnp.float32),
        lax.psum_scatter(
            grad_up.astype(jnp.bfloat16), "ctx", scatter_dimension=0, tiled=True
        ).astype(jnp.float32),
        lax.psum_scatter(
            grad_down.astype(jnp.bfloat16), "ctx", scatter_dimension=0, tiled=True
        ).astype(jnp.float32),
    )
    shards = (
        lax.psum(shards[0].astype(jnp.bfloat16), "group").astype(jnp.float32),
        lax.psum(shards[1].astype(jnp.bfloat16), "group").astype(jnp.float32),
        lax.psum(shards[2].astype(jnp.bfloat16), "group").astype(jnp.float32),
        lax.psum(shards[3].astype(jnp.bfloat16), "group").astype(jnp.float32),
        lax.psum(shards[4].astype(jnp.bfloat16), "group").astype(jnp.float32),
        lax.psum(shards[5].astype(jnp.bfloat16), "group").astype(jnp.float32),
        lax.psum(shards[6].astype(jnp.bfloat16), "group").astype(jnp.float32),
        lax.psum(shards[7].astype(jnp.bfloat16), "group").astype(jnp.float32),
        lax.psum(shards[8].astype(jnp.bfloat16), "group").astype(jnp.float32),
    )
    return (
        output,
        tokens_grad,
        shards[0],
        shards[1],
        shards[2],
        shards[3],
        shards[4],
        shards[5],
        shards[6],
        shards[7],
        shards[8],
    )


PLANE = 4
CORES = 2
TP = ("group", "core")
F32 = jnp.float32
BF16 = jnp.bfloat16


def dot_nt(left, right):
    return lax.dot_general(left, right, (((1,), (1,)), ((), ())), preferred_element_type=F32)


def head_mask(rows, head):
    lane = lax.broadcasted_iota(jnp.int32, (rows, 2 * HEAD), 1)
    return (lane >= head * HEAD) & (lane < (head + 1) * HEAD)


def causal_mask():
    key = lax.broadcasted_iota(jnp.int32, (CONT, CONT), 0)
    query = lax.broadcasted_iota(jnp.int32, (CONT, CONT), 1)
    return key <= query


MESH = pl.DeviceIdType.MESH
COPIES = 224


def spots():
    chip, line, core = lax.axis_index("group"), lax.axis_index("z"), lax.axis_index("core")
    side = chip + 1 - 2 * lax.rem(chip, 2)
    over = lax.rem(chip + 2, PLANE)
    far = PLANE - 1 - chip
    return chip, line, core, side, over, far


def plane_partners():
    chip, line, core, side, over, far = spots()
    return [(q, line, core) for q in (far, side, over)]


def line_partners():
    chip, line, core, side, over, far = spots()
    lines = [lax.rem(line + d, PLANE) for d in range(1, PLANE)]
    same = [(chip, z, core) for z in lines]
    return same + [(chip, z, 1 - core) for z in lines] + [(chip, line, 1 - core)]


class Copies:
    def __init__(self, sems, parent=None):
        self.sems, self.parent = sems, parent
        self.count, self.started, self.branches = 0, [], []

    def branch(self):
        self.branches.append(Copies(self.sems, self))
        return self.branches[-1]

    def number(self):
        if self.parent is not None:
            return self.parent.number()
        self.count += 1
        return self.count - 1

    def enter(self):
        barrier = pltpu.get_barrier_semaphore()
        partners = plane_partners() + line_partners()
        for partner in partners:
            pl.semaphore_signal(barrier, inc=1, device_id=partner, device_id_type=MESH)
        pl.semaphore_wait(barrier, len(partners))

    def send(self, source, target, partner):
        number = self.number()
        copy = pltpu.make_async_remote_copy(
            src_ref=source,
            dst_ref=target,
            send_sem=self.sems.at[0, number],
            recv_sem=self.sems.at[1, number],
            device_id=partner,
            device_id_type=MESH,
        )
        copy.start()
        self.started.append(copy)
        return copy

    def keep(self, source, target):
        copy = pltpu.make_async_copy(source, target, self.sems.at[0, self.number()])
        copy.start()
        return copy

    def finish(self):
        for copy in self.started:
            copy.wait_send()
        self.started = []
        for branch in self.branches:
            branch.finish()


def arrived(copies):
    for copy in copies:
        copy.wait_recv()


def finished(copies):
    for copy in copies:
        copy.wait()


def gather_stream(copies, own_ref, out_ref, twin=True):
    chip, line, core, side, over, far = spots()
    half = own_ref.shape[0] // 2
    to_far, to_side, to_over = plane_partners()
    to_twin = (chip, line, 1 - core)

    def slot_of(q):
        return CORES * q + core if twin else q

    def part(slot, number):
        return out_ref.at[slot, pl.ds(number * half, half)]

    def own(number):
        return own_ref.at[pl.ds(number * half, half)]

    def on(slot, number, partner):
        return copies.send(part(slot, number), part(slot, number), partner)

    def share(slot, number):
        return [on(slot, number, to_twin)] if twin else []

    mine, slot_side, slot_over, slot_far = map(slot_of, (chip, side, over, far))
    sides, overs = [None, None], [None, None]
    overs[0] = copies.send(own(0), part(mine, 0), to_over)
    sides[1] = copies.send(own(1), part(mine, 1), to_side)
    sides[0] = copies.send(own(0), part(mine, 0), to_side)
    overs[1] = copies.send(own(1), part(mine, 1), to_over)
    twins = [copies.send(own(h), part(mine, h), to_twin) for h in range(2)] if twin else []
    local = copies.keep(own_ref, out_ref.at[mine])
    yield
    local.wait()
    arrived(twins)
    yield
    overs[0].wait_recv()
    far0 = on(slot_over, 0, to_side)
    twins = share(slot_over, 0)
    sides[1].wait_recv()
    far1 = on(slot_side, 1, to_over)
    twins += share(slot_side, 1)
    yield
    sides[0].wait_recv()
    twins += share(slot_side, 0)
    overs[1].wait_recv()
    twins += share(slot_over, 1)
    yield
    arrived(twins)
    yield
    far0.wait_recv()
    twins = share(slot_far, 0)
    far1.wait_recv()
    twins += share(slot_far, 1)
    yield
    arrived(twins)
    yield


def scatter_stream(copies, part_ref, out_ref, scratch):
    twin, from_side, from_over, go = scratch
    chip, line, core, side, over, far = spots()
    rows = out_ref.shape[0]
    half = rows // 2
    to_far, to_side, to_over = plane_partners()
    to_twin = (chip, line, 1 - core)
    chips = (far, side, over, chip)
    twins = [[], [], [], []]

    def share(n, h):
        half_rows = pl.ds(h * half, half)
        source = part_ref.at[CORES * chips[n] + 1 - core, half_rows]
        twins[n].append(copies.send(source, twin.at[n, half_rows], to_twin))

    for n, h in ((1, 0), (2, 0), (2, 1), (1, 1), (3, 0), (3, 1)):
        share(n, h)

    def pair(n, h):
        part = slice(h * half, (h + 1) * half)
        twins[n][h].wait_recv()
        own = part_ref[CORES * chips[n] + core, part]
        return own.astype(F32) + twin[n, part].astype(F32)

    def put(n, h, value):
        part = slice(h * half, (h + 1) * half)
        go[n, part] = value.astype(BF16)
        return go.at[n, pl.ds(h * half, half)]

    side0 = copies.send(put(1, 0, pair(1, 0)), from_side.at[1], to_side)
    over1 = copies.send(put(2, 1, pair(2, 1)), from_over.at[2], to_over)
    yield
    share(0, 0)
    share(0, 1)
    far0 = copies.send(put(0, 0, pair(0, 0)), from_side.at[0], to_side)
    far1 = copies.send(put(0, 1, pair(0, 1)), from_over.at[0], to_over)
    yield
    value = pair(2, 0)
    far0.wait_recv()
    over0 = copies.send(put(2, 0, value + from_side[0].astype(F32)), from_over.at[1], to_over)
    value = pair(1, 1)
    far1.wait_recv()
    side1 = copies.send(put(1, 1, value + from_over[0].astype(F32)), from_side.at[2], to_side)
    yield
    first, second = pair(3, 0), pair(3, 1)
    side0.wait_recv()
    first = first + from_side[1].astype(F32)
    over1.wait_recv()
    second = second + from_over[2].astype(F32)
    over0.wait_recv()
    out_ref[0:half] = first + from_over[1].astype(F32)
    side1.wait_recv()
    out_ref[half:rows] = second + from_side[2].astype(F32)
    yield


def scatter_scratch(rows, width):
    return [
        pltpu.VMEM((PLANE, rows, width), BF16),
        pltpu.VMEM((3, rows // 2, width), BF16),
        pltpu.VMEM((3, rows // 2, width), BF16),
        pltpu.VMEM((3, rows, width), BF16),
    ]


def inward_stream(copies, own_ref, mid, out_ref):
    chip, line, core, side, over, far = spots()
    chunk = own_ref.shape[0] // PLANE

    def rows(q):
        return own_ref.at[pl.ds(q * chunk, chunk)]

    sent = [copies.send(rows(q[0]), mid.at[chip], q) for q in plane_partners()]
    local = copies.keep(rows(chip), mid.at[chip])
    yield
    local.wait()
    arrived(sent)
    moved = [copies.send(mid.at[q[1]], out_ref.at[line], q) for q in line_partners()[: PLANE - 1]]
    local = copies.keep(mid.at[line], out_ref.at[line])
    yield
    arrived(moved)
    local.wait()
    yield


def outward_stream(copies, own_ref, mid, out_ref):
    chip, line, core, side, over, far = spots()
    chunk = own_ref.shape[1]
    moved = [copies.send(own_ref.at[q[1]], mid.at[line], q) for q in line_partners()[: PLANE - 1]]
    local = copies.keep(own_ref.at[line], mid.at[line])
    yield
    local.wait()
    arrived(moved)
    target = out_ref.at[pl.ds(chip * chunk, chunk)]
    sent = [copies.send(mid.at[q[0]], target, q) for q in plane_partners()]
    local = copies.keep(mid.at[chip], target)
    yield
    arrived(sent)
    local.wait()
    yield


def columns_stream(copies, piece_ref, out_ref, lanes):
    chip, line, core, side, over, far = spots()
    mine = out_ref.at[CORES * line + core, :, lanes]
    sent = [copies.send(piece_ref.at[q[2], :, lanes], mine, q) for q in line_partners()]
    local = copies.keep(piece_ref.at[core, :, lanes], mine)
    yield
    arrived(sent)
    local.wait()
    yield


def rows_stream(copies, shard_ref, mid, out_ref):
    chip, line, core, side, over, far = spots()
    width = shard_ref.shape[1] // PLANE
    quarter = pl.ds(pl.multiple_of(chip * width, width), width)
    sent = [copies.send(shard_ref.at[:, quarter], mid.at[line], q) for q in line_partners()[: PLANE - 1]]
    local = copies.keep(shard_ref.at[:, quarter], mid.at[line])
    yield
    local.wait()
    arrived(sent)
    sent = [copies.send(mid.at[q[0]], out_ref.at[:, quarter], q) for q in plane_partners()]
    local = copies.keep(mid.at[chip], out_ref.at[:, quarter])
    yield
    arrived(sent)
    local.wait()
    yield


def unit_rows(value):
    inverse = lax.rsqrt(jnp.mean(value * value, axis=-1, keepdims=True) + EPS)
    return value * inverse, inverse


def comm_call(kernel, name, number, out_shape, in_specs, out_specs, scratch, vmem_mib=32):
    return pl.pallas_call(
        kernel,
        out_shape=out_shape,
        in_specs=in_specs,
        out_specs=out_specs,
        scratch_shapes=scratch + [pltpu.SemaphoreType.DMA((2, COPIES))],
        compiler_params=pltpu.CompilerParams(
            collective_id=number, has_side_effects=True, vmem_limit_bytes=vmem_mib << 20
        ),
        name=name,
    )


ANY = pl.BlockSpec(memory_space=pl.ANY)
IN_VMEM = pl.BlockSpec(memory_space=pltpu.VMEM)


def gains_of(line_ref, row):
    return jnp.concatenate([line_ref[s, row : row + 1, :] for s in range(line_ref.shape[0])], axis=1)


def column_grads_stream(copies, grad_ref, recv, sum_ref):
    chip, line, core, side, over, far = spots()
    sent = [
        copies.send(grad_ref.at[CORES * q[1] + q[2]], recv.at[core, line], q)
        for q in line_partners()
    ]
    local = copies.keep(grad_ref.at[CORES * line + core], recv.at[core, line])
    yield
    arrived(sent)
    local.wait()
    for number in range(CORES):
        total = recv[number, 0].astype(F32)
        for family in range(1, PLANE):
            total = total + recv[number, family].astype(F32)
        sum_ref[number] = total.astype(BF16)
    yield


def row_grads_stream(copies, grad_ref, mid, recv, summed, out_ref):
    chip, line, core, side, over, far = spots()
    width = out_ref.shape[1] // PLANE

    def quarter(q):
        return pl.ds(pl.multiple_of(q * width, width), width)

    sent = [copies.send(grad_ref.at[:, quarter(q[0])], mid.at[chip], q) for q in plane_partners()]
    local = copies.keep(grad_ref.at[:, quarter(chip)], mid.at[chip])
    yield
    local.wait()
    arrived(sent)
    sent = [copies.send(mid.at[q[1]], recv.at[line], q) for q in line_partners()[: PLANE - 1]]
    local = copies.keep(mid.at[line], recv.at[line])
    yield
    arrived(sent)
    local.wait()
    total = recv[0].astype(F32)
    for family in range(1, PLANE):
        total = total + recv[family].astype(F32)
    summed[...] = total.astype(BF16)
    sent = [copies.send(summed, out_ref.at[:, quarter(chip)], q) for q in plane_partners()]
    local = copies.keep(summed, out_ref.at[:, quarter(chip)])
    yield
    arrived(sent)
    local.wait()
    yield


def gain_grads_stream(copies, own, recv, summed, plane, out_ref):
    chip, line, core, side, over, far = spots()
    mine = CORES * line + core
    sent = [copies.send(own.at[CORES * q[1] + q[2]], recv.at[mine], q) for q in line_partners()]
    local = copies.keep(own.at[mine], recv.at[mine])
    yield
    arrived(sent)
    local.wait()
    summed[...] = jnp.sum(recv[...], axis=0)
    sent = [copies.send(summed, plane.at[chip], q) for q in plane_partners()]
    local = copies.keep(summed, plane.at[chip])
    yield
    arrived(sent)
    local.wait()
    out_ref[...] = jnp.sum(plane[...], axis=0)
    yield


def norm_back(grad, value, gain):
    unit, inverse = unit_rows(value)
    scaled = grad * gain
    back = inverse * (scaled - unit * jnp.mean(scaled * unit, axis=-1, keepdims=True))
    return back, jnp.sum(grad * unit, axis=0, keepdims=True)


def chunk_row(stored, part, chunk):
    plane, core, line = 2 * (stored % 2) + part, (stored // 2) % 2, stored // 4
    return ((plane * CORES + core) * PLANE + line) * chunk


def chosen(blocks, flags):
    value = blocks[0]
    for block, flag in zip(blocks[1:], flags[1:]):
        value = jnp.where(flag, block, value)
    return value


def in_place_order(table_ref, source, lanes, target, scale=None):
    chunk = BLK // 2
    blocks = source.shape[0] // BLK
    for place in range(blocks):
        flags = [table_ref[0, stored] == place for stored in range(blocks)]
        for part in range(2):
            rows = [chunk_row(stored, part, chunk) for stored in range(blocks)]
            block = chosen([source[row : row + chunk, lanes] for row in rows], flags)
            row = place * BLK + part * chunk
            target[row : row + chunk, :] = block if scale is None else block * scale


def in_gathered_order(table_ref, source, target, lanes):
    chunk = BLK // 2
    blocks = source.shape[0] // BLK
    for stored in range(blocks):
        flags = [table_ref[0, stored] == place for place in range(blocks)]
        for part in range(2):
            rows = [place * BLK + part * chunk for place in range(blocks)]
            block = chosen([source[row : row + chunk, :] for row in rows], flags)
            row = chunk_row(stored, part, chunk)
            target[row : row + chunk, lanes] = block


def attend_block(number, prompt, qs, ks, vt, att, ot_ref, lse_ref):
    start = number * CONT
    before = min(start, prompt)
    own_rows = slice(start, start + CONT)
    query = qs[own_rows, :]
    outs = []
    for head in range(2):
        masked = jnp.where(head_mask(CONT, head), query, jnp.zeros_like(query))
        own = dot_nt(ks[own_rows, :], masked)
        own = jnp.where(causal_mask(), own, -1e30)
        best = jnp.max(own, axis=0, keepdims=True)
        if before:
            past = dot_nt(ks[0:before, :], masked)
            best = jnp.maximum(best, jnp.max(past, axis=0, keepdims=True))
        terms = jnp.exp(own - best)
        total_terms = jnp.sum(terms, axis=0, keepdims=True)
        rows = slice(head * HEAD, (head + 1) * HEAD)
        out = matmul(vt[rows, own_rows], terms.astype(BF16))
        if before:
            terms = jnp.exp(past - best)
            total_terms = total_terms + jnp.sum(terms, axis=0, keepdims=True)
            out = out + matmul(vt[rows, 0:before], terms.astype(BF16))
        outs.append(out / total_terms)
        lse_ref[head : head + 1, own_rows] = best + jnp.log(total_terms)
    joined = jnp.concatenate(outs, axis=0)
    ot_ref[:, own_rows] = joined.astype(BF16)
    att[own_rows, :] = joined.T.astype(BF16)


def chip_slots(group):
    chip, line, core, side, over, far = spots()
    if group == 1:
        return 2 * CORES, lambda n: CORES * (side + lax.div(n, CORES) * (over - side)) + lax.rem(n, CORES)
    q = chip if group == 0 else far
    return CORES, lambda n: CORES * q + n


def each_slot(group, body):
    count, slot_of = chip_slots(group)

    @pl.loop(0, count)
    def _(n):
        body(slot_of(n))


def front_kernel(
    tok_ref, cot_ref, small_ref, table_ref, wq_ref, wk_ref, wv_ref, wo_ref, wg_ref, wu_ref, wd_ref,
    n1_out, x_ref, cotp_ref, line_ref, wqkv, wout, qs, ks, vs, ot_ref, lse_ref, att_ref,
    h1_ref, dn2_ref, mix_out, ggu_ref, gd_ref, table_out,
    *rest,
):
    scratch, other, rest = rest[:4], rest[4:8], rest[8:]
    mid_x, mid_c, mid_o, mid_d, tables, table, pieces, gate_w, up_w, gu, normed, rest = *rest[:11], rest[11:]
    n1s, n2s, cots, qkv, vt, att, parts, summed, wgu, wgu_t, wd, wd_t, us, dabs, sems = rest
    copies = Copies(sems)
    chip, line, core, side, over, far = spots()
    total, heads = qkv.shape[0], wo_ref.shape[0]
    hidden, lanes = wd_ref.shape[0], wd.shape[0]
    chunk, width = x_ref.shape[1], x_ref.shape[2]
    ranks = PLANE * CORES

    loads = [copies.keep(wg_ref, gate_w), copies.keep(wu_ref, up_w)]
    for c in range(CORES):
        column = pl.ds(pl.multiple_of((CORES * chip + c) * heads, heads), heads)
        for n, w in enumerate((wq_ref, wk_ref, wv_ref)):
            loads.append(copies.keep(w.at[:, column], pieces.at[c, :, n * heads : (n + 1) * heads]))
    copies.enter()
    tokens = inward_stream(copies, tok_ref, mid_x, x_ref)
    next(tokens)
    finished(loads)
    query_key = columns_stream(copies, pieces, wqkv, pl.ds(0, 2 * heads))
    next(query_key)
    mine = CORES * line + core
    small = [copies.send(small_ref, line_ref.at[mine], q) for q in line_partners()]
    small += [copies.send(table_ref, tables.at[chip], q) for q in plane_partners()]
    local = [copies.keep(small_ref, line_ref.at[mine]), copies.keep(table_ref, tables.at[chip])]
    gu[...] = jnp.zeros_like(gu)
    for k in range(PLANE):
        @pl.when(chip == k)
        def _():
            for c in range(CORES):
                begin = (CORES * k + c) * hidden
                gu[c, :, 0:hidden] = gate_w[:, begin : begin + hidden]
                gu[c, :, lanes : lanes + hidden] = up_w[:, begin : begin + hidden]
    wd[hidden:lanes] = jnp.zeros((lanes - hidden, width), BF16)
    next(tokens)
    cotangents = inward_stream(copies, cot_ref, mid_c, cotp_ref)
    next(cotangents)
    arrived(small)
    finished(local)
    load = [copies.keep(tables.at[line], table), copies.keep(tables.at[line], table_out)]
    next(tokens)
    value = columns_stream(copies, pieces, wqkv, pl.ds(2 * heads, heads))
    next(value)
    out_rows = rows_stream(copies, wo_ref, mid_o, wout)
    next(out_rows)
    finished(load)
    gain = gains_of(line_ref, 0)
    for n in range(PLANE):
        unit, ignored = unit_rows(x_ref[n].astype(F32))
        normed[n * chunk : (n + 1) * chunk] = (unit * gain).astype(BF16)
    gathering = copies.branch()
    gather = gather_stream(gathering, normed, n1s)
    next(gather)
    next(gather)
    next(gather)
    next(query_key)
    next(value)
    next(cotangents)

    def project(slot):
        rows = pl.ds(pl.multiple_of(slot * PLANE * chunk, PLANE * chunk), PLANE * chunk)
        qkv[rows, :] = matmul(n1s[slot], wqkv[...].reshape(width, 3 * heads)).astype(BF16)

    each_slot(0, project)
    next(gather)
    next(gather)
    each_slot(1, project)
    next(gather)
    next(out_rows)
    next(gather)
    each_slot(2, project)
    keep_n1 = copies.keep(n1s, n1_out)
    next(cotangents)
    gather_cot = gather_stream(copies, cotp_ref.reshape(PLANE * chunk, width), cots)
    next(gather_cot)
    gate_up = columns_stream(copies, gu, wgu, pl.ds(0, 2 * lanes))
    next(gate_up)
    down_rows = rows_stream(copies, wd_ref, mid_d, wd.at[pl.ds(0, hidden)])
    next(down_rows)

    for n, ref in enumerate((qs, ks, vs)):
        scale = jnp.bfloat16(SCALE) if n == 0 else None
        in_place_order(table, qkv, slice(n * heads, (n + 1) * heads), ref, scale)
    for start in range(0, total, CONT):
        rows = slice(start, start + CONT)
        vt[:, rows] = vs[rows, :].astype(F32).T.astype(BF16)
    for number in range(total // CONT):
        attend_block(number, total // 2, qs, ks, vt, att, ot_ref, lse_ref)
        if number == 4:
            next(gather_cot)
            next(gather_cot)
    next(gather_cot)
    in_gathered_order(table, att, att_ref, slice(0, heads))
    next(out_rows)

    def spread(slot):
        rows = pl.ds(pl.multiple_of(slot * PLANE * chunk, PLANE * chunk), PLANE * chunk)
        parts[slot] = matmul(att_ref[rows, :], wout[...]).astype(BF16)

    for group in range(3):
        each_slot(group, spread)
    scattering = copies.branch()
    scatter = scatter_stream(scattering, parts, summed, scratch)
    next(scatter)
    next(scatter)
    for ignored in gather_cot:
        pass
    next(scatter)
    next(scatter)
    gathering.finish()
    gain = gains_of(line_ref, 1)
    for n in range(PLANE):
        part = slice(n * chunk, (n + 1) * chunk)
        hidden_rows = x_ref[n].astype(F32) + summed[part]
        h1_ref[part] = hidden_rows
        unit, ignored = unit_rows(hidden_rows)
        normed[part] = (unit * gain).astype(BF16)
    gather = gather_stream(copies, normed, n2s)
    next(gather)
    next(gather)
    next(gather)
    next(gate_up)
    for s in range(ranks):
        wgu_t[:, s * heads : (s + 1) * heads] = wgu[s].T
    next(gather)
    next(down_rows)
    scattering.finish()
    next(down_rows)
    wd_t[...] = wd[...].T

    def feed(slot):
        block, cot = n2s[slot], cots[slot]
        both = matmul(block, wgu[...].reshape(width, 2 * lanes))
        gate, upper = both[:, :lanes], both[:, lanes:]
        bend = jnp.tanh(0.7978845608028654 * (gate + 0.044715 * gate * gate * gate))
        half = 0.5 * (1.0 + bend)
        active = gate * half
        slope = half + (0.5 * 0.7978845608028654) * gate * (1.0 - bend * bend) * (
            1.0 + 3 * 0.044715 * gate * gate
        )
        mixed = (active * upper).astype(BF16)
        us[slot] = mixed
        parts[slot] = matmul(mixed, wd[...]).astype(BF16)
        du = matmul(cot, wd_t[...])
        dabs[slot, :, 0:lanes] = (du * upper * slope).astype(BF16)
        dabs[slot, :, lanes:] = (du * active).astype(BF16)
        n1s[slot] = matmul(dabs[slot], wgu_t[...]).astype(BF16)

    keep_n1.wait()
    each_slot(0, feed)
    next(gather)
    each_slot(1, feed)
    next(gather)
    scatter = scatter_stream(copies, n1s, dn2_ref, other)
    next(scatter)
    next(gather)
    each_slot(2, feed)
    next(scatter)
    keep_mix = copies.keep(parts, mix_out)

    def tokens_of(ref, columns):
        return jnp.concatenate([ref[slot, :, columns] for slot in range(ranks)], axis=0)

    def by_rows(s):
        columns = pl.ds(pl.multiple_of(s * heads, heads), heads)
        grad = jnp.zeros((heads, 2 * lanes), F32)
        for slot in range(ranks):
            grad = grad + inner(n2s[slot, :, columns], dabs[slot])
        ggu_ref[s] = grad.astype(BF16)

    pl.loop(0, ranks // 2)(by_rows)
    next(scatter)
    pl.loop(ranks // 2, ranks)(by_rows)
    grad = jnp.zeros((lanes, width), F32)
    for slot in range(ranks):
        grad = grad + inner(us[slot], cots[slot])
    gd_ref[...] = grad[0:hidden].astype(BF16)
    next(scatter)
    keep_mix.wait()
    copies.finish()


def front(tokens, cotangent, small, table, w_query, w_key, w_value, w_out, w_gate, w_up, w_down):
    rows, width = tokens.shape
    heads, hidden = w_out.shape[0], w_down.shape[0]
    lanes = -(-hidden // 128) * 128
    ranks = PLANE * CORES
    total = ranks * rows
    chunks, blocks = (PLANE, rows // PLANE, width), (ranks, rows, width)
    low = lambda *shape: jax.ShapeDtypeStruct(shape, BF16)
    wide = lambda *shape: jax.ShapeDtypeStruct(shape, F32)
    shapes = (
        low(*blocks), low(*chunks), low(*chunks), wide(ranks, *small.shape), low(ranks, heads, 3 * heads),
        low(heads, width), low(total, heads), low(total, heads), low(total, heads), low(heads, total),
        wide(2, total), low(total, heads), wide(rows, width), wide(rows, width), low(*blocks),
        low(ranks, heads, 2 * lanes), low(hidden, width), jax.ShapeDtypeStruct(table.shape, jnp.int32),
    )
    held = lambda *shape: pltpu.VMEM(shape, BF16)
    scratch = scatter_scratch(rows, width) * 2
    scratch += [held(*chunks), held(*chunks), held(PLANE, heads, width // PLANE), held(PLANE, hidden, width // PLANE)]
    scratch += [pltpu.VMEM((PLANE,) + table.shape, jnp.int32), pltpu.SMEM(table.shape, jnp.int32)]
    scratch += [held(CORES, heads, 3 * heads), held(*w_gate.shape), held(*w_up.shape), held(CORES, heads, 2 * lanes)]
    scratch += [held(rows, width), held(*blocks), held(*blocks), held(*blocks), held(total, 3 * heads)]
    scratch += [held(heads, total), held(total, heads), held(*blocks), pltpu.VMEM((rows, width), F32)]
    scratch += [held(ranks, heads, 2 * lanes), held(2 * lanes, width), held(lanes, width), held(width, lanes)]
    scratch += [held(ranks, rows, lanes), held(ranks, rows, 2 * lanes)]
    return comm_call(
        front_kernel, "front", 1, shapes, [ANY] * 11,
        (ANY,) + (IN_VMEM,) * 13 + (ANY, IN_VMEM, IN_VMEM, ANY),
        scratch, 60,
    )(tokens, cotangent, small, table, w_query, w_key, w_value, w_out, w_gate, w_up, w_down)


def attend_back_block(number, prompt, qs, ks, vs, gs, kt, ot_ref, lse_ref, dqs, dks, dvs):
    start = number * CONT
    own = slice(start, start + CONT)
    query, grad = qs[own, :], gs[own, :]
    product = grad.astype(F32).T * ot_ref[:, own].astype(F32)
    outs = []
    for head in range(2):
        rows = slice(head * HEAD, (head + 1) * HEAD)
        delta = jnp.sum(product[rows], axis=0, keepdims=True)
        lse = lse_ref[head : head + 1, own]
        keep = head_mask(CONT, head)
        query_head = jnp.where(keep, query, jnp.zeros_like(query))
        grad_head = jnp.where(keep, grad, jnp.zeros_like(grad))
        dq = None
        for keys in [own] + ([slice(0, min(start, prompt))] if start else []):
            prob = jnp.exp(dot_nt(ks[keys, :], query_head) - lse)
            if keys == own:
                prob = jnp.where(causal_mask(), prob, 0.0)
            dprob = dot_nt(vs[keys, :], grad_head)
            dscore = (prob * (dprob - delta)).astype(BF16)
            dvs[keys, :] += matmul(prob.astype(BF16), grad_head)
            dks[keys, :] += matmul(dscore, query_head)
            term = matmul(kt[rows, keys], dscore)
            dq = term if dq is None else dq + term
        outs.append(dq)
    dqs[own, :] = (jnp.concatenate(outs, axis=0) * SCALE).T.astype(BF16)


def rear_kernel(
    table, summed_ref, h1_ref, cot_ref, x_ref, line_ref, n1_ref, mix_ref, wqkv_ref, wo_ref,
    qs, ks, vs, ot_ref, lse_ref, att_ref, gu_ref, down_ref,
    out_ref, grad_ref, gains_ref, gate_out, up_out, q_out, k_out, v_out, wo_all, wd_all,
    *rest,
):
    scratch, other, rest = rest[:4], rest[4:8], rest[8:]
    n1s, parts, gas, datt, gs, kt, dqs, dks, dvs, dqkv, w_t, rest = *rest[:11], rest[11:]
    dh1, summed, mixed, low, low_tok, low_out, mid_tok, mid_out, rest = *rest[:8], rest[8:]
    recv_gu, sum_gu, gu_all, gqkv, recv_qkv, sum_qkv, qkv_all, gwo, rest = *rest[:8], rest[8:]
    mid_wo, recv_wo, sum_wo, mid_wd, recv_wd, sum_wd, own, recv_gain, sum_gain, plane, sems = rest
    copies = Copies(sems)
    total, heads = att_ref.shape
    ranks = PLANE * CORES
    chunk, width = x_ref.shape[1], x_ref.shape[2]
    rows = PLANE * chunk
    hidden = down_ref.shape[0]
    lanes = gu_ref.shape[2] // 2
    load_mix, load_n1 = copies.keep(mix_ref, parts), copies.keep(n1_ref, n1s)
    copies.enter()
    gain = gains_of(line_ref, 1)
    gain2_sum = jnp.zeros((1, width), F32)
    for n in range(PLANE):
        part = slice(n * chunk, (n + 1) * chunk)
        back, by_gain = norm_back(summed_ref[part], h1_ref[part], gain)
        grad = cot_ref[n].astype(F32) + back
        gain2_sum = gain2_sum + by_gain
        dh1[part] = grad
        low[part] = grad.astype(BF16)
    gather = gather_stream(copies, low, gas)
    next(gather)
    gate_up = column_grads_stream(copies, gu_ref, recv_gu, sum_gu)
    next(gate_up)
    for start in range(0, total, CONT):
        part = slice(start, start + CONT)
        kt[:, part] = ks[part, :].astype(F32).T.astype(BF16)
    for s in range(ranks):
        w_t[:, s * heads : (s + 1) * heads] = wqkv_ref[s].T
    dks[...] = jnp.zeros_like(dks)
    dvs[...] = jnp.zeros_like(dvs)

    def slot_rows(slot):
        return pl.ds(pl.multiple_of(slot * rows, rows), rows)

    def attended_grad(slot):
        datt[slot_rows(slot), :] = outer(gas[slot], wo_ref[...]).astype(BF16)

    next(gather)
    each_slot(0, attended_grad)
    next(gather)
    next(gather)
    next(gather)
    each_slot(1, attended_grad)
    next(gather)
    load_mix.wait()
    mixing = copies.branch()
    second = scatter_stream(mixing, parts, mixed, other)
    next(second)
    next(gather)
    each_slot(2, attended_grad)
    in_place_order(table, datt, slice(0, heads), gs)
    down = row_grads_stream(copies, down_ref, mid_wd, recv_wd, sum_wd, wd_all)
    for number in range(total // CONT):
        attend_back_block(number, total // 2, qs, ks, vs, gs, kt, ot_ref, lse_ref, dqs, dks, dvs)
        if number == 1:
            next(second)
        if number == 4:
            next(second)
            next(down)
        if number == 6:
            next(gate_up)
            gather_gu = gather_stream(copies, sum_gu, gu_all, twin=False)
    next(second)
    for n in range(PLANE):
        part = slice(n * chunk, (n + 1) * chunk)
        low_out[n] = (h1_ref[part] + mixed[part]).astype(BF16)
    output = outward_stream(copies, low_out, mid_out, out_ref)
    next(output)
    ks_low, vs_low = gs, datt
    for start in range(0, total, CONT):
        part = slice(start, start + CONT)
        ks_low[part, :] = dks[part, :].astype(BF16)
        vs_low[part, :] = dvs[part, :].astype(BF16)
    for n, ref in enumerate((dqs, ks_low, vs_low)):
        in_gathered_order(table, ref, dqkv, slice(n * heads, (n + 1) * heads))
    mixing.finish()

    def spread(slot):
        parts[slot] = matmul(dqkv[slot_rows(slot), :], w_t[...]).astype(BF16)

    each_slot(1, spread)
    each_slot(0, spread)
    scatter = scatter_stream(copies, parts, summed, scratch)
    next(scatter)
    each_slot(2, spread)
    next(scatter)
    load_n1.wait()

    def by_rows(s):
        columns = pl.ds(pl.multiple_of(s * heads, heads), heads)
        grad = jnp.zeros((heads, 3 * heads), F32)
        for slot in range(ranks):
            grad = grad + inner(n1s[slot, :, columns], dqkv[slot * rows : (slot + 1) * rows, :])
        gqkv[s] = grad.astype(BF16)

    pl.loop(0, ranks)(by_rows)
    qkv = column_grads_stream(copies, gqkv, recv_qkv, sum_qkv)
    next(qkv)
    grad = jnp.zeros((heads, width), F32)
    for slot in range(ranks):
        grad = grad + inner(att_ref[slot * rows : (slot + 1) * rows, :], gas[slot])
    gwo[...] = grad.astype(BF16)
    next(scatter)
    next(scatter)
    gain = gains_of(line_ref, 0)
    gain1_sum = jnp.zeros((1, width), F32)
    for n in range(PLANE):
        part = slice(n * chunk, (n + 1) * chunk)
        back, by_gain = norm_back(summed[part], x_ref[n].astype(F32), gain)
        gain1_sum = gain1_sum + by_gain
        low_tok[n] = (dh1[part] + back).astype(BF16)
    tokens = outward_stream(copies, low_tok, mid_tok, grad_ref)
    next(tokens)
    own[...] = jnp.zeros_like(own)
    for s in range(ranks):
        part = slice(s * heads, (s + 1) * heads)
        own[s, 0:1] = gain1_sum[:, part]
        own[s, 1:2] = gain2_sum[:, part]
    gains = gain_grads_stream(copies, own, recv_gain, sum_gain, plane, gains_ref)
    next(gains)
    next(gather_gu)
    next(down)
    out_w = row_grads_stream(copies, gwo, mid_wo, recv_wo, sum_wo, wo_all)
    next(out_w)
    next(output)
    next(gather_gu)
    next(gather_gu)
    next(qkv)
    gather_qkv = gather_stream(copies, sum_qkv, qkv_all, twin=False)
    next(gather_qkv)
    next(out_w)
    next(tokens)
    next(gains)
    next(gather_gu)
    for ignored in gather_gu:
        pass
    next(down)
    for chip in range(PLANE):
        for c in range(CORES):
            begin = (CORES * chip + c) * hidden
            gate_out[:, begin : begin + hidden] = gu_all[chip, c, :, 0:hidden]
            up_out[:, begin : begin + hidden] = gu_all[chip, c, :, lanes : lanes + hidden]
    next(gather_qkv)
    next(gather_qkv)
    next(out_w)
    for ignored in gather_qkv:
        pass
    for chip in range(PLANE):
        for c in range(CORES):
            begin = (CORES * chip + c) * heads
            for n, ref in enumerate((q_out, k_out, v_out)):
                ref[:, begin : begin + heads] = qkv_all[chip, c, :, n * heads : (n + 1) * heads]
    for stream in (output, tokens, gains, down, out_w):
        for ignored in stream:
            pass
    copies.finish()


def rear(table, summed, h1, cot, x, lines, n1, mixed, w_qkv, w_o, qs, ks, vs, ot, lse, att, gate_up_grad, down_grad, ff):
    ranks = PLANE * CORES
    rows, width = h1.shape
    total, heads = att.shape
    hidden = down_grad.shape[0]
    quarter = width // PLANE
    small = lines.shape[1:]
    low = lambda *shape: jax.ShapeDtypeStruct(shape, BF16)
    shapes = (
        low(rows, width), low(rows, width), jax.ShapeDtypeStruct(small, F32),
        low(heads, ff), low(heads, ff), low(heads, width), low(heads, width), low(heads, width),
        low(heads, width), low(hidden, width),
    )
    held = lambda *shape: pltpu.VMEM(shape, BF16)
    wide = lambda *shape: pltpu.VMEM(shape, F32)
    scratch = scatter_scratch(rows, width) * 2
    scratch += [held(*n1.shape)] * 3 + [held(total, heads)] * 2 + [held(heads, total), held(total, heads)]
    scratch += [wide(total, heads)] * 2 + [held(total, 3 * heads), held(3 * heads, width)]
    scratch += [wide(rows, width)] * 3 + [held(rows, width)] + [held(*x.shape)] * 4
    for grad in (gate_up_grad, w_qkv):
        piece = (CORES,) + grad.shape[1:]
        if grad is w_qkv:
            scratch += [held(*grad.shape)]
        scratch += [held(CORES, PLANE, *grad.shape[1:]), held(*piece), held(PLANE, *piece)]
    scratch += [held(heads, width)]
    for count in (heads, hidden):
        scratch += [held(PLANE, count, quarter)] * 2 + [held(count, quarter)]
    scratch += [wide(*lines.shape)] * 2 + [wide(*small), wide(PLANE, *small)]
    return comm_call(
        rear_kernel, "rear", 2, shapes,
        [pl.BlockSpec(memory_space=pltpu.SMEM)] + [IN_VMEM] * 5 + [ANY] * 2 + [IN_VMEM] * 8 + [ANY] * 2,
        (ANY, ANY) + (IN_VMEM,) * 6 + (ANY, ANY),
        scratch, 60,
    )(table, summed, h1, cot, x, lines, n1, mixed, w_qkv, w_o, qs, ks, vs, ot, lse, att, gate_up_grad, down_grad)


def plane_local(
    tokens,
    cotangent,
    block_table,
    norm1_gain,
    w_query,
    w_key,
    w_value,
    w_out,
    norm2_gain,
    w_gate,
    w_up,
    w_down,
):
    rows, width = tokens.shape[1:]
    heads = width // (PLANE * CORES)
    small = jnp.stack([norm1_gain, norm2_gain]).astype(F32)
    small = jnp.pad(small, ((0, 6), (0, 0)))
    tables = jnp.pad(block_table, ((0, 7), (0, heads - block_table.shape[1])))
    (
        n1, x, cot, gains, w_qkv, w_o, qs, ks, vs, ot, lse, att, h1, dn2, mixed, g_gu, g_down, table
    ) = front(tokens[0], cotangent[0], small, tables, w_query, w_key, w_value, w_out, w_gate, w_up, w_down)
    output, tokens_grad, gain_grads, *grads = rear(
        table, dn2, h1, cot, x, gains, n1, mixed, w_qkv, w_o, qs, ks, vs, ot, lse, att, g_gu, g_down,
        w_gate.shape[1],
    )
    gate, up, query, key, value, out, down = [grad.astype(F32) for grad in grads]
    return (
        output[None], tokens_grad[None],
        gain_grads[0], query, key, value, out, gain_grads[1], gate, up, down,
    )


def plane_solution(mesh):
    split = Mesh(mesh.devices.reshape(PLANE, PLANE, CORES), ("group", "z", "core"))
    ctx = ("z", "core")
    token, weight = P("group", ctx, None), P(ctx, None)
    in_specs = (token, token, P("group", None), P(ctx)) + (weight,) * 4 + (P(ctx),) + (weight,) * 3
    out_specs = (token, token, P(ctx)) + (weight,) * 4 + (P(ctx),) + (weight,) * 3
    return jax.shard_map(
        plane_local, mesh=split, in_specs=in_specs, out_specs=out_specs, check_vma=False
    )


def family_solution(mesh):
    in_specs = (
        P("group", "ctx", None),
        P("group", "ctx", None),
        P("group", None),
        P("ctx"),
        P("ctx", None),
        P("ctx", None),
        P("ctx", None),
        P("ctx", None),
        P("ctx"),
        P("ctx", None),
        P("ctx", None),
        P("ctx", None),
    )
    out_specs = (
        P("group", "ctx", None),
        P("group", "ctx", None),
        P("ctx"),
        P("ctx", None),
        P("ctx", None),
        P("ctx", None),
        P("ctx", None),
        P("ctx"),
        P("ctx", None),
        P("ctx", None),
        P("ctx", None),
    )
    return jax.shard_map(local, mesh=mesh, in_specs=in_specs, out_specs=out_specs, check_vma=False)


def solution(mesh):
    groups, ranks = mesh.shape["group"], mesh.shape["ctx"]
    if groups == PLANE and ranks == 2 * PLANE:
        return plane_solution(mesh)
    return family_solution(mesh)
```

```python
import jax
import jax.numpy as jnp
from jax import lax
from jax.experimental import pallas as pl
from jax.experimental.pallas import tpu as pltpu
from jax.sharding import Mesh
from jax.sharding import PartitionSpec as P

HEADS = 16
HEAD = 64
BLK = 128
KEYBLK = 512
PROMPT_MAX = 2048
CONT = 256


EPS = 1e-06
SCALE = 0.125


def rms_scale(hidden, gain):
    return hidden * lax.rsqrt(jnp.mean(hidden * hidden, axis=-1, keepdims=True) + EPS) * gain


def gated(gate, upper):
    return jax.nn.gelu(gate, approximate=True) * upper


def matmul(left, right):
    return jnp.dot(left, right, preferred_element_type=jnp.float32)


def inner(left, right):
    return lax.dot_general(
        left, right, (((0,), (0,)), ((), ())), preferred_element_type=jnp.float32
    )


def outer(left, right):
    return lax.dot_general(
        left, right, (((1,), (1,)), ((), ())), preferred_element_type=jnp.float32
    )


def family_index(table):
    offsets = jnp.arange(BLK, dtype=jnp.int32)
    return (table[:, None] * BLK + offsets[None, :]).reshape(-1)


def segment_of(index, prompt_len):
    return jnp.where(index < prompt_len, 0, 1 + (index - prompt_len) // CONT)


def allowed(query_index, key_index, prompt_len):
    query_seg = segment_of(query_index, prompt_len)
    key_seg = segment_of(key_index, prompt_len)
    same = (query_seg[:, None] == key_seg[None, :]) & (key_index[None, :] <= query_index[:, None])
    prompt = (key_seg[None, :] == 0) & (query_seg[:, None] > 0)
    return same | prompt


def head_split(block):
    return block.reshape(block.shape[0], HEADS, HEAD)


def scores_of(query_heads, key_block, query_index, key_index, prompt_len):
    score = (
        jnp.einsum(
            "qhd,khd->hqk", query_heads, head_split(key_block), preferred_element_type=jnp.float32
        )
        * SCALE
    )
    return (score, allowed(query_index, key_index, prompt_len))


def attend_stats(queries, keys, query_index, key_index, prompt_len):
    query_heads = head_split(queries)

    def step(carry, number):
        best, total = carry
        start = number * KEYBLK
        key_block = lax.dynamic_slice_in_dim(keys, start, KEYBLK, 0)
        block_index = lax.dynamic_slice_in_dim(key_index, start, KEYBLK, 0)
        score, keep = scores_of(query_heads, key_block, query_index, block_index, prompt_len)
        score = jnp.where(keep[None], score, -1e30)
        larger = jnp.maximum(best, jnp.max(score, axis=-1))
        terms = jnp.where(keep[None], jnp.exp(score - larger[:, :, None]), 0.0)
        total = total * jnp.exp(best - larger) + jnp.sum(terms, axis=-1)
        return ((larger, total), None)

    start_best = jnp.full((HEADS, queries.shape[0]), -1e30, jnp.float32)
    (best, total), ignored = lax.scan(
        step, (start_best, jnp.zeros_like(start_best)), jnp.arange(keys.shape[0] // KEYBLK)
    )
    return best + jnp.log(total)


def attend_values(queries, keys, values, lse, query_index, key_index, prompt_len):
    query_heads = head_split(queries)

    def step(acc, number):
        start = number * KEYBLK
        key_block = lax.dynamic_slice_in_dim(keys, start, KEYBLK, 0)
        value_block = lax.dynamic_slice_in_dim(values, start, KEYBLK, 0)
        block_index = lax.dynamic_slice_in_dim(key_index, start, KEYBLK, 0)
        score, keep = scores_of(query_heads, key_block, query_index, block_index, prompt_len)
        prob = jnp.where(keep[None], jnp.exp(score - lse[:, :, None]), 0.0).astype(jnp.bfloat16)
        return (
            acc
            + jnp.einsum(
                "hqk,khd->qhd", prob, head_split(value_block), preferred_element_type=jnp.float32
            ),
            None,
        )

    start_acc = jnp.zeros((queries.shape[0], HEADS, HEAD), jnp.float32)
    acc, ignored = lax.scan(step, start_acc, jnp.arange(keys.shape[0] // KEYBLK))
    return acc.reshape(queries.shape[0], HEADS * HEAD)


def block_grads(query_heads, grad_heads, key_block, value_block, lse, delta, keep):
    key_heads = head_split(key_block)
    value_heads = head_split(value_block)
    score = (
        jnp.einsum("qhd,khd->hqk", query_heads, key_heads, preferred_element_type=jnp.float32)
        * SCALE
    )
    prob = jnp.where(keep[None], jnp.exp(score - lse[:, :, None]), 0.0)
    dvalue = jnp.einsum(
        "hqk,qhd->khd", prob.astype(jnp.bfloat16), grad_heads, preferred_element_type=jnp.float32
    )
    dprob = jnp.einsum("qhd,khd->hqk", grad_heads, value_heads, preferred_element_type=jnp.float32)
    dscore = (prob * (dprob - delta[:, :, None])).astype(jnp.bfloat16)
    dquery = (
        jnp.einsum("hqk,khd->qhd", dscore, key_heads, preferred_element_type=jnp.float32) * SCALE
    )
    dkey = (
        jnp.einsum("hqk,qhd->khd", dscore, query_heads, preferred_element_type=jnp.float32) * SCALE
    )
    return (dquery, dkey, dvalue)


def local(
    tokens,
    cotangent,
    block_table,
    norm1_gain,
    w_query,
    w_key,
    w_value,
    w_out,
    norm2_gain,
    w_gate,
    w_up,
    w_down,
):
    row_count = tokens.shape[1]
    width = tokens.shape[2]
    every_index = family_index(block_table[0])
    prompt_len = min(PROMPT_MAX, every_index.shape[0] // 2)
    own_index = lax.dynamic_slice_in_dim(
        every_index, lax.axis_index("ctx") * row_count, row_count, 0
    )
    gain1, wq_full, wk_full, wv_full, wo_full = (
        lax.all_gather(norm1_gain, "ctx", axis=0, tiled=True),
        lax.all_gather(w_query, "ctx", axis=0, tiled=True),
        lax.all_gather(w_key, "ctx", axis=0, tiled=True),
        lax.all_gather(w_value, "ctx", axis=0, tiled=True),
        lax.all_gather(w_out, "ctx", axis=0, tiled=True),
    )
    inputs = tokens[0].astype(jnp.float32)
    normed1, norm1_pull = jax.vjp(rms_scale, inputs, gain1.astype(jnp.float32))
    first_low = normed1.astype(jnp.bfloat16)
    queries = matmul(first_low, wq_full).astype(jnp.bfloat16)
    keys_own = matmul(first_low, wk_full).astype(jnp.bfloat16)
    values_own = matmul(first_low, wv_full).astype(jnp.bfloat16)
    keys_all, values_all = (
        lax.all_gather(keys_own, "ctx", axis=0, tiled=True),
        lax.all_gather(values_own, "ctx", axis=0, tiled=True),
    )
    lse = attend_stats(queries, keys_all, own_index, every_index, prompt_len)
    attended_wide = attend_values(
        queries, keys_all, values_all, lse, own_index, every_index, prompt_len
    )
    attended = attended_wide.astype(jnp.bfloat16)
    hidden = inputs + matmul(attended, wo_full)
    gain2, wg_full, wu_full, wd_full = (
        lax.all_gather(norm2_gain, "ctx", axis=0, tiled=True),
        lax.all_gather(w_gate, "ctx", axis=0, tiled=True),
        lax.all_gather(w_up, "ctx", axis=0, tiled=True),
        lax.all_gather(w_down, "ctx", axis=0, tiled=True),
    )
    normed2, norm2_pull = jax.vjp(rms_scale, hidden, gain2.astype(jnp.float32))
    second_low = normed2.astype(jnp.bfloat16)
    gate = matmul(second_low, wg_full)
    upper = matmul(second_low, wu_full)
    mixed_wide, gate_pull = jax.vjp(gated, gate, upper)
    mixed = mixed_wide.astype(jnp.bfloat16)
    result = hidden + matmul(mixed, wd_full)
    output = result.astype(jnp.bfloat16)[None]
    grad_low = cotangent[0]
    grad_down = inner(mixed, grad_low)
    dmixed = outer(grad_low, wd_full)
    dgate, dupper = gate_pull(dmixed)
    dgate_low = dgate.astype(jnp.bfloat16)
    dupper_low = dupper.astype(jnp.bfloat16)
    grad_gate = inner(second_low, dgate_low)
    grad_up = inner(second_low, dupper_low)
    dnormed2 = outer(dgate_low, wg_full) + outer(dupper_low, wu_full)
    dhidden_norm, grad_gain2 = norm2_pull(dnormed2)
    dhidden = grad_low.astype(jnp.float32) + dhidden_norm
    attn_low = dhidden.astype(jnp.bfloat16)
    grad_out_w = inner(attended, attn_low)
    dattended = outer(attn_low, wo_full).astype(jnp.bfloat16)
    delta = jnp.sum(
        (dattended.astype(jnp.float32) * attended_wide).reshape(row_count, HEADS, HEAD), axis=-1
    ).T
    query_heads = head_split(queries)
    grad_heads = head_split(dattended)

    def key_step(carry, number):
        start = number * KEYBLK
        key_block = lax.dynamic_slice_in_dim(keys_all, start, KEYBLK, 0)
        value_block = lax.dynamic_slice_in_dim(values_all, start, KEYBLK, 0)
        block_index = lax.dynamic_slice_in_dim(every_index, start, KEYBLK, 0)
        keep = allowed(own_index, block_index, prompt_len)
        dquery, dkey, dvalue = block_grads(
            query_heads, grad_heads, key_block, value_block, lse, delta, keep
        )
        joined = jnp.concatenate(
            [dkey.reshape(KEYBLK, width), dvalue.reshape(KEYBLK, width)], axis=1
        )
        return (carry + dquery, joined)

    start_query = jnp.zeros((row_count, HEADS, HEAD), jnp.float32)
    query_sum, key_terms = lax.scan(
        key_step, start_query, jnp.arange(every_index.shape[0] // KEYBLK)
    )
    summed = lax.psum_scatter(
        key_terms.reshape(every_index.shape[0], 2 * width).astype(jnp.bfloat16),
        "ctx",
        scatter_dimension=0,
        tiled=True,
    ).astype(jnp.float32)
    query_grad = query_sum.reshape(row_count, width)
    key_grad = summed[:, :width]
    value_grad = summed[:, width:]
    query_low = query_grad.astype(jnp.bfloat16)
    key_low = key_grad.astype(jnp.bfloat16)
    value_low = value_grad.astype(jnp.bfloat16)
    grad_query = inner(first_low, query_low)
    grad_key = inner(first_low, key_low)
    grad_value = inner(first_low, value_low)
    dnormed1 = outer(query_low, wq_full) + outer(key_low, wk_full) + outer(value_low, wv_full)
    dinput_norm, grad_gain1 = norm1_pull(dnormed1)
    tokens_grad = (dhidden + dinput_norm).astype(jnp.bfloat16)[None]
    shards = (
        lax.psum_scatter(
            grad_gain1.astype(jnp.bfloat16), "ctx", scatter_dimension=0, tiled=True
        ).astype(jnp.float32),
        lax.psum_scatter(
            grad_query.astype(jnp.bfloat16), "ctx", scatter_dimension=0, tiled=True
        ).astype(jnp.float32),
        lax.psum_scatter(
            grad_key.astype(jnp.bfloat16), "ctx", scatter_dimension=0, tiled=True
        ).astype(jnp.float32),
        lax.psum_scatter(
            grad_value.astype(jnp.bfloat16), "ctx", scatter_dimension=0, tiled=True
        ).astype(jnp.float32),
        lax.psum_scatter(
            grad_out_w.astype(jnp.bfloat16), "ctx", scatter_dimension=0, tiled=True
        ).astype(jnp.float32),
        lax.psum_scatter(
            grad_gain2.astype(jnp.bfloat16), "ctx", scatter_dimension=0, tiled=True
        ).astype(jnp.float32),
        lax.psum_scatter(
            grad_gate.astype(jnp.bfloat16), "ctx", scatter_dimension=0, tiled=True
        ).astype(jnp.float32),
        lax.psum_scatter(
            grad_up.astype(jnp.bfloat16), "ctx", scatter_dimension=0, tiled=True
        ).astype(jnp.float32),
        lax.psum_scatter(
            grad_down.astype(jnp.bfloat16), "ctx", scatter_dimension=0, tiled=True
        ).astype(jnp.float32),
    )
    shards = (
        lax.psum(shards[0].astype(jnp.bfloat16), "group").astype(jnp.float32),
        lax.psum(shards[1].astype(jnp.bfloat16), "group").astype(jnp.float32),
        lax.psum(shards[2].astype(jnp.bfloat16), "group").astype(jnp.float32),
        lax.psum(shards[3].astype(jnp.bfloat16), "group").astype(jnp.float32),
        lax.psum(shards[4].astype(jnp.bfloat16), "group").astype(jnp.float32),
        lax.psum(shards[5].astype(jnp.bfloat16), "group").astype(jnp.float32),
        lax.psum(shards[6].astype(jnp.bfloat16), "group").astype(jnp.float32),
        lax.psum(shards[7].astype(jnp.bfloat16), "group").astype(jnp.float32),
        lax.psum(shards[8].astype(jnp.bfloat16), "group").astype(jnp.float32),
    )
    return (
        output,
        tokens_grad,
        shards[0],
        shards[1],
        shards[2],
        shards[3],
        shards[4],
        shards[5],
        shards[6],
        shards[7],
        shards[8],
    )


PLANE = 4
CORES = 2
TP = ("group", "core")
F32 = jnp.float32
BF16 = jnp.bfloat16


def dot_nt(left, right):
    return lax.dot_general(left, right, (((1,), (1,)), ((), ())), preferred_element_type=F32)


def head_mask(rows, head):
    lane = lax.broadcasted_iota(jnp.int32, (rows, 2 * HEAD), 1)
    return (lane >= head * HEAD) & (lane < (head + 1) * HEAD)


def causal_mask():
    key = lax.broadcasted_iota(jnp.int32, (CONT, CONT), 0)
    query = lax.broadcasted_iota(jnp.int32, (CONT, CONT), 1)
    return key <= query


MESH = pl.DeviceIdType.MESH


def spots():
    chip, line, core = lax.axis_index("group"), lax.axis_index("z"), lax.axis_index("core")
    side = chip + 1 - 2 * lax.rem(chip, 2)
    over = lax.rem(chip + 2, PLANE)
    far = PLANE - 1 - chip
    return chip, line, core, side, over, far


def plane_partners():
    chip, line, core, side, over, far = spots()
    return [(q, line, core) for q in (far, side, over)]


def line_partners():
    chip, line, core, side, over, far = spots()
    lines = [lax.rem(line + d, PLANE) for d in range(1, PLANE)]
    same = [(chip, z, core) for z in lines]
    return same + [(chip, z, 1 - core) for z in lines] + [(chip, line, 1 - core)]


class Copies:
    def __init__(self, sems, parent=None):
        self.sems, self.parent = sems, parent
        self.counts, self.started, self.branches = [0, 0], [], []

    def branch(self):
        self.branches.append(Copies(self.sems, self))
        return self.branches[-1]

    def number(self, side=0):
        if self.parent is not None:
            return self.parent.number(side)
        self.counts[side] += 1
        return self.counts[side] - 1

    def left(self):
        return self.sems[0].at[self.number(0)]

    def enter(self, crossing=False):
        barrier = pltpu.get_barrier_semaphore()
        partners = plane_partners() + line_partners()
        chip, line, core, side, over, far = spots()
        if crossing:
            partners += [(line, lax.rem(line + d, PLANE), core) for d in range(1, PLANE)]
            partners += [(lax.rem(chip + d, PLANE), chip, core) for d in range(1, PLANE)]

        def greet(partner):
            pl.semaphore_signal(barrier, inc=1, device_id=partner, device_id_type=MESH)

        for partner in partners:
            greet(partner)
        if not crossing:
            pl.semaphore_wait(barrier, len(partners))
            return

        @pl.when(chip != line)
        def _():
            greet((line, line, core))
            greet((chip, chip, core))
            pl.semaphore_wait(barrier, len(partners) + 2)

        @pl.when(chip == line)
        def _():
            pl.semaphore_wait(barrier, len(partners))

    def send(self, source, target, partner):
        copy = pltpu.make_async_remote_copy(
            src_ref=source,
            dst_ref=target,
            send_sem=self.left(),
            recv_sem=self.sems[1].at[self.number(1)],
            device_id=partner,
            device_id_type=MESH,
        )
        copy.start()
        self.started.append(copy)
        return copy

    def keep(self, source, target):
        copy = pltpu.make_async_copy(source, target, self.left())
        copy.start()
        return copy

    def finish(self):
        for copy in self.started:
            copy.wait_send()
        self.started = []
        for branch in self.branches:
            branch.finish()


def arrived(copies):
    for copy in copies:
        copy.wait_recv()


def finished(copies):
    for copy in copies:
        copy.wait()


def gather_stream(copies, own_ref, out_ref, twin=True):
    chip, line, core, side, over, far = spots()
    half = own_ref.shape[0] // 2
    to_far, to_side, to_over = plane_partners()
    to_twin = (chip, line, 1 - core)

    def slot_of(q):
        return CORES * q + core if twin else q

    def part(slot, number):
        return out_ref.at[slot, pl.ds(number * half, half)]

    def own(number):
        return own_ref.at[pl.ds(number * half, half)]

    def on(slot, number, partner):
        return copies.send(part(slot, number), part(slot, number), partner)

    def share(slot, number):
        return [on(slot, number, to_twin)] if twin else []

    mine, slot_side, slot_over, slot_far = map(slot_of, (chip, side, over, far))
    sides, overs = [None, None], [None, None]
    overs[0] = copies.send(own(0), part(mine, 0), to_over)
    sides[1] = copies.send(own(1), part(mine, 1), to_side)
    sides[0] = copies.send(own(0), part(mine, 0), to_side)
    overs[1] = copies.send(own(1), part(mine, 1), to_over)
    twins = [copies.send(own(h), part(mine, h), to_twin) for h in range(2)] if twin else []
    local = copies.keep(own_ref, out_ref.at[mine])
    yield
    local.wait()
    arrived(twins)
    yield
    overs[0].wait_recv()
    far0 = on(slot_over, 0, to_side)
    twins = share(slot_over, 0)
    sides[1].wait_recv()
    far1 = on(slot_side, 1, to_over)
    twins += share(slot_side, 1)
    yield
    sides[0].wait_recv()
    twins += share(slot_side, 0)
    overs[1].wait_recv()
    twins += share(slot_over, 1)
    yield
    arrived(twins)
    yield
    far0.wait_recv()
    twins = share(slot_far, 0)
    far1.wait_recv()
    twins += share(slot_far, 1)
    yield
    arrived(twins)
    yield


class Scatter:
    def __init__(self, copies, part_ref, out_ref, scratch):
        self.copies, self.part_ref, self.out_ref = copies, part_ref, out_ref
        self.twin, self.from_side, self.from_over, self.go = scratch
        chip, line, self.core, side, over, far = spots()
        self.half = out_ref.shape[0] // 2
        ignored, self.to_side, self.to_over = plane_partners()
        self.to_twin = (chip, line, 1 - self.core)
        self.chips = (far, side, over, chip)
        self.twins = [None] * 4

    def share(self, *numbers):
        for n in numbers:
            self.twins[n] = []
            for h in range(2):
                rows = pl.ds(h * self.half, self.half)
                source = self.part_ref.at[CORES * self.chips[n] + 1 - self.core, rows]
                self.twins[n].append(self.copies.send(source, self.twin.at[n, rows], self.to_twin))

    def _pair(self, n, h):
        part = slice(h * self.half, (h + 1) * self.half)
        self.twins[n][h].wait_recv()
        own = self.part_ref[CORES * self.chips[n] + self.core, part]
        return own.astype(F32) + self.twin[n, part].astype(F32)

    def _send(self, n, h, value, target, partner):
        self.go[n, h * self.half : (h + 1) * self.half] = value.astype(BF16)
        return self.copies.send(self.go.at[n, pl.ds(h * self.half, self.half)], target, partner)

    def far(self):
        self.far0 = self._send(0, 0, self._pair(0, 0), self.from_side.at[0], self.to_side)
        self.far1 = self._send(0, 1, self._pair(0, 1), self.from_over.at[0], self.to_over)

    def side(self):
        self.side0 = self._send(1, 0, self._pair(1, 0), self.from_side.at[1], self.to_side)

    def over(self):
        self.over1 = self._send(2, 1, self._pair(2, 1), self.from_over.at[2], self.to_over)

    def cross(self):
        value = self._pair(2, 0)
        self.far0.wait_recv()
        value = value + self.from_side[0].astype(F32)
        self.over0 = self._send(2, 0, value, self.from_over.at[1], self.to_over)
        value = self._pair(1, 1)
        self.far1.wait_recv()
        value = value + self.from_over[0].astype(F32)
        self.side1 = self._send(1, 1, value, self.from_side.at[2], self.to_side)

    def end(self):
        first, second = self._pair(3, 0), self._pair(3, 1)
        self.side0.wait_recv()
        first = first + self.from_side[1].astype(F32)
        self.over1.wait_recv()
        second = second + self.from_over[2].astype(F32)
        self.over0.wait_recv()
        self.out_ref[0 : self.half] = first + self.from_over[1].astype(F32)
        self.side1.wait_recv()
        self.out_ref[self.half :] = second + self.from_side[2].astype(F32)


def scatter_scratch(rows, width):
    return [
        pltpu.VMEM((PLANE, rows, width), BF16),
        pltpu.VMEM((3, rows // 2, width), BF16),
        pltpu.VMEM((3, rows // 2, width), BF16),
        pltpu.VMEM((3, rows, width), BF16),
    ]


def inward_stream(copies, own_ref, mid, out_ref):
    chip, line, core, side, over, far = spots()
    chunk = own_ref.shape[0] // PLANE
    half = chunk // 2
    sent, moved, local = [[], []], [], []
    for h in range(2):
        part = pl.ds(h * half, half)
        for q in plane_partners():
            rows = own_ref.at[pl.ds(q[0] * chunk + h * half, half)]
            sent[h].append(copies.send(rows, mid.at[chip, part], q))
    local = [copies.keep(own_ref.at[pl.ds(chip * chunk, chunk)], mid.at[chip])]
    yield
    finished(local)
    for h in range(2):
        part = pl.ds(h * half, half)
        arrived(sent[h])
        for q in line_partners()[: PLANE - 1]:
            moved.append(copies.send(mid.at[q[1], part], out_ref.at[line, part], q))
    local = copies.keep(mid.at[line], out_ref.at[line])
    yield
    arrived(moved)
    local.wait()
    yield


class Outward:
    def __init__(self, copies, own_ref, out_ref):
        self.chip, self.line, self.core = (lax.axis_index(name) for name in ("group", "z", "core"))
        self.copies, self.chunk, self.out_ref = copies, own_ref.shape[1], out_ref
        self.arrive = [copies.number(1) for ignored in range(PLANE)]
        self.sends, self.away = [], self.chip != self.line
        for d in range(PLANE):
            z = lax.rem(self.line + d, PLANE)
            copy = self._copy(own_ref.at[z], self.chip, z, copies.left())
            self.sends.append(copy)
            if d:
                copy.start()
        self.local = pltpu.make_async_copy(
            own_ref.at[self.line], self._rows(self.chip), copies.left()
        )

        @pl.when(self.away)
        def _():
            self.sends[0].start()

        @pl.when(self.chip == self.line)
        def _():
            self.local.start()

    def _rows(self, chip):
        return self.out_ref.at[pl.ds(pl.multiple_of(chip * self.chunk, self.chunk), self.chunk)]

    def _copy(self, source, chip, z, left):
        return pltpu.make_async_remote_copy(
            src_ref=source,
            dst_ref=self._rows(chip),
            send_sem=left,
            recv_sem=self.copies.sems[1].at[self.arrive[0] + chip],
            device_id=(self.line, z, self.core),
            device_id_type=MESH,
        )

    def wait(self):
        for chip in range(PLANE):
            copy = self._copy(self._rows(chip), chip, self.line, self.copies.sems[0].at[0])

            @pl.when((chip != self.chip) | self.away)
            def _():
                copy.wait_recv()

        @pl.when(self.chip == self.line)
        def _():
            self.local.wait()

        @pl.when(self.away)
        def _():
            self.sends[0].wait_send()

        for copy in self.sends[1:]:
            copy.wait_send()


def columns_stream(copies, piece_ref, out_ref, lanes):
    chip, line, core, side, over, far = spots()
    mine = out_ref.at[CORES * line + core, :, lanes]
    sent = [copies.send(piece_ref.at[q[2], :, lanes], mine, q) for q in line_partners()]
    local = copies.keep(piece_ref.at[core, :, lanes], mine)
    yield
    arrived(sent)
    local.wait()
    yield


class Relay:
    def __init__(self, copies, piece, slot, both=True):
        self.line, self.core = lax.axis_index("z"), lax.axis_index("core")
        self.copies, self.slot, self.both = copies, slot, both
        self.cores = range(CORES) if both else (self.core,)
        self.twin = None
        count = PLANE * CORES if both else PLANE
        self.arrive = [copies.number(1) for ignored in range(count)]
        self.sends = []
        mine = slot(self.line, self.core)
        if both:
            self.twin = self._copy(piece(1 - self.core), mine, self.line, self.core, self.line, 1 - self.core, copies.left())
            self.twin.start()
        self.local = copies.keep(piece(self.core), mine)
        for step in (1, -1):
            for core in self.cores:
                copy = self._copy(piece(core), mine, self.line, self.core, self.line + step, core, copies.left())
                self._start(self._inside(self.line + step), copy)

    def _inside(self, z):
        return (z >= 0) & (z < PLANE)

    def _sem(self, z, core):
        number = CORES * z + core if self.both else z
        return self.copies.sems[1].at[self.arrive[0] + number]

    def _copy(self, source, target, z, core, to, to_core, left=None):
        return pltpu.make_async_remote_copy(
            src_ref=source,
            dst_ref=target,
            send_sem=self.copies.sems[0].at[0] if left is None else left,
            recv_sem=self._sem(z, core),
            device_id=(lax.axis_index("group"), to, to_core),
            device_id_type=MESH,
        )

    def _start(self, when, copy):
        @pl.when(when)
        def _():
            copy.start()

        self.sends.append((when, copy))

    def hop(self, distance):
        if distance == 1:
            self.local.wait()
            if self.both:
                self._copy(*[self.slot(self.line, 1 - self.core)] * 2, self.line, 1 - self.core, self.line, self.core).wait_recv()
        for step in (1, -1):
            z = self.line - step * distance
            there, on = self._inside(z), self._inside(z) & self._inside(self.line + step)
            for core in self.cores:
                slot = self.slot(jnp.clip(z, 0, PLANE - 1), core)
                left = self.copies.left() if distance < PLANE - 1 else None
                copy = self._copy(slot, slot, jnp.clip(z, 0, PLANE - 1), core, self.line + step, self.core, left)

                @pl.when(there)
                def _():
                    copy.wait_recv()

                if distance < PLANE - 1:
                    self._start(on, copy)

    def finish(self):
        if self.both:
            self.twin.wait_send()
        for when, copy in self.sends:
            @pl.when(when)
            def _():
                copy.wait_send()


def columns_relay(copies, piece_ref, out_ref, lanes):
    return Relay(
        copies,
        lambda core: piece_ref.at[core, :, lanes],
        lambda z, core: out_ref.at[CORES * z + core, :, lanes],
    )


def sum_stream(copies, grad_ref, recv, sum_ref):
    chip, line, core, side, over, far = spots()
    sent = [
        copies.send(grad_ref.at[q[1]], recv.at[line], q) for q in line_partners()[: PLANE - 1]
    ]
    local = copies.keep(grad_ref.at[line], recv.at[line])
    yield
    arrived(sent)
    local.wait()
    total = recv[0].astype(F32)
    for family in range(1, PLANE):
        total = total + recv[family].astype(F32)
    sum_ref[...] = total.astype(BF16)
    yield


def quarter_columns(ref, number):
    width = ref.shape[1] // PLANE
    return ref.at[:, pl.ds(pl.multiple_of(number * width, width), width)]


def to_ranks_stream(copies, mid, out_ref):
    chip, line, core, side, over, far = spots()
    target = quarter_columns(out_ref, chip)
    sent = [copies.send(mid.at[q[0]], target, q) for q in plane_partners()]
    local = copies.keep(mid.at[chip], target)
    yield
    arrived(sent)
    local.wait()
    yield


def unit_rows(value):
    inverse = lax.rsqrt(jnp.mean(value * value, axis=-1, keepdims=True) + EPS)
    return value * inverse, inverse


def comm_call(kernel, name, number, out_shape, in_specs, out_specs, scratch, sends, arrivals, vmem_mib=60):
    return pl.pallas_call(
        kernel,
        out_shape=out_shape,
        in_specs=in_specs,
        out_specs=out_specs,
        scratch_shapes=scratch + [pltpu.SemaphoreType.DMA((sends,)), pltpu.SemaphoreType.DMA((arrivals,))],
        compiler_params=pltpu.CompilerParams(
            collective_id=number, has_side_effects=True, vmem_limit_bytes=vmem_mib << 20
        ),
        name=name,
    )


ANY = pl.BlockSpec(memory_space=pl.ANY)
IN_VMEM = pl.BlockSpec(memory_space=pltpu.VMEM)


def gains_of(line_ref, row):
    return jnp.concatenate([line_ref[s, row : row + 1, :] for s in range(line_ref.shape[0])], axis=1)


def column_grads_stream(copies, grad_ref, recv, sum_ref):
    chip, line, core, side, over, far = spots()
    sent = [
        copies.send(grad_ref.at[CORES * q[1] + q[2]], recv.at[core, line], q)
        for q in line_partners()
    ]
    local = copies.keep(grad_ref.at[CORES * line + core], recv.at[core, line])
    yield
    arrived(sent)
    local.wait()
    for number in range(CORES):
        total = recv[number, 0].astype(F32)
        for family in range(1, PLANE):
            total = total + recv[number, family].astype(F32)
        sum_ref[number] = total.astype(BF16)
    yield


def row_grads_stream(copies, grad_ref, mid, recv, summed, out_ref):
    chip, line, core, side, over, far = spots()
    width = out_ref.shape[1] // PLANE

    def quarter(q):
        return pl.ds(pl.multiple_of(q * width, width), width)

    sent = [copies.send(grad_ref.at[:, quarter(q[0])], mid.at[chip], q) for q in plane_partners()]
    local = copies.keep(grad_ref.at[:, quarter(chip)], mid.at[chip])
    yield
    local.wait()
    arrived(sent)
    sent = [copies.send(mid.at[q[1]], recv.at[line], q) for q in line_partners()[: PLANE - 1]]
    local = copies.keep(mid.at[line], recv.at[line])
    yield
    arrived(sent)
    local.wait()
    total = recv[0].astype(F32)
    for family in range(1, PLANE):
        total = total + recv[family].astype(F32)
    summed[...] = total.astype(BF16)
    sent = [copies.send(summed, out_ref.at[:, quarter(chip)], q) for q in plane_partners()]
    local = copies.keep(summed, out_ref.at[:, quarter(chip)])
    yield
    arrived(sent)
    local.wait()
    yield


def gain_grads_stream(copies, own, recv, summed, plane, out_ref):
    chip, line, core, side, over, far = spots()
    mine = CORES * line + core
    sent = [copies.send(own.at[CORES * q[1] + q[2]], recv.at[mine], q) for q in line_partners()]
    local = copies.keep(own.at[mine], recv.at[mine])
    yield
    arrived(sent)
    local.wait()
    summed[...] = jnp.sum(recv[...], axis=0)
    sent = [copies.send(summed, plane.at[chip], q) for q in plane_partners()]
    local = copies.keep(summed, plane.at[chip])
    yield
    arrived(sent)
    local.wait()
    out_ref[...] = jnp.sum(plane[...], axis=0)
    yield


def norm_back(grad, value, gain):
    unit, inverse = unit_rows(value)
    scaled = grad * gain
    back = inverse * (scaled - unit * jnp.mean(scaled * unit, axis=-1, keepdims=True))
    return back, jnp.sum(grad * unit, axis=0, keepdims=True)


TABLE_ROW = 2


def chunk_row(stored, part, chunk):
    plane, core, line = 2 * (stored % 2) + part, (stored // 2) % 2, stored // 4
    return ((plane * CORES + core) * PLANE + line) * chunk


def chosen(blocks, flags):
    value = blocks[0]
    for block, flag in zip(blocks[1:], flags[1:]):
        value = jnp.where(flag, block, value)
    return value


def in_place_order(table_ref, source, lanes, target, scale=None):
    chunk = BLK // 2
    blocks = source.shape[0] // BLK
    for place in range(blocks):
        flags = [table_ref[TABLE_ROW, stored] == float(place) for stored in range(blocks)]
        for part in range(2):
            rows = [chunk_row(stored, part, chunk) for stored in range(blocks)]
            block = chosen([source[row : row + chunk, lanes] for row in rows], flags)
            row = place * BLK + part * chunk
            target[row : row + chunk, :] = block if scale is None else block * scale


def in_gathered_order(table_ref, source, target, lanes):
    chunk = BLK // 2
    blocks = source.shape[0] // BLK
    for stored in range(blocks):
        flags = [table_ref[TABLE_ROW, stored] == float(place) for place in range(blocks)]
        for part in range(2):
            rows = [place * BLK + part * chunk for place in range(blocks)]
            block = chosen([source[row : row + chunk, :] for row in rows], flags)
            row = chunk_row(stored, part, chunk)
            target[row : row + chunk, lanes] = block


def attend_block(number, prompt, qs, ks, vt, att, ot_ref, lse_ref):
    start = number * CONT
    before = min(start, prompt)
    own_rows = slice(start, start + CONT)
    query = qs[own_rows, :]
    outs = []
    for head in range(2):
        masked = jnp.where(head_mask(CONT, head), query, jnp.zeros_like(query))
        own = dot_nt(ks[own_rows, :], masked)
        own = jnp.where(causal_mask(), own, -1e30)
        best = jnp.max(own, axis=0, keepdims=True)
        if before:
            past = dot_nt(ks[0:before, :], masked)
            best = jnp.maximum(best, jnp.max(past, axis=0, keepdims=True))
        terms = jnp.exp(own - best)
        total_terms = jnp.sum(terms, axis=0, keepdims=True)
        rows = slice(head * HEAD, (head + 1) * HEAD)
        out = matmul(vt[rows, own_rows], terms.astype(BF16))
        if before:
            terms = jnp.exp(past - best)
            total_terms = total_terms + jnp.sum(terms, axis=0, keepdims=True)
            out = out + matmul(vt[rows, 0:before], terms.astype(BF16))
        outs.append(out / total_terms)
        lse_ref[head : head + 1, own_rows] = best + jnp.log(total_terms)
    joined = jnp.concatenate(outs, axis=0)
    ot_ref[:, own_rows] = joined.astype(BF16)
    att[own_rows, :] = joined.T.astype(BF16)


def chip_slots(group):
    chip, line, core, side, over, far = spots()
    if group == "near":
        return 2 * CORES, lambda n: CORES * (side + lax.div(n, CORES) * (over - side)) + lax.rem(n, CORES)
    q = {"own": chip, "side": side, "over": over, "far": far}[group]
    return CORES, lambda n: CORES * q + n


def each_slot(group, body):
    count, slot_of = chip_slots(group)

    @pl.loop(0, count)
    def _(n):
        body(slot_of(n))


def front_kernel(
    tok_ref, cot_ref, small_ref, wq_ref, wk_ref, wv_ref, wo_ref, wg_ref, wu_ref, wd_ref,
    n1_out, x_out, cot_out, line_out, wqkv_out, wo_out, q_out, k_out, v_out, ot_out, lse_out, att_out,
    h1_out, dn2_out, mix_out, ggu_out, gd_out, table_out,
    *rest,
):
    scratch, other, rest = rest[:4], rest[4:8], rest[8:]
    x_ref, cotp_ref, line_ref, wqkv, wout, qs, ks, vs, ot_ref, lse_ref, att_ref, rest = *rest[:11], rest[11:]
    h1_ref, dn2_ref, ggu_ref, gd_ref, rest = *rest[:4], rest[4:]
    mid_x, mid_c, mid_o, down, tables, table, pieces, gate_w, up_w, gu, normed, rest = *rest[:11], rest[11:]
    n1s, n2s, cots, qkv, vt, att, parts, summed, wgu, wgu_t, wd, wd_t, us, dabs, *sems = rest
    copies = Copies(sems)
    chip, line, core, side, over, far = spots()
    total, heads = qkv.shape[0], wo_ref.shape[0]
    hidden, lanes = wd_ref.shape[0], wd.shape[0]
    chunk, width = x_ref.shape[1], x_ref.shape[2]
    rows = PLANE * chunk
    ranks = PLANE * CORES
    share = hidden // PLANE
    stores = []

    def store(source, target):
        stores.append(copies.keep(source, target))

    loads = [copies.keep(wg_ref, gate_w), copies.keep(wu_ref, up_w)]
    for c in range(CORES):
        column = pl.ds(pl.multiple_of((CORES * chip + c) * heads, heads), heads)
        for n, w in enumerate((wq_ref, wk_ref, wv_ref)):
            loads.append(copies.keep(w.at[:, column], pieces.at[c, :, n * heads : (n + 1) * heads]))
    copies.enter()
    tokens = inward_stream(copies, tok_ref, mid_x, x_ref)
    next(tokens)
    finished(loads)
    query_key = columns_relay(copies, pieces, wqkv, pl.ds(0, 2 * heads))
    mine = CORES * line + core
    small = [copies.send(small_ref, line_ref.at[mine], q) for q in line_partners()]
    small += [copies.send(small_ref, tables.at[chip], q) for q in plane_partners()]
    local = [copies.keep(small_ref, line_ref.at[mine]), copies.keep(small_ref, tables.at[chip])]
    query_key.hop(1)
    next(tokens)
    cotangents = inward_stream(copies, cot_ref, mid_c, cotp_ref)
    next(cotangents)
    query_key.hop(2)
    gu[...] = jnp.zeros_like(gu)
    for k in range(PLANE):
        @pl.when(chip == k)
        def _():
            for c in range(CORES):
                for z in range(PLANE):
                    begin, at = (CORES * z + c) * hidden + k * share, z * share
                    gu[c, :, at : at + share] = gate_w[:, begin : begin + share]
                    gu[c, :, lanes + at : lanes + at + share] = up_w[:, begin : begin + share]
    wd[hidden:lanes] = jnp.zeros((lanes - hidden, width), BF16)
    arrived(small)
    finished(local)
    load = [copies.keep(tables.at[line], table), copies.keep(tables.at[line], table_out)]
    store(line_ref, line_out)
    query_key.hop(3)
    gain = gains_of(line_ref, 0)
    next(tokens)
    value = columns_stream(copies, pieces, wqkv, pl.ds(2 * heads, heads))
    next(value)
    for n in range(PLANE):
        unit, ignored = unit_rows(x_ref[n].astype(F32))
        normed[n * chunk : (n + 1) * chunk] = (unit * gain).astype(BF16)
    gathering = copies.branch()
    gather = gather_stream(gathering, normed, n1s)
    next(gather)
    finished(load)
    next(gather)
    next(value)
    out_quarter = Relay(copies, lambda core: quarter_columns(wo_ref, chip), lambda z, core: mid_o.at[z], False)
    next(cotangents)

    def slot_rows(slot):
        return pl.ds(pl.multiple_of(slot * rows, rows), rows)

    def project(slot):
        qkv[slot_rows(slot), :] = matmul(n1s[slot], wqkv[...].reshape(width, 3 * heads)).astype(BF16)

    each_slot("own", project)
    next(gather)
    out_quarter.hop(1)
    next(gather)
    next(gather)
    out_quarter.hop(2)
    each_slot("near", project)
    next(gather)
    next(gather)
    each_slot("far", project)
    for source, target in ((n1s, n1_out), (x_ref, x_out), (wqkv, wqkv_out)):
        store(source, target)

    for n, ref in enumerate((qs, ks, vs)):
        scale = jnp.bfloat16(SCALE) if n == 0 else None
        in_place_order(table, qkv, slice(n * heads, (n + 1) * heads), ref, scale)
    out_quarter.hop(3)
    out_rows = to_ranks_stream(copies, mid_o, wout)
    next(out_rows)
    next(cotangents)
    gather_cot = gather_stream(copies, cotp_ref.reshape(rows, width), cots)
    next(gather_cot)
    gate_up = columns_relay(copies, gu, wgu, pl.ds(0, 2 * lanes))
    down_part = wd_ref.at[pl.ds(pl.multiple_of(chip * share, 8), share)]
    down_rows = Relay(copies, lambda core: down_part, lambda z, core: down.at[z], False)
    for start in range(0, total, CONT):
        part = slice(start, start + CONT)
        vt[:, part] = vs[part, :].astype(F32).T.astype(BF16)
    for source, target in ((qs, q_out), (ks, k_out), (vs, v_out), (cotp_ref, cot_out)):
        store(source, target)
    for number in range(total // CONT):
        attend_block(number, total // 2, qs, ks, vt, att, ot_ref, lse_ref)
        if number == 5:
            next(gather_cot)
            next(gather_cot)
            gate_up.hop(1)
    next(gather_cot)
    down_rows.hop(1)
    in_gathered_order(table, att, att_ref, slice(0, heads))
    next(out_rows)

    def spread(slot):
        parts[slot] = matmul(att_ref[slot_rows(slot), :], wout[...]).astype(BF16)

    scattering = copies.branch()
    scatter = Scatter(scattering, parts, summed, scratch)
    each_slot("far", spread)
    scatter.share(0)
    each_slot("near", spread)
    scatter.share(1, 2)
    each_slot("own", spread)
    scatter.share(3)
    scatter.far()
    scatter.side()
    scatter.over()
    next(gather_cot)
    next(gather_cot)
    gate_up.hop(2)
    down_rows.hop(2)
    for source, target in ((wout, wo_out), (ot_ref, ot_out), (lse_ref, lse_out), (att_ref, att_out)):
        store(source, target)
    scatter.cross()
    next(gather_cot)
    gate_up.hop(3)
    for s in range(ranks):
        wgu_t[:, s * heads : (s + 1) * heads] = wgu[s].T
    gathering.finish()
    gain = gains_of(line_ref, 1)
    scatter.end()
    for n in range(PLANE):
        part = slice(n * chunk, (n + 1) * chunk)
        hidden_rows = x_ref[n].astype(F32) + summed[part]
        h1_ref[part] = hidden_rows
        unit, ignored = unit_rows(hidden_rows)
        normed[part] = (unit * gain).astype(BF16)
    gather = gather_stream(copies, normed, n2s)
    next(gather)
    store(h1_ref, h1_out)
    down_rows.hop(3)
    for z in range(PLANE):
        wd[z * share : (z + 1) * share] = down[z]
    wd_t[...] = wd[...].T
    next(gather)
    scattering.finish()
    finished(stores)
    stores.clear()

    def feed(slot):
        block, cot = n2s[slot], cots[slot]
        both = matmul(block, wgu[...].reshape(width, 2 * lanes))
        gate, upper = both[:, :lanes], both[:, lanes:]
        bend = jnp.tanh(0.7978845608028654 * (gate + 0.044715 * gate * gate * gate))
        half = 0.5 * (1.0 + bend)
        active = gate * half
        slope = half + (0.5 * 0.7978845608028654) * gate * (1.0 - bend * bend) * (
            1.0 + 3 * 0.044715 * gate * gate
        )
        mixed = (active * upper).astype(BF16)
        us[slot] = mixed
        parts[slot] = matmul(mixed, wd[...]).astype(BF16)
        du = matmul(cot, wd_t[...])
        dabs[slot, :, 0:lanes] = (du * upper * slope).astype(BF16)
        dabs[slot, :, lanes:] = (du * active).astype(BF16)
        n1s[slot] = matmul(dabs[slot], wgu_t[...]).astype(BF16)

    scatter = Scatter(copies, n1s, dn2_ref, other)
    each_slot("own", feed)
    scatter.share(3)
    next(gather)
    next(gather)
    next(gather)
    each_slot("side", feed)
    scatter.share(1)
    next(gather)
    each_slot("over", feed)
    scatter.share(2)
    scatter.side()
    next(gather)
    each_slot("far", feed)
    scatter.share(0)
    scatter.over()
    scatter.far()
    store(parts, mix_out)

    def by_rows(s):
        columns = pl.ds(pl.multiple_of(s * heads, heads), heads)
        grad = jnp.zeros((heads, 2 * lanes), F32)
        for slot in range(ranks):
            grad = grad + inner(n2s[slot, :, columns], dabs[slot])
        ggu_ref[s] = grad.astype(BF16)

    pl.loop(0, ranks // 2)(by_rows)
    scatter.cross()
    pl.loop(ranks // 2, ranks)(by_rows)
    store(ggu_ref, ggu_out)
    grad = jnp.zeros((lanes, width), F32)
    for slot in range(ranks):
        grad = grad + inner(us[slot], cots[slot])
    for z in range(PLANE):
        for h in range(2):
            block = grad[z * share : (z + 1) * share, h * (width // 2) : (h + 1) * (width // 2)]
            gd_ref[z, h] = block.astype(BF16)
    store(gd_ref, gd_out)
    scatter.end()
    store(dn2_ref, dn2_out)
    for relay in (query_key, out_quarter, gate_up, down_rows):
        relay.finish()
    copies.finish()
    finished(stores)


def front(tokens, cotangent, small, w_query, w_key, w_value, w_out, w_gate, w_up, w_down):
    rows, width = tokens.shape
    heads, hidden = w_out.shape[0], w_down.shape[0]
    lanes = -(-hidden // 128) * 128
    ranks = PLANE * CORES
    total = ranks * rows
    chunks, blocks = (PLANE, rows // PLANE, width), (ranks, rows, width)
    low = lambda *shape: jax.ShapeDtypeStruct(shape, BF16)
    wide = lambda *shape: jax.ShapeDtypeStruct(shape, F32)
    held = [
        low(*chunks), low(*chunks), wide(ranks, *small.shape), low(ranks, heads, 3 * heads),
        low(heads, width), low(total, heads), low(total, heads), low(total, heads), low(heads, total),
        wide(2, total), low(total, heads), wide(rows, width), wide(rows, width),
    ]
    grads = [low(ranks, heads, 2 * lanes), low(PLANE, 2, hidden // PLANE, width // 2)]
    shapes = [low(*blocks)] + held + [low(*blocks)] + grads + [wide(*small.shape)]
    scratch = scatter_scratch(rows, width) * 2
    scratch += [pltpu.VMEM(a.shape, a.dtype) for a in held + grads]
    held = lambda *shape: pltpu.VMEM(shape, BF16)
    scratch += [held(*chunks), held(*chunks), held(PLANE, heads, width // PLANE), held(PLANE, hidden // PLANE, width)]
    scratch += [pltpu.VMEM((PLANE,) + small.shape, F32), pltpu.SMEM(small.shape, F32)]
    scratch += [held(CORES, heads, 3 * heads), held(*w_gate.shape), held(*w_up.shape), held(CORES, heads, 2 * lanes)]
    scratch += [held(rows, width), held(*blocks), held(*blocks), held(*blocks), held(total, 3 * heads)]
    scratch += [held(heads, total), held(total, heads), held(*blocks), pltpu.VMEM((rows, width), F32)]
    scratch += [held(ranks, heads, 2 * lanes), held(2 * lanes, width), held(lanes, width), held(width, lanes)]
    scratch += [held(ranks, rows, lanes), held(ranks, rows, 2 * lanes)]
    return comm_call(
        front_kernel, "front", 1, tuple(shapes), [ANY] * 10, (ANY,) * len(shapes), scratch, 194, 138,
    )(tokens, cotangent, small, w_query, w_key, w_value, w_out, w_gate, w_up, w_down)


def attend_back_block(number, prompt, qs, ks, vs, gs, kt, ot_ref, lse_ref, dqs, dks, dvs):
    start = number * CONT
    own = slice(start, start + CONT)
    query, grad = qs[own, :], gs[own, :]
    product = grad.astype(F32).T * ot_ref[:, own].astype(F32)
    outs = []
    for head in range(2):
        rows = slice(head * HEAD, (head + 1) * HEAD)
        delta = jnp.sum(product[rows], axis=0, keepdims=True)
        lse = lse_ref[head : head + 1, own]
        keep = head_mask(CONT, head)
        query_head = jnp.where(keep, query, jnp.zeros_like(query))
        grad_head = jnp.where(keep, grad, jnp.zeros_like(grad))
        dq = None
        for keys in [own] + ([slice(0, min(start, prompt))] if start else []):
            prob = jnp.exp(dot_nt(ks[keys, :], query_head) - lse)
            if keys == own:
                prob = jnp.where(causal_mask(), prob, 0.0)
            dprob = dot_nt(vs[keys, :], grad_head)
            dscore = (prob * (dprob - delta)).astype(BF16)
            dvs[keys, :] += matmul(prob.astype(BF16), grad_head)
            dks[keys, :] += matmul(dscore, query_head)
            term = matmul(kt[rows, keys], dscore)
            dq = term if dq is None else dq + term
        outs.append(dq)
    dqs[own, :] = (jnp.concatenate(outs, axis=0) * SCALE).T.astype(BF16)


def rear_kernel(
    table, summed_in, h1_in, cot_in, x_in, line_in, n1_in, mix_in, wqkv_in, wo_in,
    q_in, k_in, v_in, ot_in, lse_in, att_in, gu_ref, down_ref,
    out_ref, grad_ref, gains_ref, gate_end, up_end, q_end, k_end, v_end, wo_all, wd_end,
    *rest,
):
    scratch, other, rest = rest[:4], rest[4:8], rest[8:]
    summed_ref, h1_ref, cot_ref, x_ref, line_ref, wqkv_ref, wo_ref, rest = *rest[:7], rest[7:]
    qs, ks, vs, ot_ref, lse_ref, att_ref, rest = *rest[:6], rest[6:]
    gate_out, up_out, q_out, k_out, v_out, wd_out, rest = *rest[:6], rest[6:]
    n1s, parts, gas, datt, gs, kt, dqs, dks, dvs, dqkv, w_t, rest = *rest[:11], rest[11:]
    dh1, summed, mixed, low, low_tok, low_out, rest = *rest[:6], rest[6:]
    recv_gu, sum_gu, gu_all, gqkv, recv_qkv, sum_qkv, qkv_all, gwo, rest = *rest[:8], rest[8:]
    mid_wo, recv_wo, sum_wo, recv_wd, sum_wd, down_all, own, recv_gain, sum_gain, plane, *sems = rest
    copies = Copies(sems)
    total, heads = att_ref.shape
    ranks = PLANE * CORES
    chunk, width = x_ref.shape[1], x_ref.shape[2]
    rows = PLANE * chunk
    share = down_ref.shape[2]
    hidden = PLANE * share
    lanes = gu_ref.shape[2] // 2

    def load(*pairs):
        return [copies.keep(source, target) for source, target in pairs]

    first = load((summed_in, summed_ref), (h1_in, h1_ref), (cot_in, cot_ref), (line_in, line_ref))
    second_load = load((k_in, ks), (wqkv_in, wqkv_ref), (wo_in, wo_ref))
    third = load((mix_in, parts))
    fourth = load((q_in, qs), (v_in, vs), (ot_in, ot_ref), (lse_in, lse_ref), (x_in, x_ref))
    fifth = load((n1_in, n1s), (att_in, att_ref))
    stores = []
    copies.enter(crossing=True)
    finished(first)
    gain = gains_of(line_ref, 1)
    gain2_sum = jnp.zeros((1, width), F32)
    for n in range(PLANE):
        part = slice(n * chunk, (n + 1) * chunk)
        back, by_gain = norm_back(summed_ref[part], h1_ref[part], gain)
        grad = cot_ref[n].astype(F32) + back
        gain2_sum = gain2_sum + by_gain
        dh1[part] = grad
        low[part] = grad.astype(BF16)
    gather = gather_stream(copies, low, gas)
    next(gather)
    gate_up = column_grads_stream(copies, gu_ref, recv_gu, sum_gu)
    next(gate_up)
    finished(second_load)
    for start in range(0, total, CONT):
        part = slice(start, start + CONT)
        kt[:, part] = ks[part, :].astype(F32).T.astype(BF16)
    for s in range(ranks):
        w_t[:, s * heads : (s + 1) * heads] = wqkv_ref[s].T
    dks[...] = jnp.zeros_like(dks)
    dvs[...] = jnp.zeros_like(dvs)

    def slot_rows(slot):
        return pl.ds(pl.multiple_of(slot * rows, rows), rows)

    def attended_grad(slot):
        datt[slot_rows(slot), :] = outer(gas[slot], wo_ref[...]).astype(BF16)

    next(gather)
    each_slot("own", attended_grad)
    next(gather)
    finished(third)
    next(gather)
    next(gather)
    each_slot("near", attended_grad)
    next(gather)
    mixing = copies.branch()
    second = Scatter(mixing, parts, mixed, other)
    second.share(0, 1, 2, 3)
    second.far()
    second.side()
    second.over()
    next(gather)
    each_slot("far", attended_grad)
    in_place_order(table, datt, slice(0, heads), gs)
    finished(fourth)
    finished(fifth)
    for number in range(total // CONT):
        attend_back_block(number, total // 2, qs, ks, vs, gs, kt, ot_ref, lse_ref, dqs, dks, dvs)
        if number == 3:
            second.cross()
        if number == 6:
            next(gate_up)
            gather_gu = gather_stream(copies, sum_gu, gu_all, twin=False)
            next(gather_gu)
            down = sum_stream(copies, down_ref, recv_wd, sum_wd)
            next(down)
    second.end()
    for n in range(PLANE):
        part = slice(n * chunk, (n + 1) * chunk)
        low_out[n] = (h1_ref[part] + mixed[part]).astype(BF16)
    output = Outward(copies, low_out, out_ref)
    ks_low, vs_low = gs, datt
    for start in range(0, total, CONT):
        part = slice(start, start + CONT)
        ks_low[part, :] = dks[part, :].astype(BF16)
        vs_low[part, :] = dvs[part, :].astype(BF16)
    for n, ref in enumerate((dqs, ks_low, vs_low)):
        in_gathered_order(table, ref, dqkv, slice(n * heads, (n + 1) * heads))
    mixing.finish()
    next(gather_gu)
    next(gather_gu)

    def spread(slot):
        parts[slot] = matmul(dqkv[slot_rows(slot), :], w_t[...]).astype(BF16)

    scatter = Scatter(copies, parts, summed, scratch)
    each_slot("far", spread)
    scatter.share(0)
    each_slot("near", spread)
    scatter.share(1, 2)
    each_slot("own", spread)
    scatter.share(3)
    scatter.far()
    scatter.side()
    scatter.over()

    def by_rows(s):
        columns = pl.ds(pl.multiple_of(s * heads, heads), heads)
        grad = jnp.zeros((heads, 3 * heads), F32)
        for slot in range(ranks):
            grad = grad + inner(n1s[slot, :, columns], dqkv[slot * rows : (slot + 1) * rows, :])
        gqkv[s] = grad.astype(BF16)

    pl.loop(0, ranks)(by_rows)
    qkv = column_grads_stream(copies, gqkv, recv_qkv, sum_qkv)
    next(qkv)
    grad = jnp.zeros((heads, width), F32)
    for slot in range(ranks):
        grad = grad + inner(att_ref[slot * rows : (slot + 1) * rows, :], gas[slot])
    gwo[...] = grad.astype(BF16)
    out_w = row_grads_stream(copies, gwo, mid_wo, recv_wo, sum_wo, wo_all)
    next(out_w)
    for ignored in gather_gu:
        pass
    scatter.cross()
    next(out_w)
    next(down)
    gather_down = gather_stream(copies, sum_wd, down_all, twin=False)
    next(gather_down)

    def format_gate(chip, c, z):
        begin, at = (CORES * z + c) * hidden + chip * share, z * share
        gate_out[:, begin : begin + share] = gu_all[chip, c, :, at : at + share]
        up_out[:, begin : begin + share] = gu_all[chip, c, :, lanes + at : lanes + at + share]

    places = [(chip, c, z) for chip in range(PLANE) for c in range(CORES) for z in range(PLANE)]
    for place in places[: len(places) // 2]:
        format_gate(*place)
    scatter.end()
    gain = gains_of(line_ref, 0)
    gain1_sum = jnp.zeros((1, width), F32)
    for n in range(PLANE):
        part = slice(n * chunk, (n + 1) * chunk)
        back, by_gain = norm_back(summed[part], x_ref[n].astype(F32), gain)
        gain1_sum = gain1_sum + by_gain
        low_tok[n] = (dh1[part] + back).astype(BF16)
    tokens = Outward(copies, low_tok, grad_ref)
    own[...] = jnp.zeros_like(own)
    for s in range(ranks):
        part = slice(s * heads, (s + 1) * heads)
        own[s, 0:1] = gain1_sum[:, part]
        own[s, 1:2] = gain2_sum[:, part]
    gains = gain_grads_stream(copies, own, recv_gain, sum_gain, plane, gains_ref)
    next(gains)
    next(gather_down)
    next(gather_down)
    next(out_w)
    for place in places[len(places) // 2 :]:
        format_gate(*place)
    stores += load((gate_out, gate_end), (up_out, up_end))
    for ignored in gather_down:
        pass
    for chip in range(PLANE):
        for h in range(2):
            wd_out[chip * share : (chip + 1) * share, h * (width // 2) : (h + 1) * (width // 2)] = down_all[chip, h]
    stores += load((wd_out, wd_end))
    next(qkv)
    gather_qkv = gather_stream(copies, sum_qkv, qkv_all, twin=False)
    next(gather_qkv)
    next(gains)
    next(gather_qkv)
    next(gather_qkv)
    next(gains)
    next(out_w)
    for ignored in gather_qkv:
        pass
    for chip in range(PLANE):
        for c in range(CORES):
            begin = (CORES * chip + c) * heads
            for n, ref in enumerate((q_out, k_out, v_out)):
                ref[:, begin : begin + heads] = qkv_all[chip, c, :, n * heads : (n + 1) * heads]
    stores += load((q_out, q_end), (k_out, k_end), (v_out, v_end))
    output.wait()
    tokens.wait()
    copies.finish()
    finished(stores)


def rear(table, summed, h1, cot, x, lines, n1, mixed, w_qkv, w_o, qs, ks, vs, ot, lse, att, gate_up_grad, down_grad, ff):
    ranks = PLANE * CORES
    rows, width = h1.shape
    total, heads = att.shape
    hidden = PLANE * down_grad.shape[2]
    quarter = width // PLANE
    small = lines.shape[1:]
    low = lambda *shape: jax.ShapeDtypeStruct(shape, BF16)
    shapes = (
        low(rows, width), low(rows, width), jax.ShapeDtypeStruct(small, F32),
        low(heads, ff), low(heads, ff), low(heads, width), low(heads, width), low(heads, width),
        low(heads, width), low(hidden, width),
    )
    held = lambda *shape: pltpu.VMEM(shape, BF16)
    wide = lambda *shape: pltpu.VMEM(shape, F32)
    scratch = scatter_scratch(rows, width) * 2
    scratch += [pltpu.VMEM(a.shape, a.dtype) for a in (summed, h1, cot, x, lines, w_qkv, w_o, qs, ks, vs, ot, lse, att)]
    scratch += [held(*shapes[n].shape) for n in (3, 4, 5, 6, 7, 9)]
    scratch += [held(*n1.shape)] * 3 + [held(total, heads)] * 2 + [held(heads, total), held(total, heads)]
    scratch += [wide(total, heads)] * 2 + [held(total, 3 * heads), held(3 * heads, width)]
    scratch += [wide(rows, width)] * 3 + [held(rows, width)] + [held(*x.shape)] * 2
    for grad in (gate_up_grad, w_qkv):
        piece = (CORES,) + grad.shape[1:]
        if grad is w_qkv:
            scratch += [held(*grad.shape)]
        scratch += [held(CORES, PLANE, *grad.shape[1:]), held(*piece), held(PLANE, *piece)]
    scratch += [held(heads, width)]
    scratch += [held(PLANE, heads, quarter)] * 2 + [held(heads, quarter)]
    scratch += [held(*down_grad.shape), held(*down_grad.shape[1:]), held(*down_grad.shape)]
    scratch += [wide(*lines.shape)] * 2 + [wide(*small), wide(PLANE, *small)]
    return comm_call(
        rear_kernel, "rear", 2, shapes,
        [pl.BlockSpec(memory_space=pltpu.SMEM)] + [ANY] * 17,
        (ANY, ANY, IN_VMEM) + (ANY,) * 7,
        scratch, 139, 104,
    )(table, summed, h1, cot, x, lines, n1, mixed, w_qkv, w_o, qs, ks, vs, ot, lse, att, gate_up_grad, down_grad)


def finish_kernel(*refs):
    count = (len(refs) - 1) // 4
    inputs, outputs, held, stage = (refs[n * count : (n + 1) * count] for n in range(4))
    sems = refs[-1]
    loads, stores = [], []
    for n, (source, buffer) in enumerate(zip(inputs, held)):
        loads.append(pltpu.make_async_copy(source, buffer, sems.at[0, n]))
        loads[-1].start()
    for n, (target, buffer, wide) in enumerate(zip(outputs, held, stage)):
        loads[n].wait()
        if buffer.dtype != target.dtype:
            wide[...] = buffer[...].astype(F32)
            buffer = wide
        stores.append(pltpu.make_async_copy(buffer, target, sems.at[1, n]))
        stores[-1].start()
    for copy in stores:
        copy.wait()


def finish(tokens, grads):
    inputs = list(tokens) + list(grads)
    shapes = [jax.ShapeDtypeStruct(a.shape, a.dtype) for a in tokens]
    shapes += [jax.ShapeDtypeStruct(a.shape, F32) for a in grads]
    small = pltpu.VMEM((8, 128), F32)
    held = [pltpu.VMEM(a.shape, a.dtype) for a in inputs]
    stage = [small] * len(tokens) + [pltpu.VMEM(a.shape, F32) for a in grads]
    return pl.pallas_call(
        finish_kernel,
        out_shape=tuple(shapes),
        in_specs=[ANY] * len(inputs),
        out_specs=(ANY,) * len(inputs),
        scratch_shapes=held + stage + [pltpu.SemaphoreType.DMA((2, len(inputs)))],
        compiler_params=pltpu.CompilerParams(vmem_limit_bytes=60 << 20),
        name="finish",
    )(*inputs)


def plane_local(
    tokens,
    cotangent,
    block_table,
    norm1_gain,
    w_query,
    w_key,
    w_value,
    w_out,
    norm2_gain,
    w_gate,
    w_up,
    w_down,
):
    rows, width = tokens.shape[1:]
    heads = width // (PLANE * CORES)
    table = jnp.pad(block_table.astype(F32), ((0, 0), (0, heads - block_table.shape[1])))
    small = jnp.concatenate([norm1_gain[None].astype(F32), norm2_gain[None].astype(F32), table])
    small = jnp.pad(small, ((0, 8 - small.shape[0]), (0, 0)))
    (
        n1, x, cot, gains, w_qkv, w_o, qs, ks, vs, ot, lse, att, h1, dn2, mixed, g_gu, g_down, table
    ) = front(tokens[0], cotangent[0], small, w_query, w_key, w_value, w_out, w_gate, w_up, w_down)
    output, tokens_grad, gain_grads, *grads = rear(
        table, dn2, h1, cot, x, gains, n1, mixed, w_qkv, w_o, qs, ks, vs, ot, lse, att, g_gu, g_down,
        w_gate.shape[1],
    )
    output, tokens_grad, gate, up, query, key, value, out, down = finish((output, tokens_grad), grads)
    return (
        output[None], tokens_grad[None],
        gain_grads[0], query, key, value, out, gain_grads[1], gate, up, down,
    )


def plane_solution(mesh):
    split = Mesh(mesh.devices.reshape(PLANE, PLANE, CORES), ("group", "z", "core"))
    ctx = ("z", "core")
    token, weight = P("group", ctx, None), P(ctx, None)
    in_specs = (token, token, P("group", None), P(ctx)) + (weight,) * 4 + (P(ctx),) + (weight,) * 3
    out_specs = (token, token, P(ctx)) + (weight,) * 4 + (P(ctx),) + (weight,) * 3
    return jax.shard_map(
        plane_local, mesh=split, in_specs=in_specs, out_specs=out_specs, check_vma=False
    )


def family_solution(mesh):
    in_specs = (
        P("group", "ctx", None),
        P("group", "ctx", None),
        P("group", None),
        P("ctx"),
        P("ctx", None),
        P("ctx", None),
        P("ctx", None),
        P("ctx", None),
        P("ctx"),
        P("ctx", None),
        P("ctx", None),
        P("ctx", None),
    )
    out_specs = (
        P("group", "ctx", None),
        P("group", "ctx", None),
        P("ctx"),
        P("ctx", None),
        P("ctx", None),
        P("ctx", None),
        P("ctx", None),
        P("ctx"),
        P("ctx", None),
        P("ctx", None),
        P("ctx", None),
    )
    return jax.shard_map(local, mesh=mesh, in_specs=in_specs, out_specs=out_specs, check_vma=False)


def solution(mesh):
    groups, ranks = mesh.shape["group"], mesh.shape["ctx"]
    if groups == PLANE and ranks == 2 * PLANE:
        return plane_solution(mesh)
    return family_solution(mesh)
```

```python
import jax
import jax.numpy as jnp
from jax import lax
from jax.experimental import pallas as pl
from jax.experimental.pallas import tpu as pltpu
from jax.sharding import Mesh
from jax.sharding import PartitionSpec as P

HEADS = 16
HEAD = 64
BLK = 128
KEYBLK = 512
PROMPT_MAX = 2048
CONT = 256


EPS = 1e-06
SCALE = 0.125


def rms_scale(hidden, gain):
    return hidden * lax.rsqrt(jnp.mean(hidden * hidden, axis=-1, keepdims=True) + EPS) * gain


def gated(gate, upper):
    return jax.nn.gelu(gate, approximate=True) * upper


def matmul(left, right):
    return jnp.dot(left, right, preferred_element_type=jnp.float32)


def inner(left, right):
    return lax.dot_general(
        left, right, (((0,), (0,)), ((), ())), preferred_element_type=jnp.float32
    )


def outer(left, right):
    return lax.dot_general(
        left, right, (((1,), (1,)), ((), ())), preferred_element_type=jnp.float32
    )


def family_index(table):
    offsets = jnp.arange(BLK, dtype=jnp.int32)
    return (table[:, None] * BLK + offsets[None, :]).reshape(-1)


def segment_of(index, prompt_len):
    return jnp.where(index < prompt_len, 0, 1 + (index - prompt_len) // CONT)


def allowed(query_index, key_index, prompt_len):
    query_seg = segment_of(query_index, prompt_len)
    key_seg = segment_of(key_index, prompt_len)
    same = (query_seg[:, None] == key_seg[None, :]) & (key_index[None, :] <= query_index[:, None])
    prompt = (key_seg[None, :] == 0) & (query_seg[:, None] > 0)
    return same | prompt


def head_split(block):
    return block.reshape(block.shape[0], HEADS, HEAD)


def scores_of(query_heads, key_block, query_index, key_index, prompt_len):
    score = (
        jnp.einsum(
            "qhd,khd->hqk", query_heads, head_split(key_block), preferred_element_type=jnp.float32
        )
        * SCALE
    )
    return (score, allowed(query_index, key_index, prompt_len))


def attend_stats(queries, keys, query_index, key_index, prompt_len):
    query_heads = head_split(queries)

    def step(carry, number):
        best, total = carry
        start = number * KEYBLK
        key_block = lax.dynamic_slice_in_dim(keys, start, KEYBLK, 0)
        block_index = lax.dynamic_slice_in_dim(key_index, start, KEYBLK, 0)
        score, keep = scores_of(query_heads, key_block, query_index, block_index, prompt_len)
        score = jnp.where(keep[None], score, -1e30)
        larger = jnp.maximum(best, jnp.max(score, axis=-1))
        terms = jnp.where(keep[None], jnp.exp(score - larger[:, :, None]), 0.0)
        total = total * jnp.exp(best - larger) + jnp.sum(terms, axis=-1)
        return ((larger, total), None)

    start_best = jnp.full((HEADS, queries.shape[0]), -1e30, jnp.float32)
    (best, total), ignored = lax.scan(
        step, (start_best, jnp.zeros_like(start_best)), jnp.arange(keys.shape[0] // KEYBLK)
    )
    return best + jnp.log(total)


def attend_values(queries, keys, values, lse, query_index, key_index, prompt_len):
    query_heads = head_split(queries)

    def step(acc, number):
        start = number * KEYBLK
        key_block = lax.dynamic_slice_in_dim(keys, start, KEYBLK, 0)
        value_block = lax.dynamic_slice_in_dim(values, start, KEYBLK, 0)
        block_index = lax.dynamic_slice_in_dim(key_index, start, KEYBLK, 0)
        score, keep = scores_of(query_heads, key_block, query_index, block_index, prompt_len)
        prob = jnp.where(keep[None], jnp.exp(score - lse[:, :, None]), 0.0).astype(jnp.bfloat16)
        return (
            acc
            + jnp.einsum(
                "hqk,khd->qhd", prob, head_split(value_block), preferred_element_type=jnp.float32
            ),
            None,
        )

    start_acc = jnp.zeros((queries.shape[0], HEADS, HEAD), jnp.float32)
    acc, ignored = lax.scan(step, start_acc, jnp.arange(keys.shape[0] // KEYBLK))
    return acc.reshape(queries.shape[0], HEADS * HEAD)


def block_grads(query_heads, grad_heads, key_block, value_block, lse, delta, keep):
    key_heads = head_split(key_block)
    value_heads = head_split(value_block)
    score = (
        jnp.einsum("qhd,khd->hqk", query_heads, key_heads, preferred_element_type=jnp.float32)
        * SCALE
    )
    prob = jnp.where(keep[None], jnp.exp(score - lse[:, :, None]), 0.0)
    dvalue = jnp.einsum(
        "hqk,qhd->khd", prob.astype(jnp.bfloat16), grad_heads, preferred_element_type=jnp.float32
    )
    dprob = jnp.einsum("qhd,khd->hqk", grad_heads, value_heads, preferred_element_type=jnp.float32)
    dscore = (prob * (dprob - delta[:, :, None])).astype(jnp.bfloat16)
    dquery = (
        jnp.einsum("hqk,khd->qhd", dscore, key_heads, preferred_element_type=jnp.float32) * SCALE
    )
    dkey = (
        jnp.einsum("hqk,qhd->khd", dscore, query_heads, preferred_element_type=jnp.float32) * SCALE
    )
    return (dquery, dkey, dvalue)


def local(
    tokens,
    cotangent,
    block_table,
    norm1_gain,
    w_query,
    w_key,
    w_value,
    w_out,
    norm2_gain,
    w_gate,
    w_up,
    w_down,
):
    row_count = tokens.shape[1]
    width = tokens.shape[2]
    every_index = family_index(block_table[0])
    prompt_len = min(PROMPT_MAX, every_index.shape[0] // 2)
    own_index = lax.dynamic_slice_in_dim(
        every_index, lax.axis_index("ctx") * row_count, row_count, 0
    )
    gain1, wq_full, wk_full, wv_full, wo_full = (
        lax.all_gather(norm1_gain, "ctx", axis=0, tiled=True),
        lax.all_gather(w_query, "ctx", axis=0, tiled=True),
        lax.all_gather(w_key, "ctx", axis=0, tiled=True),
        lax.all_gather(w_value, "ctx", axis=0, tiled=True),
        lax.all_gather(w_out, "ctx", axis=0, tiled=True),
    )
    inputs = tokens[0].astype(jnp.float32)
    normed1, norm1_pull = jax.vjp(rms_scale, inputs, gain1.astype(jnp.float32))
    first_low = normed1.astype(jnp.bfloat16)
    queries = matmul(first_low, wq_full).astype(jnp.bfloat16)
    keys_own = matmul(first_low, wk_full).astype(jnp.bfloat16)
    values_own = matmul(first_low, wv_full).astype(jnp.bfloat16)
    keys_all, values_all = (
        lax.all_gather(keys_own, "ctx", axis=0, tiled=True),
        lax.all_gather(values_own, "ctx", axis=0, tiled=True),
    )
    lse = attend_stats(queries, keys_all, own_index, every_index, prompt_len)
    attended_wide = attend_values(
        queries, keys_all, values_all, lse, own_index, every_index, prompt_len
    )
    attended = attended_wide.astype(jnp.bfloat16)
    hidden = inputs + matmul(attended, wo_full)
    gain2, wg_full, wu_full, wd_full = (
        lax.all_gather(norm2_gain, "ctx", axis=0, tiled=True),
        lax.all_gather(w_gate, "ctx", axis=0, tiled=True),
        lax.all_gather(w_up, "ctx", axis=0, tiled=True),
        lax.all_gather(w_down, "ctx", axis=0, tiled=True),
    )
    normed2, norm2_pull = jax.vjp(rms_scale, hidden, gain2.astype(jnp.float32))
    second_low = normed2.astype(jnp.bfloat16)
    gate = matmul(second_low, wg_full)
    upper = matmul(second_low, wu_full)
    mixed_wide, gate_pull = jax.vjp(gated, gate, upper)
    mixed = mixed_wide.astype(jnp.bfloat16)
    result = hidden + matmul(mixed, wd_full)
    output = result.astype(jnp.bfloat16)[None]
    grad_low = cotangent[0]
    grad_down = inner(mixed, grad_low)
    dmixed = outer(grad_low, wd_full)
    dgate, dupper = gate_pull(dmixed)
    dgate_low = dgate.astype(jnp.bfloat16)
    dupper_low = dupper.astype(jnp.bfloat16)
    grad_gate = inner(second_low, dgate_low)
    grad_up = inner(second_low, dupper_low)
    dnormed2 = outer(dgate_low, wg_full) + outer(dupper_low, wu_full)
    dhidden_norm, grad_gain2 = norm2_pull(dnormed2)
    dhidden = grad_low.astype(jnp.float32) + dhidden_norm
    attn_low = dhidden.astype(jnp.bfloat16)
    grad_out_w = inner(attended, attn_low)
    dattended = outer(attn_low, wo_full).astype(jnp.bfloat16)
    delta = jnp.sum(
        (dattended.astype(jnp.float32) * attended_wide).reshape(row_count, HEADS, HEAD), axis=-1
    ).T
    query_heads = head_split(queries)
    grad_heads = head_split(dattended)

    def key_step(carry, number):
        start = number * KEYBLK
        key_block = lax.dynamic_slice_in_dim(keys_all, start, KEYBLK, 0)
        value_block = lax.dynamic_slice_in_dim(values_all, start, KEYBLK, 0)
        block_index = lax.dynamic_slice_in_dim(every_index, start, KEYBLK, 0)
        keep = allowed(own_index, block_index, prompt_len)
        dquery, dkey, dvalue = block_grads(
            query_heads, grad_heads, key_block, value_block, lse, delta, keep
        )
        joined = jnp.concatenate(
            [dkey.reshape(KEYBLK, width), dvalue.reshape(KEYBLK, width)], axis=1
        )
        return (carry + dquery, joined)

    start_query = jnp.zeros((row_count, HEADS, HEAD), jnp.float32)
    query_sum, key_terms = lax.scan(
        key_step, start_query, jnp.arange(every_index.shape[0] // KEYBLK)
    )
    summed = lax.psum_scatter(
        key_terms.reshape(every_index.shape[0], 2 * width).astype(jnp.bfloat16),
        "ctx",
        scatter_dimension=0,
        tiled=True,
    ).astype(jnp.float32)
    query_grad = query_sum.reshape(row_count, width)
    key_grad = summed[:, :width]
    value_grad = summed[:, width:]
    query_low = query_grad.astype(jnp.bfloat16)
    key_low = key_grad.astype(jnp.bfloat16)
    value_low = value_grad.astype(jnp.bfloat16)
    grad_query = inner(first_low, query_low)
    grad_key = inner(first_low, key_low)
    grad_value = inner(first_low, value_low)
    dnormed1 = outer(query_low, wq_full) + outer(key_low, wk_full) + outer(value_low, wv_full)
    dinput_norm, grad_gain1 = norm1_pull(dnormed1)
    tokens_grad = (dhidden + dinput_norm).astype(jnp.bfloat16)[None]
    shards = (
        lax.psum_scatter(
            grad_gain1.astype(jnp.bfloat16), "ctx", scatter_dimension=0, tiled=True
        ).astype(jnp.float32),
        lax.psum_scatter(
            grad_query.astype(jnp.bfloat16), "ctx", scatter_dimension=0, tiled=True
        ).astype(jnp.float32),
        lax.psum_scatter(
            grad_key.astype(jnp.bfloat16), "ctx", scatter_dimension=0, tiled=True
        ).astype(jnp.float32),
        lax.psum_scatter(
            grad_value.astype(jnp.bfloat16), "ctx", scatter_dimension=0, tiled=True
        ).astype(jnp.float32),
        lax.psum_scatter(
            grad_out_w.astype(jnp.bfloat16), "ctx", scatter_dimension=0, tiled=True
        ).astype(jnp.float32),
        lax.psum_scatter(
            grad_gain2.astype(jnp.bfloat16), "ctx", scatter_dimension=0, tiled=True
        ).astype(jnp.float32),
        lax.psum_scatter(
            grad_gate.astype(jnp.bfloat16), "ctx", scatter_dimension=0, tiled=True
        ).astype(jnp.float32),
        lax.psum_scatter(
            grad_up.astype(jnp.bfloat16), "ctx", scatter_dimension=0, tiled=True
        ).astype(jnp.float32),
        lax.psum_scatter(
            grad_down.astype(jnp.bfloat16), "ctx", scatter_dimension=0, tiled=True
        ).astype(jnp.float32),
    )
    shards = (
        lax.psum(shards[0].astype(jnp.bfloat16), "group").astype(jnp.float32),
        lax.psum(shards[1].astype(jnp.bfloat16), "group").astype(jnp.float32),
        lax.psum(shards[2].astype(jnp.bfloat16), "group").astype(jnp.float32),
        lax.psum(shards[3].astype(jnp.bfloat16), "group").astype(jnp.float32),
        lax.psum(shards[4].astype(jnp.bfloat16), "group").astype(jnp.float32),
        lax.psum(shards[5].astype(jnp.bfloat16), "group").astype(jnp.float32),
        lax.psum(shards[6].astype(jnp.bfloat16), "group").astype(jnp.float32),
        lax.psum(shards[7].astype(jnp.bfloat16), "group").astype(jnp.float32),
        lax.psum(shards[8].astype(jnp.bfloat16), "group").astype(jnp.float32),
    )
    return (
        output,
        tokens_grad,
        shards[0],
        shards[1],
        shards[2],
        shards[3],
        shards[4],
        shards[5],
        shards[6],
        shards[7],
        shards[8],
    )


PLANE = 4
CORES = 2
TP = ("group", "core")
F32 = jnp.float32
BF16 = jnp.bfloat16


def dot_nt(left, right):
    return lax.dot_general(left, right, (((1,), (1,)), ((), ())), preferred_element_type=F32)


def head_mask(rows, head):
    lane = lax.broadcasted_iota(jnp.int32, (rows, 2 * HEAD), 1)
    return (lane >= head * HEAD) & (lane < (head + 1) * HEAD)


def causal_mask():
    key = lax.broadcasted_iota(jnp.int32, (CONT, CONT), 0)
    query = lax.broadcasted_iota(jnp.int32, (CONT, CONT), 1)
    return key <= query


MESH = pl.DeviceIdType.MESH
EARLY = 256
FRONT_SEMS = (126, 137)
REAR_SEMS = (114, 104)


def spots():
    chip, line, core = lax.axis_index("group"), lax.axis_index("z"), lax.axis_index("core")
    side = chip + 1 - 2 * lax.rem(chip, 2)
    over = lax.rem(chip + 2, PLANE)
    far = PLANE - 1 - chip
    return chip, line, core, side, over, far


def plane_partners():
    chip, line, core, side, over, far = spots()
    return [(q, line, core) for q in (far, side, over)]


def line_partners():
    chip, line, core, side, over, far = spots()
    lines = [lax.rem(line + d, PLANE) for d in range(1, PLANE)]
    same = [(chip, z, core) for z in lines]
    return same + [(chip, z, 1 - core) for z in lines] + [(chip, line, 1 - core)]


class Kept:
    def __init__(self, copies, copy, held):
        self.copies, self.copy, self.held = copies, copy, held
        copy.start()

    def wait(self):
        self.copy.wait()
        self.copies.root().free.extend(self.held)


class Copies:
    def __init__(self, sems, parent=None):
        self.sems, self.parent = sems, parent
        self.counts, self.free, self.started, self.branches = [0, 0], [], [], []

    def branch(self):
        self.branches.append(Copies(self.sems, self))
        return self.branches[-1]

    def number(self, side=0):
        if self.parent is not None:
            return self.parent.number(side)
        self.counts[side] += 1
        return self.counts[side] - 1

    def root(self):
        return self if self.parent is None else self.parent.root()

    def left(self, held=None):
        free = self.root().free
        number = free.pop() if held is not None and free else self.number(0)
        if held is not None:
            held.append(number)
        return self.sems[0].at[number]

    def enter(self, crossing=False):
        barrier = pltpu.get_barrier_semaphore()
        partners = plane_partners() + line_partners()
        chip, line, core, side, over, far = spots()
        if crossing:
            partners += [(line, lax.rem(line + d, PLANE), core) for d in range(1, PLANE)]
            partners += [(lax.rem(chip + d, PLANE), chip, core) for d in range(1, PLANE)]

        def greet(partner):
            pl.semaphore_signal(barrier, inc=1, device_id=partner, device_id_type=MESH)

        for partner in partners:
            greet(partner)
        if not crossing:
            pl.semaphore_wait(barrier, len(partners))
            return

        @pl.when(chip != line)
        def _():
            greet((line, line, core))
            greet((chip, chip, core))
            pl.semaphore_wait(barrier, len(partners) + 2)

        @pl.when(chip == line)
        def _():
            pl.semaphore_wait(barrier, len(partners))

    def send(self, source, target, partner, start=True):
        held = []
        copy = pltpu.make_async_remote_copy(
            src_ref=source,
            dst_ref=target,
            send_sem=self.left(held),
            recv_sem=self.sems[1].at[self.number(1)],
            device_id=partner,
            device_id_type=MESH,
        )
        if start:
            copy.start()
        self.started.append((copy, held))
        return copy

    def keep(self, source, target):
        held = []
        return Kept(self, pltpu.make_async_copy(source, target, self.left(held)), held)

    def finish(self):
        for copy, held in self.started:
            copy.wait_send()
            self.root().free.extend(held)
        self.started = []
        for branch in self.branches:
            branch.finish()


def arrived(copies):
    for copy in copies:
        copy.wait_recv()


def finished(copies):
    for copy in copies:
        copy.wait()


def gather_stream(copies, own_ref, out_ref, twin=True):
    chip, line, core, side, over, far = spots()
    half = own_ref.shape[0] // 2
    to_far, to_side, to_over = plane_partners()
    to_twin = (chip, line, 1 - core)

    def slot_of(q):
        return CORES * q + core if twin else q

    def part(slot, number):
        return out_ref.at[slot, pl.ds(number * half, half)]

    def own(number):
        return own_ref.at[pl.ds(number * half, half)]

    def on(slot, number, partner):
        return copies.send(part(slot, number), part(slot, number), partner)

    def share(slot, number):
        return [on(slot, number, to_twin)] if twin else []

    mine, slot_side, slot_over, slot_far = map(slot_of, (chip, side, over, far))
    sides, overs = [None, None], [None, None]
    overs[0] = copies.send(own(0), part(mine, 0), to_over)
    sides[1] = copies.send(own(1), part(mine, 1), to_side)
    sides[0] = copies.send(own(0), part(mine, 0), to_side)
    overs[1] = copies.send(own(1), part(mine, 1), to_over)
    twins = [copies.send(own(h), part(mine, h), to_twin) for h in range(2)] if twin else []
    local = copies.keep(own_ref, out_ref.at[mine])
    yield
    local.wait()
    arrived(twins)
    yield
    overs[0].wait_recv()
    far0 = on(slot_over, 0, to_side)
    twins = share(slot_over, 0)
    sides[1].wait_recv()
    far1 = on(slot_side, 1, to_over)
    twins += share(slot_side, 1)
    yield
    arrived(twins)
    yield
    sides[0].wait_recv()
    twins = share(slot_side, 0)
    overs[1].wait_recv()
    twins += share(slot_over, 1)
    yield
    arrived(twins)
    yield
    twins = [
        copies.send(part(slot_far, h), part(slot_far, h), to_twin, start=False)
        for h in range(2 if twin else 0)
    ]

    def pass_on():
        for number, copy in enumerate((far0, far1)):
            copy.wait_recv()
            if twin:
                twins[number].start()

    yield pass_on
    arrived(twins)
    yield


class Scatter:
    def __init__(self, copies, part_ref, out_ref, scratch):
        self.copies, self.part_ref, self.out_ref = copies, part_ref, out_ref
        self.twin, self.from_side, self.from_over, self.go = scratch
        chip, line, self.core, side, over, far = spots()
        self.half = out_ref.shape[0] // 2
        ignored, self.to_side, self.to_over = plane_partners()
        self.to_twin = (chip, line, 1 - self.core)
        self.chips = (far, side, over, chip)
        self.twins = [None] * 4

    def share(self, *numbers, start=True):
        for n in numbers:
            self.twins[n] = []
            for h in range(2):
                rows = pl.ds(h * self.half, self.half)
                source = self.part_ref.at[CORES * self.chips[n] + 1 - self.core, rows]
                self.twins[n].append(self.copies.send(source, self.twin.at[n, rows], self.to_twin, start))

    def share_between(self, n, slot_of, body):
        self.share(n, start=False)

        @pl.loop(0, CORES)
        def _(number):
            @pl.when(number == 1)
            def _():
                for copy in self.twins[n]:
                    copy.start()

            body(slot_of(number))

    def _pair(self, n, h):
        part = slice(h * self.half, (h + 1) * self.half)
        self.twins[n][h].wait_recv()
        own = self.part_ref[CORES * self.chips[n] + self.core, part]
        return own.astype(F32) + self.twin[n, part].astype(F32)

    def _send(self, n, h, value, target, partner):
        self.go[n, h * self.half : (h + 1) * self.half] = value.astype(BF16)
        return self.copies.send(self.go.at[n, pl.ds(h * self.half, self.half)], target, partner)

    def far(self):
        self.far0 = self._send(0, 0, self._pair(0, 0), self.from_side.at[0], self.to_side)
        self.far1 = self._send(0, 1, self._pair(0, 1), self.from_over.at[0], self.to_over)

    def side(self):
        self.side0 = self._send(1, 0, self._pair(1, 0), self.from_side.at[1], self.to_side)

    def over(self):
        self.over1 = self._send(2, 1, self._pair(2, 1), self.from_over.at[2], self.to_over)

    def cross(self):
        value = self._pair(2, 0)
        self.far0.wait_recv()
        value = value + self.from_side[0].astype(F32)
        self.over0 = self._send(2, 0, value, self.from_over.at[1], self.to_over)
        value = self._pair(1, 1)
        self.far1.wait_recv()
        value = value + self.from_over[0].astype(F32)
        self.side1 = self._send(1, 1, value, self.from_side.at[2], self.to_side)

    def end(self):
        first, second = self._pair(3, 0), self._pair(3, 1)
        self.side0.wait_recv()
        first = first + self.from_side[1].astype(F32)
        self.over1.wait_recv()
        second = second + self.from_over[2].astype(F32)
        self.over0.wait_recv()
        self.out_ref[0 : self.half] = first + self.from_over[1].astype(F32)
        self.side1.wait_recv()
        self.out_ref[self.half :] = second + self.from_side[2].astype(F32)


def drain(gather):
    for step in gather:
        if step is not None:
            step()


def scatter_scratch(rows, width):
    return [
        pltpu.VMEM((PLANE, rows, width), BF16),
        pltpu.VMEM((3, rows // 2, width), BF16),
        pltpu.VMEM((3, rows // 2, width), BF16),
        pltpu.VMEM((3, rows, width), BF16),
    ]


def inward_stream(copies, own_ref, mid, out_ref):
    chip, line, core, side, over, far = spots()
    chunk = own_ref.shape[0] // PLANE
    half = chunk // 2
    sent, moved, local = [[], []], [], []
    for h in range(2):
        part = pl.ds(h * half, half)
        for q in plane_partners():
            rows = own_ref.at[pl.ds(q[0] * chunk + h * half, half)]
            sent[h].append(copies.send(rows, mid.at[chip, part], q))
    local = [copies.keep(own_ref.at[pl.ds(chip * chunk, chunk)], mid.at[chip])]
    yield
    finished(local)
    for h in range(2):
        part = pl.ds(h * half, half)
        arrived(sent[h])
        for q in line_partners()[: PLANE - 1]:
            moved.append(copies.send(mid.at[q[1], part], out_ref.at[line, part], q))
    local = copies.keep(mid.at[line], out_ref.at[line])
    yield
    arrived(moved)
    local.wait()
    yield


class Outward:
    def __init__(self, copies, own_ref, out_ref):
        self.chip, self.line, self.core = (lax.axis_index(name) for name in ("group", "z", "core"))
        self.copies, self.chunk, self.out_ref = copies, own_ref.shape[1], out_ref
        self.arrive = [copies.number(1) for ignored in range(PLANE)]
        self.sends, self.away = [], self.chip != self.line
        for d in range(PLANE):
            z = lax.rem(self.line + d, PLANE)
            copy = self._copy(own_ref.at[z], self.chip, z, copies.left())
            self.sends.append(copy)
            if d:
                copy.start()
        self.local = pltpu.make_async_copy(
            own_ref.at[self.line], self._rows(self.chip), copies.left()
        )

        @pl.when(self.away)
        def _():
            self.sends[0].start()

        @pl.when(self.chip == self.line)
        def _():
            self.local.start()

    def _rows(self, chip):
        return self.out_ref.at[pl.ds(pl.multiple_of(chip * self.chunk, self.chunk), self.chunk)]

    def _copy(self, source, chip, z, left):
        return pltpu.make_async_remote_copy(
            src_ref=source,
            dst_ref=self._rows(chip),
            send_sem=left,
            recv_sem=self.copies.sems[1].at[self.arrive[0] + chip],
            device_id=(self.line, z, self.core),
            device_id_type=MESH,
        )

    def wait(self):
        for chip in range(PLANE):
            copy = self._copy(self._rows(chip), chip, self.line, self.copies.sems[0].at[0])

            @pl.when((chip != self.chip) | self.away)
            def _():
                copy.wait_recv()

        @pl.when(self.chip == self.line)
        def _():
            self.local.wait()

        @pl.when(self.away)
        def _():
            self.sends[0].wait_send()

        for copy in self.sends[1:]:
            copy.wait_send()


def columns_stream(copies, piece_ref, out_ref, lanes):
    chip, line, core, side, over, far = spots()
    mine = out_ref.at[CORES * line + core, :, lanes]
    sent = [copies.send(piece_ref.at[q[2], :, lanes], mine, q) for q in line_partners()]
    local = copies.keep(piece_ref.at[core, :, lanes], mine)
    yield
    arrived(sent)
    local.wait()
    yield


class Relay:
    def __init__(self, copies, piece, slot, both=True):
        self.line, self.core = lax.axis_index("z"), lax.axis_index("core")
        self.copies, self.slot, self.both = copies, slot, both
        self.cores = range(CORES) if both else (self.core,)
        self.twin = None
        count = PLANE * CORES if both else PLANE
        self.arrive = [copies.number(1) for ignored in range(count)]
        self.sends = []
        mine = slot(self.line, self.core)
        if both:
            self.twin = self._copy(piece(1 - self.core), mine, self.line, self.core, self.line, 1 - self.core, copies.left())
            self.twin.start()
        self.local = copies.keep(piece(self.core), mine)
        for step in (1, -1):
            for core in self.cores:
                copy = self._copy(piece(core), mine, self.line, self.core, self.line + step, core, copies.left())
                self._start(self._inside(self.line + step), copy)

    def _inside(self, z):
        return (z >= 0) & (z < PLANE)

    def _sem(self, z, core):
        number = CORES * z + core if self.both else z
        return self.copies.sems[1].at[self.arrive[0] + number]

    def _copy(self, source, target, z, core, to, to_core, left=None):
        return pltpu.make_async_remote_copy(
            src_ref=source,
            dst_ref=target,
            send_sem=self.copies.sems[0].at[0] if left is None else left,
            recv_sem=self._sem(z, core),
            device_id=(lax.axis_index("group"), to, to_core),
            device_id_type=MESH,
        )

    def _start(self, when, copy):
        @pl.when(when)
        def _():
            copy.start()

        self.sends.append((when, copy))

    def hop(self, distance):
        if distance == 1:
            self.local.wait()
            if self.both:
                self._copy(*[self.slot(self.line, 1 - self.core)] * 2, self.line, 1 - self.core, self.line, self.core).wait_recv()
        for step in (1, -1):
            z = self.line - step * distance
            there, on = self._inside(z), self._inside(z) & self._inside(self.line + step)
            for core in self.cores:
                slot = self.slot(jnp.clip(z, 0, PLANE - 1), core)
                left = self.copies.left() if distance < PLANE - 1 else None
                copy = self._copy(slot, slot, jnp.clip(z, 0, PLANE - 1), core, self.line + step, self.core, left)

                @pl.when(there)
                def _():
                    copy.wait_recv()

                if distance < PLANE - 1:
                    self._start(on, copy)

    def finish(self):
        if self.both:
            self.twin.wait_send()
        for when, copy in self.sends:
            @pl.when(when)
            def _():
                copy.wait_send()


def columns_relay(copies, piece_ref, out_ref, lanes):
    return Relay(
        copies,
        lambda core: piece_ref.at[core, :, lanes],
        lambda z, core: out_ref.at[CORES * z + core, :, lanes],
    )


def sum_stream(copies, grad_ref, recv, sum_ref):
    chip, line, core, side, over, far = spots()
    sent = [
        copies.send(grad_ref.at[q[1]], recv.at[line], q) for q in line_partners()[: PLANE - 1]
    ]
    local = copies.keep(grad_ref.at[line], recv.at[line])
    yield
    arrived(sent)
    local.wait()
    total = recv[0].astype(F32)
    for family in range(1, PLANE):
        total = total + recv[family].astype(F32)
    sum_ref[...] = total.astype(BF16)
    yield


def quarter_columns(ref, number):
    width = ref.shape[1] // PLANE
    return ref.at[:, pl.ds(pl.multiple_of(number * width, width), width)]


def to_ranks_stream(copies, mid, out_ref):
    chip, line, core, side, over, far = spots()
    target = quarter_columns(out_ref, chip)
    sent = [copies.send(mid.at[q[0]], target, q) for q in plane_partners()]
    local = copies.keep(mid.at[chip], target)
    yield
    arrived(sent)
    local.wait()
    yield


def unit_rows(value):
    inverse = lax.rsqrt(jnp.mean(value * value, axis=-1, keepdims=True) + EPS)
    return value * inverse, inverse


def comm_call(kernel, name, number, out_shape, in_specs, out_specs, scratch, sends, arrivals, vmem_mib=60):
    return pl.pallas_call(
        kernel,
        out_shape=out_shape,
        in_specs=in_specs,
        out_specs=out_specs,
        scratch_shapes=scratch + [pltpu.SemaphoreType.DMA((sends,)), pltpu.SemaphoreType.DMA((arrivals,))],
        compiler_params=pltpu.CompilerParams(
            collective_id=number, has_side_effects=True, vmem_limit_bytes=vmem_mib << 20
        ),
        name=name,
    )


ANY = pl.BlockSpec(memory_space=pl.ANY)
IN_VMEM = pl.BlockSpec(memory_space=pltpu.VMEM)


def gains_of(line_ref, row):
    return jnp.concatenate([line_ref[s, row : row + 1, :] for s in range(line_ref.shape[0])], axis=1)


def column_grads_stream(copies, grad_ref, recv, sum_ref, lanes):
    chip, line, core, side, over, far = spots()
    sent = [
        copies.send(grad_ref.at[CORES * q[1] + q[2], :, lanes], recv.at[core, line], q)
        for q in line_partners()
    ]
    local = copies.keep(grad_ref.at[CORES * line + core, :, lanes], recv.at[core, line])
    yield
    arrived(sent)
    local.wait()
    for number in range(CORES):
        total = recv[number, 0].astype(F32)
        for family in range(1, PLANE):
            total = total + recv[number, family].astype(F32)
        sum_ref[number, :, lanes] = total.astype(BF16)
    yield


def row_grads_stream(copies, grad_ref, mid, recv, summed, out_ref):
    chip, line, core, side, over, far = spots()
    width = out_ref.shape[1] // PLANE

    def quarter(q):
        return pl.ds(pl.multiple_of(q * width, width), width)

    sent = [copies.send(grad_ref.at[:, quarter(q[0])], mid.at[chip], q) for q in plane_partners()]
    local = copies.keep(grad_ref.at[:, quarter(chip)], mid.at[chip])
    yield
    local.wait()
    arrived(sent)
    sent = [copies.send(mid.at[q[1]], recv.at[line], q) for q in line_partners()[: PLANE - 1]]
    local = copies.keep(mid.at[line], recv.at[line])
    yield
    arrived(sent)
    local.wait()
    total = recv[0].astype(F32)
    for family in range(1, PLANE):
        total = total + recv[family].astype(F32)
    summed[...] = total.astype(BF16)
    sent = [copies.send(summed, out_ref.at[:, quarter(chip)], q) for q in plane_partners()]
    local = copies.keep(summed, out_ref.at[:, quarter(chip)])
    yield
    arrived(sent)
    local.wait()
    yield


def gain_grads_stream(copies, own, recv, summed, plane, out_ref):
    chip, line, core, side, over, far = spots()
    mine = CORES * line + core
    sent = [copies.send(own.at[CORES * q[1] + q[2]], recv.at[mine], q) for q in line_partners()]
    local = copies.keep(own.at[mine], recv.at[mine])
    yield
    arrived(sent)
    local.wait()
    summed[...] = jnp.sum(recv[...], axis=0)
    sent = [copies.send(summed, plane.at[chip], q) for q in plane_partners()]
    local = copies.keep(summed, plane.at[chip])
    yield
    arrived(sent)
    local.wait()
    out_ref[...] = jnp.sum(plane[...], axis=0)
    yield


def norm_back(grad, value, gain):
    unit, inverse = unit_rows(value)
    scaled = grad * gain
    back = inverse * (scaled - unit * jnp.mean(scaled * unit, axis=-1, keepdims=True))
    return back, jnp.sum(grad * unit, axis=0, keepdims=True)


TABLE_ROW = 2


def chunk_row(stored, part, chunk):
    plane, core, line = 2 * (stored % 2) + part, (stored // 2) % 2, stored // 4
    return ((plane * CORES + core) * PLANE + line) * chunk


def chosen(blocks, flags):
    value = blocks[0]
    for block, flag in zip(blocks[1:], flags[1:]):
        value = jnp.where(flag, block, value)
    return value


def in_place_order(table_ref, source, lanes, target, scale=None):
    chunk = BLK // 2
    blocks = source.shape[0] // BLK
    for place in range(blocks):
        flags = [table_ref[TABLE_ROW, stored] == float(place) for stored in range(blocks)]
        for part in range(2):
            rows = [chunk_row(stored, part, chunk) for stored in range(blocks)]
            block = chosen([source[row : row + chunk, lanes] for row in rows], flags)
            row = place * BLK + part * chunk
            target[row : row + chunk, :] = block if scale is None else block * scale


def in_gathered_order(table_ref, source, target, lanes):
    chunk = BLK // 2
    blocks = source.shape[0] // BLK
    for stored in range(blocks):
        flags = [table_ref[TABLE_ROW, stored] == float(place) for place in range(blocks)]
        for part in range(2):
            rows = [place * BLK + part * chunk for place in range(blocks)]
            block = chosen([source[row : row + chunk, :] for row in rows], flags)
            row = chunk_row(stored, part, chunk)
            target[row : row + chunk, lanes] = block


def attend_block(number, prompt, qs, ks, vt, att, ot_ref, lse_ref):
    start = number * CONT
    before = min(start, prompt)
    own_rows = slice(start, start + CONT)
    query = qs[own_rows, :]
    outs = []
    for head in range(2):
        masked = jnp.where(head_mask(CONT, head), query, jnp.zeros_like(query))
        own = dot_nt(ks[own_rows, :], masked)
        own = jnp.where(causal_mask(), own, -1e30)
        best = jnp.max(own, axis=0, keepdims=True)
        if before:
            past = dot_nt(ks[0:before, :], masked)
            best = jnp.maximum(best, jnp.max(past, axis=0, keepdims=True))
        terms = jnp.exp(own - best)
        total_terms = jnp.sum(terms, axis=0, keepdims=True)
        rows = slice(head * HEAD, (head + 1) * HEAD)
        out = matmul(vt[rows, own_rows], terms.astype(BF16))
        if before:
            terms = jnp.exp(past - best)
            total_terms = total_terms + jnp.sum(terms, axis=0, keepdims=True)
            out = out + matmul(vt[rows, 0:before], terms.astype(BF16))
        outs.append(out / total_terms)
        lse_ref[head : head + 1, own_rows] = best + jnp.log(total_terms)
    joined = jnp.concatenate(outs, axis=0)
    ot_ref[:, own_rows] = joined.astype(BF16)
    att[own_rows, :] = joined.T.astype(BF16)


def chip_slots(group):
    chip, line, core, side, over, far = spots()
    if group == "near":
        return 2 * CORES, lambda n: CORES * (side + lax.div(n, CORES) * (over - side)) + lax.rem(n, CORES)
    q = {"own": chip, "far": far}[group]
    return CORES, lambda n: CORES * q + lax.rem(core + 1 + n, CORES)


def each_slot(group, body):
    count, slot_of = chip_slots(group)

    @pl.loop(0, count)
    def _(n):
        body(slot_of(n))


def front_kernel(
    tok_ref, cot_ref, gain1_ref, gain2_ref, place_ref, wq_ref, wk_ref, wv_ref, wo_ref, wg_ref, wu_ref, wd_ref,
    n1_out, x_out, cot_out, line_out, wqkv_out, wo_out, q_out, k_out, v_out, ot_out, lse_out, att_out,
    h1_out, dn2_out, mix_out, ggu_out, gd_out, gusum_out, table_out,
    *rest,
):
    scratch, other, rest = rest[:4], rest[4:8], rest[8:]
    x_ref, cotp_ref, line_ref, wqkv, wout, qs, ks, vs, ot_ref, lse_ref, att_ref, rest = *rest[:11], rest[11:]
    h1_ref, dn2_ref, ggu_ref, gd_ref, gusum, rest = *rest[:5], rest[5:]
    small_ref, recv_gu, rest = *rest[:2], rest[2:]
    mid_x, mid_c, mid_o, down, tables, table, pieces, gate_w, up_w, gu, normed, rest = *rest[:11], rest[11:]
    n1s, n2s, cots, qkv, vt, att, parts, summed, wgu, wgu_t, wd, wd_t, us, dabs, *sems = rest
    copies = Copies(sems)
    chip, line, core, side, over, far = spots()
    total, heads = qkv.shape[0], wo_ref.shape[0]
    hidden, lanes = wd_ref.shape[0], wd.shape[0]
    chunk, width = x_ref.shape[1], x_ref.shape[2]
    rows = PLANE * chunk
    ranks = PLANE * CORES
    share = hidden // PLANE
    stores = []

    def store(source, target):
        stores.append(copies.keep(source, target))

    loads = [copies.keep(wg_ref, gate_w), copies.keep(wu_ref, up_w)]
    for c in range(CORES):
        column = pl.ds(pl.multiple_of((CORES * chip + c) * heads, heads), heads)
        for n, w in enumerate((wq_ref, wk_ref, wv_ref)):
            loads.append(copies.keep(w.at[:, column], pieces.at[c, :, n * heads : (n + 1) * heads]))
    small_ref[...] = jnp.zeros_like(small_ref)
    small_ref[0:1] = gain1_ref[...].astype(F32)
    small_ref[1:2] = gain2_ref[...].astype(F32)
    small_ref[TABLE_ROW : TABLE_ROW + 1, 0 : place_ref.shape[1]] = place_ref[...].astype(F32)
    copies.enter()
    early = copies.branch()
    tokens = inward_stream(early, tok_ref, mid_x, x_ref)
    next(tokens)
    out_part = quarter_columns(wo_ref, chip)
    out_sent = [early.send(out_part, mid_o.at[line], q) for q in line_partners()[: PLANE - 1]]
    out_kept = copies.keep(out_part, mid_o.at[line])
    mine = CORES * line + core
    small = [early.send(small_ref, line_ref.at[mine], q) for q in line_partners()]
    small += [early.send(small_ref, tables.at[chip], q) for q in plane_partners()]
    local = [copies.keep(small_ref, line_ref.at[mine]), copies.keep(small_ref, tables.at[chip])]
    finished(loads)
    next(tokens)
    cotangents = inward_stream(early, cot_ref, mid_c, cotp_ref)
    next(cotangents)
    gu[...] = jnp.zeros_like(gu)
    for k in range(PLANE):
        @pl.when(chip == k)
        def _():
            for c in range(CORES):
                for z in range(PLANE):
                    begin, at = (CORES * z + c) * hidden + k * share, z * share
                    gu[c, :, at : at + share] = gate_w[:, begin : begin + share]
                    gu[c, :, lanes + at : lanes + at + share] = up_w[:, begin : begin + share]
    wd[hidden:lanes] = jnp.zeros((lanes - hidden, width), BF16)
    arrived(out_sent)
    out_kept.wait()
    out_rows = to_ranks_stream(early, mid_o, wout)
    next(out_rows)
    arrived(small)
    finished(local)
    load = [copies.keep(tables.at[line], table), copies.keep(tables.at[line], table_out)]
    store(line_ref, line_out)
    gain = gains_of(line_ref, 0)
    next(tokens)
    projections = columns_relay(copies, pieces, wqkv, pl.ds(0, 3 * heads))
    for n in range(PLANE):
        unit, ignored = unit_rows(x_ref[n].astype(F32))
        normed[n * chunk : (n + 1) * chunk] = (unit * gain).astype(BF16)
    gathering = copies.branch()
    gather = gather_stream(gathering, normed, n1s)
    next(gather)
    finished(load)
    next(gather)
    projections.hop(1)
    next(gather)
    projections.hop(2)
    next(gather)
    next(gather)
    next(cotangents)

    def slot_rows(slot):
        return pl.ds(pl.multiple_of(slot * rows, rows), rows)

    def project(slot):
        qkv[slot_rows(slot), :] = matmul(n1s[slot], wqkv[...].reshape(width, 3 * heads)).astype(BF16)

    next(gather)
    projections.hop(3)
    next(gather)()
    each_slot("own", project)
    each_slot("near", project)
    next(gather)
    each_slot("far", project)
    for source, target in ((n1s, n1_out), (x_ref, x_out), (wqkv, wqkv_out)):
        store(source, target)

    for n, ref in enumerate((qs, ks, vs)):
        scale = jnp.bfloat16(SCALE) if n == 0 else None
        in_place_order(table, qkv, slice(n * heads, (n + 1) * heads), ref, scale)
    next(cotangents)
    gather_cot = gather_stream(copies, cotp_ref.reshape(rows, width), cots)
    next(gather_cot)
    gate_up = columns_relay(copies, gu, wgu, pl.ds(0, 2 * lanes))
    down_part = wd_ref.at[pl.ds(pl.multiple_of(chip * share, 8), share)]
    down_rows = Relay(copies, lambda core: down_part, lambda z, core: down.at[z], False)
    for start in range(0, total, CONT):
        part = slice(start, start + CONT)
        vt[:, part] = vs[part, :].astype(F32).T.astype(BF16)
    for source, target in ((qs, q_out), (ks, k_out), (vs, v_out), (cotp_ref, cot_out)):
        store(source, target)
    for number in range(total // CONT):
        attend_block(number, total // 2, qs, ks, vt, att, ot_ref, lse_ref)
        if number == 5:
            next(gather_cot)
            next(gather_cot)
            next(gather_cot)
            gate_up.hop(1)
    in_gathered_order(table, att, att_ref, slice(0, heads))
    next(out_rows)

    def spread(slot):
        parts[slot] = matmul(att_ref[slot_rows(slot), :], wout[...]).astype(BF16)

    scattering = copies.branch()
    scatter = Scatter(scattering, parts, summed, scratch)
    each_slot("far", spread)
    scatter.share(0)
    each_slot("near", spread)
    scatter.share(1, 2)
    each_slot("own", spread)
    scatter.share(3)
    scatter.far()
    scatter.side()
    scatter.over()
    next(gather_cot)
    down_rows.hop(1)
    next(gather_cot)
    next(gather_cot)()
    gate_up.hop(2)
    down_rows.hop(2)
    for source, target in ((wout, wo_out), (ot_ref, ot_out), (lse_ref, lse_out), (att_ref, att_out)):
        store(source, target)
    scatter.cross()
    next(gather_cot)
    gate_up.hop(3)
    for s in range(ranks):
        wgu_t[:, s * heads : (s + 1) * heads] = wgu[s].T
    down_rows.hop(3)
    for z in range(PLANE):
        wd[z * share : (z + 1) * share] = down[z]
    wd_t[...] = wd[...].T
    early.finish()
    gathering.finish()
    gain = gains_of(line_ref, 1)
    scatter.end()
    for n in range(PLANE):
        part = slice(n * chunk, (n + 1) * chunk)
        hidden_rows = x_ref[n].astype(F32) + summed[part]
        h1_ref[part] = hidden_rows
        unit, ignored = unit_rows(hidden_rows)
        normed[part] = (unit * gain).astype(BF16)
    gather = gather_stream(copies, normed, n2s)
    next(gather)
    store(h1_ref, h1_out)
    next(gather)
    scattering.finish()
    finished(stores)
    stores.clear()

    def feed_rows(slot, at):
        block, cot = n2s[slot, at, :], cots[slot, at, :]
        both = matmul(block, wgu[...].reshape(width, 2 * lanes))
        gate, upper = both[:, :lanes], both[:, lanes:]
        bend = jnp.tanh(0.7978845608028654 * (gate + 0.044715 * gate * gate * gate))
        half = 0.5 * (1.0 + bend)
        active = gate * half
        slope = half + (0.5 * 0.7978845608028654) * gate * (1.0 - bend * bend) * (
            1.0 + 3 * 0.044715 * gate * gate
        )
        mixed = (active * upper).astype(BF16)
        us[slot, at, :] = mixed
        parts[slot, at, :] = matmul(mixed, wd[...]).astype(BF16)
        du = matmul(cot, wd_t[...])
        dabs[slot, at, 0:lanes] = (du * upper * slope).astype(BF16)
        dabs[slot, at, lanes:] = (du * active).astype(BF16)
        n1s[slot, at, :] = matmul(dabs[slot, at, :], wgu_t[...]).astype(BF16)

    def feed(slot):
        feed_rows(slot, pl.ds(0, rows))

    def feed_halves(which, between):
        count, slot_of = chip_slots("near")
        half = rows // 2

        @pl.loop(0, count)
        def _(n):
            @pl.when(n == count - 1)
            def _():
                between()

            number = 1 - lax.div(n, CORES) if which == 0 else lax.div(n, CORES)
            feed_rows(slot_of(n), pl.ds(pl.multiple_of(number * half, half), half))

    scatter = Scatter(copies, n1s, dn2_ref, other)
    each_slot("own", feed)
    scatter.share(3)
    next(gather)
    next(gather)
    feed_halves(0, lambda: None)
    next(gather)
    next(gather)
    feed_halves(1, next(gather))
    scatter.share(1, 2)
    next(gather)
    scatter.side()
    scatter.over()
    scatter.share_between(0, chip_slots("far")[1], feed)
    scatter.far()
    store(parts, mix_out)

    def by_rows(s):
        columns = pl.ds(pl.multiple_of(s * heads, heads), heads)
        grad = jnp.zeros((heads, 2 * lanes), F32)
        for slot in range(ranks):
            grad = grad + inner(n2s[slot, :, columns], dabs[slot])
        ggu_ref[s] = grad.astype(BF16)

    pl.loop(0, ranks)(by_rows)
    columns = column_grads_stream(copies, ggu_ref, recv_gu, gusum, pl.ds(0, EARLY))
    next(columns)
    store(ggu_ref, ggu_out)
    scatter.cross()
    grad = jnp.zeros((lanes, width), F32)
    for slot in range(ranks):
        grad = grad + inner(us[slot], cots[slot])
    for z in range(PLANE):
        for h in range(2):
            block = grad[z * share : (z + 1) * share, h * (width // 2) : (h + 1) * (width // 2)]
            gd_ref[z, h] = block.astype(BF16)
    store(gd_ref, gd_out)
    scatter.end()
    store(dn2_ref, dn2_out)
    next(columns)
    store(gusum, gusum_out)
    for relay in (projections, gate_up, down_rows):
        relay.finish()
    copies.finish()
    finished(stores)


def front(tokens, cotangent, gain1, gain2, places, w_query, w_key, w_value, w_out, w_gate, w_up, w_down):
    rows, width = tokens.shape
    heads, hidden = w_out.shape[0], w_down.shape[0]
    lanes = -(-hidden // 128) * 128
    ranks = PLANE * CORES
    total = ranks * rows
    small = (8, heads)
    chunks, blocks = (PLANE, rows // PLANE, width), (ranks, rows, width)
    low = lambda *shape: jax.ShapeDtypeStruct(shape, BF16)
    wide = lambda *shape: jax.ShapeDtypeStruct(shape, F32)
    held = [
        low(*chunks), low(*chunks), wide(ranks, *small), low(ranks, heads, 3 * heads),
        low(heads, width), low(total, heads), low(total, heads), low(total, heads), low(heads, total),
        wide(2, total), low(total, heads), wide(rows, width), wide(rows, width),
    ]
    grads = [low(ranks, heads, 2 * lanes), low(PLANE, 2, hidden // PLANE, width // 2), low(CORES, heads, EARLY)]
    shapes = [low(*blocks)] + held + [low(*blocks)] + grads + [wide(*small)]
    scratch = scatter_scratch(rows, width) * 2
    scratch += [pltpu.VMEM(a.shape, a.dtype) for a in held + grads]
    held = lambda *shape: pltpu.VMEM(shape, BF16)
    scratch += [pltpu.VMEM(small, F32), held(CORES, PLANE, heads, EARLY)]
    scratch += [held(*chunks), held(*chunks), held(PLANE, heads, width // PLANE), held(PLANE, hidden // PLANE, width)]
    scratch += [pltpu.VMEM((PLANE,) + small, F32), pltpu.SMEM(small, F32)]
    scratch += [held(CORES, heads, 3 * heads), held(*w_gate.shape), held(*w_up.shape), held(CORES, heads, 2 * lanes)]
    scratch += [held(rows, width), held(*blocks), held(*blocks), held(*blocks), held(total, 3 * heads)]
    scratch += [held(heads, total), held(total, heads), held(*blocks), pltpu.VMEM((rows, width), F32)]
    scratch += [held(ranks, heads, 2 * lanes), held(2 * lanes, width), held(lanes, width), held(width, lanes)]
    scratch += [held(ranks, rows, lanes), held(ranks, rows, 2 * lanes)]
    return comm_call(
        front_kernel, "front", 1, tuple(shapes), [ANY] * 2 + [IN_VMEM] * 3 + [ANY] * 7, (ANY,) * len(shapes),
        scratch, FRONT_SEMS[0], FRONT_SEMS[1],
    )(tokens, cotangent, gain1, gain2, places, w_query, w_key, w_value, w_out, w_gate, w_up, w_down)


def attend_back_block(number, prompt, qs, ks, vs, gs, kt, ot_ref, lse_ref, dqs, dks, dvs):
    start = number * CONT
    own = slice(start, start + CONT)
    query, grad = qs[own, :], gs[own, :]
    product = grad.astype(F32).T * ot_ref[:, own].astype(F32)
    outs = []
    for head in range(2):
        rows = slice(head * HEAD, (head + 1) * HEAD)
        delta = jnp.sum(product[rows], axis=0, keepdims=True)
        lse = lse_ref[head : head + 1, own]
        keep = head_mask(CONT, head)
        query_head = jnp.where(keep, query, jnp.zeros_like(query))
        grad_head = jnp.where(keep, grad, jnp.zeros_like(grad))
        dq = None
        for keys in [own] + ([slice(0, min(start, prompt))] if start else []):
            prob = jnp.exp(dot_nt(ks[keys, :], query_head) - lse)
            if keys == own:
                prob = jnp.where(causal_mask(), prob, 0.0)
            dprob = dot_nt(vs[keys, :], grad_head)
            dscore = (prob * (dprob - delta)).astype(BF16)
            dvs[keys, :] += matmul(prob.astype(BF16), grad_head)
            dks[keys, :] += matmul(dscore, query_head)
            term = matmul(kt[rows, keys], dscore)
            dq = term if dq is None else dq + term
        outs.append(dq)
    dqs[own, :] = (jnp.concatenate(outs, axis=0) * SCALE).T.astype(BF16)


def rear_kernel(
    table, summed_in, h1_in, cot_in, x_in, line_in, n1_in, mix_in, wqkv_in, wo_in,
    q_in, k_in, v_in, ot_in, lse_in, att_in, gu_ref, down_ref, gusum_in,
    out_ref, grad_ref, gains_ref, gate_end, up_end, q_end, k_end, v_end, wo_all, wd_end,
    *rest,
):
    scratch, other, rest = rest[:4], rest[4:8], rest[8:]
    summed_ref, h1_ref, cot_ref, x_ref, line_ref, wqkv_ref, wo_ref, rest = *rest[:7], rest[7:]
    qs, ks, vs, ot_ref, lse_ref, att_ref, rest = *rest[:6], rest[6:]
    gate_out, up_out, q_out, k_out, v_out, wd_out, rest = *rest[:6], rest[6:]
    n1s, mix, parts, gas, datt, gs, kt, dqs, dks, dvs, dqkv, w_t, rest = *rest[:12], rest[12:]
    dh1, summed, mixed, low, low_tok, low_out, rest = *rest[:6], rest[6:]
    recv_gu, sum_gu, gu_all, gqkv, recv_qkv, sum_qkv, qkv_all, gwo, rest = *rest[:8], rest[8:]
    mid_wo, recv_wo, sum_wo, recv_wd, sum_wd, down_all, own, recv_gain, sum_gain, plane, *sems = rest
    copies = Copies(sems)
    total, heads = att_ref.shape
    ranks = PLANE * CORES
    chunk, width = x_ref.shape[1], x_ref.shape[2]
    rows = PLANE * chunk
    share = down_ref.shape[2]
    hidden = PLANE * share
    lanes = gu_ref.shape[2] // 2

    def load(*pairs):
        return [copies.keep(source, target) for source, target in pairs]

    first = load((summed_in, summed_ref), (h1_in, h1_ref), (cot_in, cot_ref), (line_in, line_ref))
    second_load = load((k_in, ks), (wqkv_in, wqkv_ref), (wo_in, wo_ref))
    third = load((mix_in, mix))
    fourth = load((q_in, qs), (v_in, vs), (ot_in, ot_ref), (lse_in, lse_ref), (x_in, x_ref))
    fifth = load((n1_in, n1s), (att_in, att_ref), (gusum_in, sum_gu.at[:, :, pl.ds(0, EARLY)]))
    stores = []
    copies.enter(crossing=True)
    finished(first)
    gain = gains_of(line_ref, 1)
    gain2_sum = jnp.zeros((1, width), F32)
    for n in range(PLANE):
        part = slice(n * chunk, (n + 1) * chunk)
        back, by_gain = norm_back(summed_ref[part], h1_ref[part], gain)
        grad = cot_ref[n].astype(F32) + back
        gain2_sum = gain2_sum + by_gain
        dh1[part] = grad
        low[part] = grad.astype(BF16)
    gather = gather_stream(copies, low, gas)
    next(gather)
    gate_up = column_grads_stream(copies, gu_ref, recv_gu, sum_gu, pl.ds(EARLY, 2 * lanes - EARLY))
    next(gate_up)
    down = sum_stream(copies, down_ref, recv_wd, sum_wd)
    next(down)
    finished(second_load)
    for start in range(0, total, CONT):
        part = slice(start, start + CONT)
        kt[:, part] = ks[part, :].astype(F32).T.astype(BF16)
    for s in range(ranks):
        w_t[:, s * heads : (s + 1) * heads] = wqkv_ref[s].T
    dks[...] = jnp.zeros_like(dks)
    dvs[...] = jnp.zeros_like(dvs)

    def slot_rows(slot):
        return pl.ds(pl.multiple_of(slot * rows, rows), rows)

    def attended_grad(slot):
        datt[slot_rows(slot), :] = outer(gas[slot], wo_ref[...]).astype(BF16)

    next(gather)
    each_slot("own", attended_grad)
    next(gather)
    finished(third)
    next(gather)
    next(gather)
    next(gather)
    each_slot("near", attended_grad)
    next(gather)()
    mixing = copies.branch()
    second = Scatter(mixing, mix, mixed, other)
    second.share(0, 1, 2, 3)
    second.far()
    second.side()
    second.over()
    next(gather)
    each_slot("far", attended_grad)
    finished(fourth)
    finished(fifth)
    grad = jnp.zeros((heads, width), F32)
    for slot in range(ranks):
        grad = grad + inner(att_ref[slot * rows : (slot + 1) * rows, :], gas[slot])
    gwo[...] = grad.astype(BF16)
    out_w = row_grads_stream(copies, gwo, mid_wo, recv_wo, sum_wo, wo_all)
    next(out_w)
    in_place_order(table, datt, slice(0, heads), gs)
    for number in range(total // CONT):
        attend_back_block(number, total // 2, qs, ks, vs, gs, kt, ot_ref, lse_ref, dqs, dks, dvs)
        if number == 3:
            second.cross()
        if number == 4:
            next(gate_up)
            gather_gu = gather_stream(copies, sum_gu, gu_all, twin=False)
            next(gather_gu)
            next(out_w)
    ks_low, vs_low = gs, datt
    for start in range(0, total, CONT):
        part = slice(start, start + CONT)
        ks_low[part, :] = dks[part, :].astype(BF16)
        vs_low[part, :] = dvs[part, :].astype(BF16)
    for n, ref in enumerate((dqs, ks_low, vs_low)):
        in_gathered_order(table, ref, dqkv, slice(n * heads, (n + 1) * heads))

    def spread(slot):
        parts[slot] = matmul(dqkv[slot_rows(slot), :], w_t[...]).astype(BF16)

    scatter = Scatter(copies, parts, summed, scratch)
    each_slot("far", spread)
    scatter.share(0)
    each_slot("near", spread)
    scatter.share(1, 2)
    each_slot("own", spread)
    scatter.share(3)
    scatter.far()
    scatter.side()
    scatter.over()
    next(gather_gu)
    next(gather_gu)
    second.end()
    for n in range(PLANE):
        part = slice(n * chunk, (n + 1) * chunk)
        low_out[n] = (h1_ref[part] + mixed[part]).astype(BF16)
    output = Outward(copies, low_out, out_ref)

    def by_rows(s):
        columns = pl.ds(pl.multiple_of(s * heads, heads), heads)
        grad = jnp.zeros((heads, 3 * heads), F32)
        for slot in range(ranks):
            grad = grad + inner(n1s[slot, :, columns], dqkv[slot * rows : (slot + 1) * rows, :])
        gqkv[s] = grad.astype(BF16)

    pl.loop(0, ranks)(by_rows)
    qkv = column_grads_stream(copies, gqkv, recv_qkv, sum_qkv, pl.ds(0, 3 * heads))
    next(qkv)
    scatter.cross()
    next(down)
    gather_down = gather_stream(copies, sum_wd, down_all, twin=False)
    next(gather_down)
    next(out_w)
    drain(gather_gu)

    def format_gate(chip, c, z):
        begin, at = (CORES * z + c) * hidden + chip * share, z * share
        gate_out[:, begin : begin + share] = gu_all[chip, c, :, at : at + share]
        up_out[:, begin : begin + share] = gu_all[chip, c, :, lanes + at : lanes + at + share]

    for chip in range(PLANE):
        for c in range(CORES):
            for z in range(PLANE):
                format_gate(chip, c, z)
    stores += load((gate_out, gate_end), (up_out, up_end))
    scatter.end()
    gain = gains_of(line_ref, 0)
    gain1_sum = jnp.zeros((1, width), F32)
    for n in range(PLANE):
        part = slice(n * chunk, (n + 1) * chunk)
        back, by_gain = norm_back(summed[part], x_ref[n].astype(F32), gain)
        gain1_sum = gain1_sum + by_gain
        low_tok[n] = (dh1[part] + back).astype(BF16)
    tokens = Outward(copies, low_tok, grad_ref)
    own[...] = jnp.zeros_like(own)
    for s in range(ranks):
        part = slice(s * heads, (s + 1) * heads)
        own[s, 0:1] = gain1_sum[:, part]
        own[s, 1:2] = gain2_sum[:, part]
    gains = gain_grads_stream(copies, own, recv_gain, sum_gain, plane, gains_ref)
    next(gains)
    next(gather_down)
    next(gather_down)
    next(qkv)
    gather_qkv = gather_stream(copies, sum_qkv, qkv_all, twin=False)
    next(gather_qkv)
    drain(gather_down)
    for chip in range(PLANE):
        for h in range(2):
            wd_out[chip * share : (chip + 1) * share, h * (width // 2) : (h + 1) * (width // 2)] = down_all[chip, h]
    stores += load((wd_out, wd_end))
    next(gather_qkv)
    next(gather_qkv)
    next(gains)
    drain(gather_qkv)
    for chip in range(PLANE):
        for c in range(CORES):
            begin = (CORES * chip + c) * heads
            for n, ref in enumerate((q_out, k_out, v_out)):
                ref[:, begin : begin + heads] = qkv_all[chip, c, :, n * heads : (n + 1) * heads]
    stores += load((q_out, q_end), (k_out, k_end), (v_out, v_end))
    next(out_w)
    next(gains)
    output.wait()
    tokens.wait()
    copies.finish()
    finished(stores)


def rear(table, summed, h1, cot, x, lines, n1, mixed, w_qkv, w_o, qs, ks, vs, ot, lse, att, gate_up_grad, down_grad, gate_up_sum, ff):
    ranks = PLANE * CORES
    rows, width = h1.shape
    total, heads = att.shape
    hidden = PLANE * down_grad.shape[2]
    quarter = width // PLANE
    small = lines.shape[1:]
    low = lambda *shape: jax.ShapeDtypeStruct(shape, BF16)
    shapes = (
        low(rows, width), low(rows, width), jax.ShapeDtypeStruct(small, F32),
        low(heads, ff), low(heads, ff), low(heads, width), low(heads, width), low(heads, width),
        low(heads, width), low(hidden, width),
    )
    held = lambda *shape: pltpu.VMEM(shape, BF16)
    wide = lambda *shape: pltpu.VMEM(shape, F32)
    scratch = scatter_scratch(rows, width) * 2
    scratch += [pltpu.VMEM(a.shape, a.dtype) for a in (summed, h1, cot, x, lines, w_qkv, w_o, qs, ks, vs, ot, lse, att)]
    scratch += [held(*shapes[n].shape) for n in (3, 4, 5, 6, 7, 9)]
    scratch += [held(*n1.shape)] * 4 + [held(total, heads)] * 2 + [held(heads, total), held(total, heads)]
    scratch += [wide(total, heads)] * 2 + [held(total, 3 * heads), held(3 * heads, width)]
    scratch += [wide(rows, width)] * 3 + [held(rows, width)] + [held(*x.shape)] * 2
    for grad in (gate_up_grad, w_qkv):
        piece = (CORES,) + grad.shape[1:]
        if grad is w_qkv:
            scratch += [held(*grad.shape)]
        columns = grad.shape[2] - (0 if grad is w_qkv else EARLY)
        scratch += [held(CORES, PLANE, grad.shape[1], columns), held(*piece), held(PLANE, *piece)]
    scratch += [held(heads, width)]
    scratch += [held(PLANE, heads, quarter)] * 2 + [held(heads, quarter)]
    scratch += [held(*down_grad.shape), held(*down_grad.shape[1:]), held(*down_grad.shape)]
    scratch += [wide(*lines.shape)] * 2 + [wide(*small), wide(PLANE, *small)]
    return comm_call(
        rear_kernel, "rear", 2, shapes,
        [pl.BlockSpec(memory_space=pltpu.SMEM)] + [ANY] * 18,
        (ANY, ANY, IN_VMEM) + (ANY,) * 7,
        scratch, REAR_SEMS[0], REAR_SEMS[1],
    )(
        table, summed, h1, cot, x, lines, n1, mixed, w_qkv, w_o, qs, ks, vs, ot, lse, att,
        gate_up_grad, down_grad, gate_up_sum,
    )


def finish_kernel(*refs):
    count = (len(refs) - 1) // 4
    inputs, outputs, held, stage = (refs[n * count : (n + 1) * count] for n in range(4))
    sems = refs[-1]
    loads, stores = [], []
    for n, (source, buffer) in enumerate(zip(inputs, held)):
        loads.append(pltpu.make_async_copy(source, buffer, sems.at[0, n]))
        loads[-1].start()
    for n, (target, buffer, wide) in enumerate(zip(outputs, held, stage)):
        loads[n].wait()
        if buffer.shape != target.shape:
            wide[...] = buffer[n - len(inputs) + 2 : n - len(inputs) + 3, :]
            buffer = wide
        elif buffer.dtype != target.dtype:
            wide[...] = buffer[...].astype(F32)
            buffer = wide
        stores.append(pltpu.make_async_copy(buffer, target, sems.at[1, n]))
        stores[-1].start()
    for copy in stores:
        copy.wait()


def finish(tokens, grads, gains):
    inputs = list(tokens) + list(grads) + [gains] * 2
    shapes = [jax.ShapeDtypeStruct(a.shape, a.dtype) for a in tokens]
    shapes += [jax.ShapeDtypeStruct(a.shape, F32) for a in grads]
    shapes += [jax.ShapeDtypeStruct((1, gains.shape[1]), F32)] * 2
    held = [pltpu.VMEM(a.shape, a.dtype) for a in inputs]
    stage = [pltpu.VMEM((8, 128), F32)] * len(tokens) + [pltpu.VMEM(a.shape, F32) for a in shapes[len(tokens) :]]
    return pl.pallas_call(
        finish_kernel,
        out_shape=tuple(shapes),
        in_specs=[ANY] * len(inputs),
        out_specs=(ANY,) * len(inputs),
        scratch_shapes=held + stage + [pltpu.SemaphoreType.DMA((2, len(inputs)))],
        compiler_params=pltpu.CompilerParams(vmem_limit_bytes=60 << 20),
        name="finish",
    )(*inputs)


def plane_local(
    tokens,
    cotangent,
    block_table,
    norm1_gain,
    w_query,
    w_key,
    w_value,
    w_out,
    norm2_gain,
    w_gate,
    w_up,
    w_down,
):
    (
        n1, x, cot, gains, w_qkv, w_o, qs, ks, vs, ot, lse, att, h1, dn2, mixed, g_gu, g_down, gu_sum, table
    ) = front(
        tokens[0], cotangent[0], norm1_gain[None], norm2_gain[None], block_table,
        w_query, w_key, w_value, w_out, w_gate, w_up, w_down,
    )
    output, tokens_grad, gain_grads, *grads = rear(
        table, dn2, h1, cot, x, gains, n1, mixed, w_qkv, w_o, qs, ks, vs, ot, lse, att, g_gu, g_down, gu_sum,
        w_gate.shape[1],
    )
    output, tokens_grad, gate, up, query, key, value, out, down, gain1, gain2 = finish(
        (output, tokens_grad), grads, gain_grads
    )
    return (
        output[None], tokens_grad[None],
        gain1[0], query, key, value, out, gain2[0], gate, up, down,
    )


def plane_solution(mesh):
    split = Mesh(mesh.devices.reshape(PLANE, PLANE, CORES), ("group", "z", "core"))
    ctx = ("z", "core")
    token, weight = P("group", ctx, None), P(ctx, None)
    in_specs = (token, token, P("group", None), P(ctx)) + (weight,) * 4 + (P(ctx),) + (weight,) * 3
    out_specs = (token, token, P(ctx)) + (weight,) * 4 + (P(ctx),) + (weight,) * 3
    return jax.shard_map(
        plane_local, mesh=split, in_specs=in_specs, out_specs=out_specs, check_vma=False
    )


def family_solution(mesh):
    in_specs = (
        P("group", "ctx", None),
        P("group", "ctx", None),
        P("group", None),
        P("ctx"),
        P("ctx", None),
        P("ctx", None),
        P("ctx", None),
        P("ctx", None),
        P("ctx"),
        P("ctx", None),
        P("ctx", None),
        P("ctx", None),
    )
    out_specs = (
        P("group", "ctx", None),
        P("group", "ctx", None),
        P("ctx"),
        P("ctx", None),
        P("ctx", None),
        P("ctx", None),
        P("ctx", None),
        P("ctx"),
        P("ctx", None),
        P("ctx", None),
        P("ctx", None),
    )
    return jax.shard_map(local, mesh=mesh, in_specs=in_specs, out_specs=out_specs, check_vma=False)


def solution(mesh):
    groups, ranks = mesh.shape["group"], mesh.shape["ctx"]
    if groups == PLANE and ranks == 2 * PLANE:
        return plane_solution(mesh)
    return family_solution(mesh)
```

```python
import jax
import jax.numpy as jnp
from jax import lax
from jax.experimental import pallas as pl
from jax.experimental.pallas import tpu as pltpu
from jax.sharding import Mesh
from jax.sharding import PartitionSpec as P

HEADS = 16
HEAD = 64
BLK = 128
KEYBLK = 512
PROMPT_MAX = 2048
CONT = 256


EPS = 1e-06
SCALE = 0.125


def rms_scale(hidden, gain):
    return hidden * lax.rsqrt(jnp.mean(hidden * hidden, axis=-1, keepdims=True) + EPS) * gain


def gated(gate, upper):
    return jax.nn.gelu(gate, approximate=True) * upper


def matmul(left, right):
    return jnp.dot(left, right, preferred_element_type=jnp.float32)


def inner(left, right):
    return lax.dot_general(
        left, right, (((0,), (0,)), ((), ())), preferred_element_type=jnp.float32
    )


def outer(left, right):
    return lax.dot_general(
        left, right, (((1,), (1,)), ((), ())), preferred_element_type=jnp.float32
    )


def family_index(table):
    offsets = jnp.arange(BLK, dtype=jnp.int32)
    return (table[:, None] * BLK + offsets[None, :]).reshape(-1)


def segment_of(index, prompt_len):
    return jnp.where(index < prompt_len, 0, 1 + (index - prompt_len) // CONT)


def allowed(query_index, key_index, prompt_len):
    query_seg = segment_of(query_index, prompt_len)
    key_seg = segment_of(key_index, prompt_len)
    same = (query_seg[:, None] == key_seg[None, :]) & (key_index[None, :] <= query_index[:, None])
    prompt = (key_seg[None, :] == 0) & (query_seg[:, None] > 0)
    return same | prompt


def head_split(block):
    return block.reshape(block.shape[0], HEADS, HEAD)


def scores_of(query_heads, key_block, query_index, key_index, prompt_len):
    score = (
        jnp.einsum(
            "qhd,khd->hqk", query_heads, head_split(key_block), preferred_element_type=jnp.float32
        )
        * SCALE
    )
    return (score, allowed(query_index, key_index, prompt_len))


def attend_stats(queries, keys, query_index, key_index, prompt_len):
    query_heads = head_split(queries)

    def step(carry, number):
        best, total = carry
        start = number * KEYBLK
        key_block = lax.dynamic_slice_in_dim(keys, start, KEYBLK, 0)
        block_index = lax.dynamic_slice_in_dim(key_index, start, KEYBLK, 0)
        score, keep = scores_of(query_heads, key_block, query_index, block_index, prompt_len)
        score = jnp.where(keep[None], score, -1e30)
        larger = jnp.maximum(best, jnp.max(score, axis=-1))
        terms = jnp.where(keep[None], jnp.exp(score - larger[:, :, None]), 0.0)
        total = total * jnp.exp(best - larger) + jnp.sum(terms, axis=-1)
        return ((larger, total), None)

    start_best = jnp.full((HEADS, queries.shape[0]), -1e30, jnp.float32)
    (best, total), ignored = lax.scan(
        step, (start_best, jnp.zeros_like(start_best)), jnp.arange(keys.shape[0] // KEYBLK)
    )
    return best + jnp.log(total)


def attend_values(queries, keys, values, lse, query_index, key_index, prompt_len):
    query_heads = head_split(queries)

    def step(acc, number):
        start = number * KEYBLK
        key_block = lax.dynamic_slice_in_dim(keys, start, KEYBLK, 0)
        value_block = lax.dynamic_slice_in_dim(values, start, KEYBLK, 0)
        block_index = lax.dynamic_slice_in_dim(key_index, start, KEYBLK, 0)
        score, keep = scores_of(query_heads, key_block, query_index, block_index, prompt_len)
        prob = jnp.where(keep[None], jnp.exp(score - lse[:, :, None]), 0.0).astype(jnp.bfloat16)
        return (
            acc
            + jnp.einsum(
                "hqk,khd->qhd", prob, head_split(value_block), preferred_element_type=jnp.float32
            ),
            None,
        )

    start_acc = jnp.zeros((queries.shape[0], HEADS, HEAD), jnp.float32)
    acc, ignored = lax.scan(step, start_acc, jnp.arange(keys.shape[0] // KEYBLK))
    return acc.reshape(queries.shape[0], HEADS * HEAD)


def block_grads(query_heads, grad_heads, key_block, value_block, lse, delta, keep):
    key_heads = head_split(key_block)
    value_heads = head_split(value_block)
    score = (
        jnp.einsum("qhd,khd->hqk", query_heads, key_heads, preferred_element_type=jnp.float32)
        * SCALE
    )
    prob = jnp.where(keep[None], jnp.exp(score - lse[:, :, None]), 0.0)
    dvalue = jnp.einsum(
        "hqk,qhd->khd", prob.astype(jnp.bfloat16), grad_heads, preferred_element_type=jnp.float32
    )
    dprob = jnp.einsum("qhd,khd->hqk", grad_heads, value_heads, preferred_element_type=jnp.float32)
    dscore = (prob * (dprob - delta[:, :, None])).astype(jnp.bfloat16)
    dquery = (
        jnp.einsum("hqk,khd->qhd", dscore, key_heads, preferred_element_type=jnp.float32) * SCALE
    )
    dkey = (
        jnp.einsum("hqk,qhd->khd", dscore, query_heads, preferred_element_type=jnp.float32) * SCALE
    )
    return (dquery, dkey, dvalue)


def local(
    tokens,
    cotangent,
    block_table,
    norm1_gain,
    w_query,
    w_key,
    w_value,
    w_out,
    norm2_gain,
    w_gate,
    w_up,
    w_down,
):
    row_count = tokens.shape[1]
    width = tokens.shape[2]
    every_index = family_index(block_table[0])
    prompt_len = min(PROMPT_MAX, every_index.shape[0] // 2)
    own_index = lax.dynamic_slice_in_dim(
        every_index, lax.axis_index("ctx") * row_count, row_count, 0
    )
    gain1, wq_full, wk_full, wv_full, wo_full = (
        lax.all_gather(norm1_gain, "ctx", axis=0, tiled=True),
        lax.all_gather(w_query, "ctx", axis=0, tiled=True),
        lax.all_gather(w_key, "ctx", axis=0, tiled=True),
        lax.all_gather(w_value, "ctx", axis=0, tiled=True),
        lax.all_gather(w_out, "ctx", axis=0, tiled=True),
    )
    inputs = tokens[0].astype(jnp.float32)
    normed1, norm1_pull = jax.vjp(rms_scale, inputs, gain1.astype(jnp.float32))
    first_low = normed1.astype(jnp.bfloat16)
    queries = matmul(first_low, wq_full).astype(jnp.bfloat16)
    keys_own = matmul(first_low, wk_full).astype(jnp.bfloat16)
    values_own = matmul(first_low, wv_full).astype(jnp.bfloat16)
    keys_all, values_all = (
        lax.all_gather(keys_own, "ctx", axis=0, tiled=True),
        lax.all_gather(values_own, "ctx", axis=0, tiled=True),
    )
    lse = attend_stats(queries, keys_all, own_index, every_index, prompt_len)
    attended_wide = attend_values(
        queries, keys_all, values_all, lse, own_index, every_index, prompt_len
    )
    attended = attended_wide.astype(jnp.bfloat16)
    hidden = inputs + matmul(attended, wo_full)
    gain2, wg_full, wu_full, wd_full = (
        lax.all_gather(norm2_gain, "ctx", axis=0, tiled=True),
        lax.all_gather(w_gate, "ctx", axis=0, tiled=True),
        lax.all_gather(w_up, "ctx", axis=0, tiled=True),
        lax.all_gather(w_down, "ctx", axis=0, tiled=True),
    )
    normed2, norm2_pull = jax.vjp(rms_scale, hidden, gain2.astype(jnp.float32))
    second_low = normed2.astype(jnp.bfloat16)
    gate = matmul(second_low, wg_full)
    upper = matmul(second_low, wu_full)
    mixed_wide, gate_pull = jax.vjp(gated, gate, upper)
    mixed = mixed_wide.astype(jnp.bfloat16)
    result = hidden + matmul(mixed, wd_full)
    output = result.astype(jnp.bfloat16)[None]
    grad_low = cotangent[0]
    grad_down = inner(mixed, grad_low)
    dmixed = outer(grad_low, wd_full)
    dgate, dupper = gate_pull(dmixed)
    dgate_low = dgate.astype(jnp.bfloat16)
    dupper_low = dupper.astype(jnp.bfloat16)
    grad_gate = inner(second_low, dgate_low)
    grad_up = inner(second_low, dupper_low)
    dnormed2 = outer(dgate_low, wg_full) + outer(dupper_low, wu_full)
    dhidden_norm, grad_gain2 = norm2_pull(dnormed2)
    dhidden = grad_low.astype(jnp.float32) + dhidden_norm
    attn_low = dhidden.astype(jnp.bfloat16)
    grad_out_w = inner(attended, attn_low)
    dattended = outer(attn_low, wo_full).astype(jnp.bfloat16)
    delta = jnp.sum(
        (dattended.astype(jnp.float32) * attended_wide).reshape(row_count, HEADS, HEAD), axis=-1
    ).T
    query_heads = head_split(queries)
    grad_heads = head_split(dattended)

    def key_step(carry, number):
        start = number * KEYBLK
        key_block = lax.dynamic_slice_in_dim(keys_all, start, KEYBLK, 0)
        value_block = lax.dynamic_slice_in_dim(values_all, start, KEYBLK, 0)
        block_index = lax.dynamic_slice_in_dim(every_index, start, KEYBLK, 0)
        keep = allowed(own_index, block_index, prompt_len)
        dquery, dkey, dvalue = block_grads(
            query_heads, grad_heads, key_block, value_block, lse, delta, keep
        )
        joined = jnp.concatenate(
            [dkey.reshape(KEYBLK, width), dvalue.reshape(KEYBLK, width)], axis=1
        )
        return (carry + dquery, joined)

    start_query = jnp.zeros((row_count, HEADS, HEAD), jnp.float32)
    query_sum, key_terms = lax.scan(
        key_step, start_query, jnp.arange(every_index.shape[0] // KEYBLK)
    )
    summed = lax.psum_scatter(
        key_terms.reshape(every_index.shape[0], 2 * width).astype(jnp.bfloat16),
        "ctx",
        scatter_dimension=0,
        tiled=True,
    ).astype(jnp.float32)
    query_grad = query_sum.reshape(row_count, width)
    key_grad = summed[:, :width]
    value_grad = summed[:, width:]
    query_low = query_grad.astype(jnp.bfloat16)
    key_low = key_grad.astype(jnp.bfloat16)
    value_low = value_grad.astype(jnp.bfloat16)
    grad_query = inner(first_low, query_low)
    grad_key = inner(first_low, key_low)
    grad_value = inner(first_low, value_low)
    dnormed1 = outer(query_low, wq_full) + outer(key_low, wk_full) + outer(value_low, wv_full)
    dinput_norm, grad_gain1 = norm1_pull(dnormed1)
    tokens_grad = (dhidden + dinput_norm).astype(jnp.bfloat16)[None]
    shards = (
        lax.psum_scatter(
            grad_gain1.astype(jnp.bfloat16), "ctx", scatter_dimension=0, tiled=True
        ).astype(jnp.float32),
        lax.psum_scatter(
            grad_query.astype(jnp.bfloat16), "ctx", scatter_dimension=0, tiled=True
        ).astype(jnp.float32),
        lax.psum_scatter(
            grad_key.astype(jnp.bfloat16), "ctx", scatter_dimension=0, tiled=True
        ).astype(jnp.float32),
        lax.psum_scatter(
            grad_value.astype(jnp.bfloat16), "ctx", scatter_dimension=0, tiled=True
        ).astype(jnp.float32),
        lax.psum_scatter(
            grad_out_w.astype(jnp.bfloat16), "ctx", scatter_dimension=0, tiled=True
        ).astype(jnp.float32),
        lax.psum_scatter(
            grad_gain2.astype(jnp.bfloat16), "ctx", scatter_dimension=0, tiled=True
        ).astype(jnp.float32),
        lax.psum_scatter(
            grad_gate.astype(jnp.bfloat16), "ctx", scatter_dimension=0, tiled=True
        ).astype(jnp.float32),
        lax.psum_scatter(
            grad_up.astype(jnp.bfloat16), "ctx", scatter_dimension=0, tiled=True
        ).astype(jnp.float32),
        lax.psum_scatter(
            grad_down.astype(jnp.bfloat16), "ctx", scatter_dimension=0, tiled=True
        ).astype(jnp.float32),
    )
    shards = (
        lax.psum(shards[0].astype(jnp.bfloat16), "group").astype(jnp.float32),
        lax.psum(shards[1].astype(jnp.bfloat16), "group").astype(jnp.float32),
        lax.psum(shards[2].astype(jnp.bfloat16), "group").astype(jnp.float32),
        lax.psum(shards[3].astype(jnp.bfloat16), "group").astype(jnp.float32),
        lax.psum(shards[4].astype(jnp.bfloat16), "group").astype(jnp.float32),
        lax.psum(shards[5].astype(jnp.bfloat16), "group").astype(jnp.float32),
        lax.psum(shards[6].astype(jnp.bfloat16), "group").astype(jnp.float32),
        lax.psum(shards[7].astype(jnp.bfloat16), "group").astype(jnp.float32),
        lax.psum(shards[8].astype(jnp.bfloat16), "group").astype(jnp.float32),
    )
    return (
        output,
        tokens_grad,
        shards[0],
        shards[1],
        shards[2],
        shards[3],
        shards[4],
        shards[5],
        shards[6],
        shards[7],
        shards[8],
    )


PLANE = 4
CORES = 2
TP = ("group", "core")
F32 = jnp.float32
BF16 = jnp.bfloat16


def dot_nt(left, right):
    return lax.dot_general(left, right, (((1,), (1,)), ((), ())), preferred_element_type=F32)


def head_mask(rows, head):
    lane = lax.broadcasted_iota(jnp.int32, (rows, 2 * HEAD), 1)
    return (lane >= head * HEAD) & (lane < (head + 1) * HEAD)


def causal_mask():
    key = lax.broadcasted_iota(jnp.int32, (CONT, CONT), 0)
    query = lax.broadcasted_iota(jnp.int32, (CONT, CONT), 1)
    return key <= query


MESH = pl.DeviceIdType.MESH
EARLY = 256
FRONT_SEMS = (126, 137)
REAR_SEMS = (114, 104)


def spots():
    chip, line, core = lax.axis_index("group"), lax.axis_index("z"), lax.axis_index("core")
    side = chip + 1 - 2 * lax.rem(chip, 2)
    over = lax.rem(chip + 2, PLANE)
    far = PLANE - 1 - chip
    return chip, line, core, side, over, far


def plane_partners():
    chip, line, core, side, over, far = spots()
    return [(q, line, core) for q in (far, side, over)]


def line_partners():
    chip, line, core, side, over, far = spots()
    lines = [lax.rem(line + d, PLANE) for d in range(1, PLANE)]
    same = [(chip, z, core) for z in lines]
    return same + [(chip, z, 1 - core) for z in lines] + [(chip, line, 1 - core)]


class Kept:
    def __init__(self, copies, copy, held):
        self.copies, self.copy, self.held = copies, copy, held
        copy.start()

    def wait(self):
        self.copy.wait()
        self.copies.root().free.extend(self.held)


class Copies:
    def __init__(self, sems, parent=None):
        self.sems, self.parent = sems, parent
        self.counts, self.free, self.started, self.branches = [0, 0], [], [], []

    def branch(self):
        self.branches.append(Copies(self.sems, self))
        return self.branches[-1]

    def number(self, side=0):
        if self.parent is not None:
            return self.parent.number(side)
        self.counts[side] += 1
        return self.counts[side] - 1

    def root(self):
        return self if self.parent is None else self.parent.root()

    def left(self, held=None):
        free = self.root().free
        number = free.pop() if held is not None and free else self.number(0)
        if held is not None:
            held.append(number)
        return self.sems[0].at[number]

    def greet(self, crossing=False):
        barrier = pltpu.get_barrier_semaphore()
        partners = plane_partners() + line_partners()
        chip, line, core, side, over, far = spots()
        if crossing:
            partners += [(line, lax.rem(line + d, PLANE), core) for d in range(1, PLANE)]
            partners += [(lax.rem(chip + d, PLANE), chip, core) for d in range(1, PLANE)]

        def signal(partner):
            pl.semaphore_signal(barrier, inc=1, device_id=partner, device_id_type=MESH)

        for partner in partners:
            signal(partner)
        if crossing:
            @pl.when(chip != line)
            def _():
                signal((line, line, core))
                signal((chip, chip, core))

        self.crossing, self.expected = crossing, len(partners)

    def welcome(self):
        barrier = pltpu.get_barrier_semaphore()
        if not self.crossing:
            pl.semaphore_wait(barrier, self.expected)
            return
        away = lax.axis_index("group") != lax.axis_index("z")

        @pl.when(away)
        def _():
            pl.semaphore_wait(barrier, self.expected + 2)

        @pl.when(jnp.logical_not(away))
        def _():
            pl.semaphore_wait(barrier, self.expected)

    def send(self, source, target, partner, start=True):
        held = []
        copy = pltpu.make_async_remote_copy(
            src_ref=source,
            dst_ref=target,
            send_sem=self.left(held),
            recv_sem=self.sems[1].at[self.number(1)],
            device_id=partner,
            device_id_type=MESH,
        )
        if start:
            copy.start()
        self.started.append((copy, held))
        return copy

    def keep(self, source, target):
        held = []
        return Kept(self, pltpu.make_async_copy(source, target, self.left(held)), held)

    def finish(self):
        for copy, held in self.started:
            copy.wait_send()
            self.root().free.extend(held)
        self.started = []
        for branch in self.branches:
            branch.finish()


def arrived(copies):
    for copy in copies:
        copy.wait_recv()


def finished(copies):
    for copy in copies:
        copy.wait()


def gather_stream(copies, own_ref, out_ref, twin=True):
    chip, line, core, side, over, far = spots()
    half = own_ref.shape[0] // 2
    to_far, to_side, to_over = plane_partners()
    to_twin = (chip, line, 1 - core)

    def slot_of(q):
        return CORES * q + core if twin else q

    def part(slot, number):
        return out_ref.at[slot, pl.ds(number * half, half)]

    def own(number):
        return own_ref.at[pl.ds(number * half, half)]

    def on(slot, number, partner):
        return copies.send(part(slot, number), part(slot, number), partner)

    def share(slot, number):
        return [on(slot, number, to_twin)] if twin else []

    mine, slot_side, slot_over, slot_far = map(slot_of, (chip, side, over, far))
    sides, overs = [None, None], [None, None]
    overs[0] = copies.send(own(0), part(mine, 0), to_over)
    sides[1] = copies.send(own(1), part(mine, 1), to_side)
    sides[0] = copies.send(own(0), part(mine, 0), to_side)
    overs[1] = copies.send(own(1), part(mine, 1), to_over)
    twins = [copies.send(own(h), part(mine, h), to_twin) for h in range(2)] if twin else []
    local = copies.keep(own_ref, out_ref.at[mine])
    yield
    local.wait()
    arrived(twins)
    yield
    overs[0].wait_recv()
    far0 = on(slot_over, 0, to_side)
    twins = share(slot_over, 0)
    sides[1].wait_recv()
    far1 = on(slot_side, 1, to_over)
    twins += share(slot_side, 1)
    yield
    arrived(twins)
    yield
    sides[0].wait_recv()
    twins = share(slot_side, 0)
    overs[1].wait_recv()
    twins += share(slot_over, 1)
    yield
    arrived(twins)
    yield
    twins = [
        copies.send(part(slot_far, h), part(slot_far, h), to_twin, start=False)
        for h in range(2 if twin else 0)
    ]

    def pass_on():
        for number, copy in enumerate((far0, far1)):
            copy.wait_recv()
            if twin:
                twins[number].start()

    yield pass_on
    arrived(twins)
    yield


class Scatter:
    def __init__(self, copies, part_ref, out_ref, scratch):
        self.copies, self.part_ref, self.out_ref = copies, part_ref, out_ref
        self.twin, self.from_side, self.from_over, self.go = scratch
        chip, line, self.core, side, over, far = spots()
        self.half = out_ref.shape[0] // 2
        ignored, self.to_side, self.to_over = plane_partners()
        self.to_twin = (chip, line, 1 - self.core)
        self.chips = (far, side, over, chip)
        self.twins = [None] * 4

    def share(self, *numbers, start=True):
        for n in numbers:
            self.twins[n] = []
            for h in range(2):
                rows = pl.ds(h * self.half, self.half)
                source = self.part_ref.at[CORES * self.chips[n] + 1 - self.core, rows]
                self.twins[n].append(self.copies.send(source, self.twin.at[n, rows], self.to_twin, start))

    def share_between(self, n, slot_of, body):
        self.share(n, start=False)

        @pl.loop(0, CORES)
        def _(number):
            @pl.when(number == 1)
            def _():
                for copy in self.twins[n]:
                    copy.start()

            body(slot_of(number))

    def _pair(self, n, h):
        part = slice(h * self.half, (h + 1) * self.half)
        self.twins[n][h].wait_recv()
        own = self.part_ref[CORES * self.chips[n] + self.core, part]
        return own.astype(F32) + self.twin[n, part].astype(F32)

    def _send(self, n, h, value, target, partner):
        self.go[n, h * self.half : (h + 1) * self.half] = value.astype(BF16)
        return self.copies.send(self.go.at[n, pl.ds(h * self.half, self.half)], target, partner)

    def far(self):
        self.far0 = self._send(0, 0, self._pair(0, 0), self.from_side.at[0], self.to_side)
        self.far1 = self._send(0, 1, self._pair(0, 1), self.from_over.at[0], self.to_over)

    def side(self):
        self.side0 = self._send(1, 0, self._pair(1, 0), self.from_side.at[1], self.to_side)

    def over(self):
        self.over1 = self._send(2, 1, self._pair(2, 1), self.from_over.at[2], self.to_over)

    def cross(self):
        value = self._pair(2, 0)
        self.far0.wait_recv()
        value = value + self.from_side[0].astype(F32)
        self.over0 = self._send(2, 0, value, self.from_over.at[1], self.to_over)
        value = self._pair(1, 1)
        self.far1.wait_recv()
        value = value + self.from_over[0].astype(F32)
        self.side1 = self._send(1, 1, value, self.from_side.at[2], self.to_side)

    def end(self):
        first, second = self._pair(3, 0), self._pair(3, 1)
        self.side0.wait_recv()
        first = first + self.from_side[1].astype(F32)
        self.over1.wait_recv()
        second = second + self.from_over[2].astype(F32)
        self.over0.wait_recv()
        self.out_ref[0 : self.half] = first + self.from_over[1].astype(F32)
        self.side1.wait_recv()
        self.out_ref[self.half :] = second + self.from_side[2].astype(F32)


def drain(gather):
    for step in gather:
        if step is not None:
            step()


def scatter_scratch(rows, width):
    return [
        pltpu.VMEM((PLANE, rows, width), BF16),
        pltpu.VMEM((3, rows // 2, width), BF16),
        pltpu.VMEM((3, rows // 2, width), BF16),
        pltpu.VMEM((3, rows, width), BF16),
    ]


def inward_stream(copies, own_ref, mid, out_ref):
    chip, line, core, side, over, far = spots()
    chunk = own_ref.shape[0] // PLANE
    half = chunk // 2
    sent, moved, local = [[], []], [], []
    for h in range(2):
        part = pl.ds(h * half, half)
        for q in plane_partners():
            rows = own_ref.at[pl.ds(q[0] * chunk + h * half, half)]
            sent[h].append(copies.send(rows, mid.at[chip, part], q))
    local = [copies.keep(own_ref.at[pl.ds(chip * chunk, chunk)], mid.at[chip])]
    yield
    finished(local)
    for h in range(2):
        part = pl.ds(h * half, half)
        arrived(sent[h])
        for q in line_partners()[: PLANE - 1]:
            moved.append(copies.send(mid.at[q[1], part], out_ref.at[line, part], q))
    local = copies.keep(mid.at[line], out_ref.at[line])
    yield
    arrived(moved)
    local.wait()
    yield


class Outward:
    def __init__(self, copies, own_ref, out_ref):
        self.chip, self.line, self.core = (lax.axis_index(name) for name in ("group", "z", "core"))
        self.copies, self.chunk, self.out_ref = copies, own_ref.shape[1], out_ref
        self.arrive = [copies.number(1) for ignored in range(PLANE)]
        self.sends, self.away = [], self.chip != self.line
        for d in range(PLANE):
            z = lax.rem(self.line + d, PLANE)
            copy = self._copy(own_ref.at[z], self.chip, z, copies.left())
            self.sends.append(copy)
            if d:
                copy.start()
        self.local = pltpu.make_async_copy(
            own_ref.at[self.line], self._rows(self.chip), copies.left()
        )

        @pl.when(self.away)
        def _():
            self.sends[0].start()

        @pl.when(self.chip == self.line)
        def _():
            self.local.start()

    def _rows(self, chip):
        return self.out_ref.at[pl.ds(pl.multiple_of(chip * self.chunk, self.chunk), self.chunk)]

    def _copy(self, source, chip, z, left):
        return pltpu.make_async_remote_copy(
            src_ref=source,
            dst_ref=self._rows(chip),
            send_sem=left,
            recv_sem=self.copies.sems[1].at[self.arrive[0] + chip],
            device_id=(self.line, z, self.core),
            device_id_type=MESH,
        )

    def wait(self):
        for chip in range(PLANE):
            copy = self._copy(self._rows(chip), chip, self.line, self.copies.sems[0].at[0])

            @pl.when((chip != self.chip) | self.away)
            def _():
                copy.wait_recv()

        @pl.when(self.chip == self.line)
        def _():
            self.local.wait()

        @pl.when(self.away)
        def _():
            self.sends[0].wait_send()

        for copy in self.sends[1:]:
            copy.wait_send()


def columns_stream(copies, piece_ref, out_ref, lanes):
    chip, line, core, side, over, far = spots()
    mine = out_ref.at[CORES * line + core, :, lanes]
    sent = [copies.send(piece_ref.at[q[2], :, lanes], mine, q) for q in line_partners()]
    local = copies.keep(piece_ref.at[core, :, lanes], mine)
    yield
    arrived(sent)
    local.wait()
    yield


class Relay:
    def __init__(self, copies, piece, slot, both=True):
        self.line, self.core = lax.axis_index("z"), lax.axis_index("core")
        self.copies, self.slot, self.both = copies, slot, both
        self.cores = range(CORES) if both else (self.core,)
        self.twin = None
        count = PLANE * CORES if both else PLANE
        self.arrive = [copies.number(1) for ignored in range(count)]
        self.sends = []
        mine = slot(self.line, self.core)
        if both:
            self.twin = self._copy(piece(1 - self.core), mine, self.line, self.core, self.line, 1 - self.core, copies.left())
            self.twin.start()
        self.local = copies.keep(piece(self.core), mine)
        for step in (1, -1):
            for core in self.cores:
                copy = self._copy(piece(core), mine, self.line, self.core, self.line + step, core, copies.left())
                self._start(self._inside(self.line + step), copy)

    def _inside(self, z):
        return (z >= 0) & (z < PLANE)

    def _sem(self, z, core):
        number = CORES * z + core if self.both else z
        return self.copies.sems[1].at[self.arrive[0] + number]

    def _copy(self, source, target, z, core, to, to_core, left=None):
        return pltpu.make_async_remote_copy(
            src_ref=source,
            dst_ref=target,
            send_sem=self.copies.sems[0].at[0] if left is None else left,
            recv_sem=self._sem(z, core),
            device_id=(lax.axis_index("group"), to, to_core),
            device_id_type=MESH,
        )

    def _start(self, when, copy):
        @pl.when(when)
        def _():
            copy.start()

        self.sends.append((when, copy))

    def hop(self, distance):
        if distance == 1:
            self.local.wait()
            if self.both:
                self._copy(*[self.slot(self.line, 1 - self.core)] * 2, self.line, 1 - self.core, self.line, self.core).wait_recv()
        for step in (1, -1):
            z = self.line - step * distance
            there, on = self._inside(z), self._inside(z) & self._inside(self.line + step)
            for core in self.cores:
                slot = self.slot(jnp.clip(z, 0, PLANE - 1), core)
                left = self.copies.left() if distance < PLANE - 1 else None
                copy = self._copy(slot, slot, jnp.clip(z, 0, PLANE - 1), core, self.line + step, self.core, left)

                @pl.when(there)
                def _():
                    copy.wait_recv()

                if distance < PLANE - 1:
                    self._start(on, copy)

    def finish(self):
        if self.both:
            self.twin.wait_send()
        for when, copy in self.sends:
            @pl.when(when)
            def _():
                copy.wait_send()


def columns_relay(copies, piece_ref, out_ref, lanes):
    return Relay(
        copies,
        lambda core: piece_ref.at[core, :, lanes],
        lambda z, core: out_ref.at[CORES * z + core, :, lanes],
    )


def sum_stream(copies, grad_ref, recv, sum_ref):
    chip, line, core, side, over, far = spots()
    sent = [
        copies.send(grad_ref.at[q[1]], recv.at[line], q) for q in line_partners()[: PLANE - 1]
    ]
    local = copies.keep(grad_ref.at[line], recv.at[line])
    yield
    arrived(sent)
    local.wait()
    total = recv[0].astype(F32)
    for family in range(1, PLANE):
        total = total + recv[family].astype(F32)
    sum_ref[...] = total.astype(BF16)
    yield


def quarter_columns(ref, number):
    width = ref.shape[1] // PLANE
    return ref.at[:, pl.ds(pl.multiple_of(number * width, width), width)]


def to_ranks_stream(copies, mid, out_ref):
    chip, line, core, side, over, far = spots()
    target = quarter_columns(out_ref, chip)
    sent = [copies.send(mid.at[q[0]], target, q) for q in plane_partners()]
    local = copies.keep(mid.at[chip], target)
    yield
    arrived(sent)
    local.wait()
    yield


def unit_rows(value):
    inverse = lax.rsqrt(jnp.mean(value * value, axis=-1, keepdims=True) + EPS)
    return value * inverse, inverse


def comm_call(kernel, name, number, out_shape, in_specs, out_specs, scratch, sends, arrivals, vmem_mib=60):
    return pl.pallas_call(
        kernel,
        out_shape=out_shape,
        in_specs=in_specs,
        out_specs=out_specs,
        scratch_shapes=scratch + [pltpu.SemaphoreType.DMA((sends,)), pltpu.SemaphoreType.DMA((arrivals,))],
        compiler_params=pltpu.CompilerParams(
            collective_id=number, has_side_effects=True, vmem_limit_bytes=vmem_mib << 20
        ),
        name=name,
    )


ANY = pl.BlockSpec(memory_space=pl.ANY)
IN_VMEM = pl.BlockSpec(memory_space=pltpu.VMEM)


def gains_of(line_ref, row):
    return jnp.concatenate([line_ref[s, row : row + 1, :] for s in range(line_ref.shape[0])], axis=1)


def column_grads_stream(copies, grad_ref, recv, sum_ref, lanes):
    chip, line, core, side, over, far = spots()
    sent = [
        copies.send(grad_ref.at[CORES * q[1] + q[2], :, lanes], recv.at[core, line], q)
        for q in line_partners()
    ]
    local = copies.keep(grad_ref.at[CORES * line + core, :, lanes], recv.at[core, line])
    yield
    arrived(sent)
    local.wait()
    for number in range(CORES):
        total = recv[number, 0].astype(F32)
        for family in range(1, PLANE):
            total = total + recv[number, family].astype(F32)
        sum_ref[number, :, lanes] = total.astype(BF16)
    yield


def row_grads_stream(copies, grad_ref, mid, recv, summed, out_ref):
    chip, line, core, side, over, far = spots()
    width = out_ref.shape[1] // PLANE

    def quarter(q):
        return pl.ds(pl.multiple_of(q * width, width), width)

    sent = [copies.send(grad_ref.at[:, quarter(q[0])], mid.at[chip], q) for q in plane_partners()]
    local = copies.keep(grad_ref.at[:, quarter(chip)], mid.at[chip])
    yield
    local.wait()
    arrived(sent)
    sent = [copies.send(mid.at[q[1]], recv.at[line], q) for q in line_partners()[: PLANE - 1]]
    local = copies.keep(mid.at[line], recv.at[line])
    yield
    arrived(sent)
    local.wait()
    total = recv[0].astype(F32)
    for family in range(1, PLANE):
        total = total + recv[family].astype(F32)
    summed[...] = total.astype(BF16)
    sent = [copies.send(summed, out_ref.at[:, quarter(chip)], q) for q in plane_partners()]
    local = copies.keep(summed, out_ref.at[:, quarter(chip)])
    yield
    arrived(sent)
    local.wait()
    yield


def gain_grads_stream(copies, own, recv, summed, plane, out_ref):
    chip, line, core, side, over, far = spots()
    mine = CORES * line + core
    sent = [copies.send(own.at[CORES * q[1] + q[2]], recv.at[mine], q) for q in line_partners()]
    local = copies.keep(own.at[mine], recv.at[mine])
    yield
    arrived(sent)
    local.wait()
    summed[...] = jnp.sum(recv[...], axis=0)
    sent = [copies.send(summed, plane.at[chip], q) for q in plane_partners()]
    local = copies.keep(summed, plane.at[chip])
    yield
    arrived(sent)
    local.wait()
    out_ref[...] = jnp.sum(plane[...], axis=0)
    yield


def norm_back(grad, value, gain):
    unit, inverse = unit_rows(value)
    scaled = grad * gain
    back = inverse * (scaled - unit * jnp.mean(scaled * unit, axis=-1, keepdims=True))
    return back, jnp.sum(grad * unit, axis=0, keepdims=True)


TABLE_ROW = 2


def chunk_row(stored, part, chunk):
    plane, core, line = 2 * (stored % 2) + part, (stored // 2) % 2, stored // 4
    return ((plane * CORES + core) * PLANE + line) * chunk


def chosen(blocks, flags):
    value = blocks[0]
    for block, flag in zip(blocks[1:], flags[1:]):
        value = jnp.where(flag, block, value)
    return value


def in_place_order(table_ref, source, lanes, target, scale=None):
    chunk = BLK // 2
    blocks = source.shape[0] // BLK
    for place in range(blocks):
        flags = [table_ref[TABLE_ROW, stored] == float(place) for stored in range(blocks)]
        for part in range(2):
            rows = [chunk_row(stored, part, chunk) for stored in range(blocks)]
            block = chosen([source[row : row + chunk, lanes] for row in rows], flags)
            row = place * BLK + part * chunk
            target[row : row + chunk, :] = block if scale is None else block * scale


def in_gathered_order(table_ref, source, target, lanes):
    chunk = BLK // 2
    blocks = source.shape[0] // BLK
    for stored in range(blocks):
        flags = [table_ref[TABLE_ROW, stored] == float(place) for place in range(blocks)]
        for part in range(2):
            rows = [place * BLK + part * chunk for place in range(blocks)]
            block = chosen([source[row : row + chunk, :] for row in rows], flags)
            row = chunk_row(stored, part, chunk)
            target[row : row + chunk, lanes] = block


def attend_block(number, prompt, qs, ks, vt, att, ot_ref, lse_ref):
    start = number * CONT
    before = min(start, prompt)
    own_rows = slice(start, start + CONT)
    query = qs[own_rows, :]
    outs = []
    for head in range(2):
        masked = jnp.where(head_mask(CONT, head), query, jnp.zeros_like(query))
        own = dot_nt(ks[own_rows, :], masked)
        own = jnp.where(causal_mask(), own, -1e30)
        best = jnp.max(own, axis=0, keepdims=True)
        if before:
            past = dot_nt(ks[0:before, :], masked)
            best = jnp.maximum(best, jnp.max(past, axis=0, keepdims=True))
        terms = jnp.exp(own - best)
        total_terms = jnp.sum(terms, axis=0, keepdims=True)
        rows = slice(head * HEAD, (head + 1) * HEAD)
        out = matmul(vt[rows, own_rows], terms.astype(BF16))
        if before:
            terms = jnp.exp(past - best)
            total_terms = total_terms + jnp.sum(terms, axis=0, keepdims=True)
            out = out + matmul(vt[rows, 0:before], terms.astype(BF16))
        outs.append(out / total_terms)
        lse_ref[head : head + 1, own_rows] = best + jnp.log(total_terms)
    joined = jnp.concatenate(outs, axis=0)
    ot_ref[:, own_rows] = joined.astype(BF16)
    att[own_rows, :] = joined.T.astype(BF16)


def chip_slots(group):
    chip, line, core, side, over, far = spots()
    if group == "near":
        return 2 * CORES, lambda n: CORES * (side + lax.div(n, CORES) * (over - side)) + lax.rem(n, CORES)
    q = {"own": chip, "far": far}[group]
    return CORES, lambda n: CORES * q + lax.rem(core + 1 + n, CORES)


def each_slot(group, body):
    count, slot_of = chip_slots(group)

    @pl.loop(0, count)
    def _(n):
        body(slot_of(n))


def front_kernel(
    tok_ref, cot_ref, gain1_ref, gain2_ref, place_ref, wq_ref, wk_ref, wv_ref, wo_ref, wg_ref, wu_ref, wd_ref,
    n1_out, x_out, cot_out, line_out, wqkv_out, wo_out, q_out, k_out, v_out, ot_out, lse_out, att_out,
    h1_out, dn2_out, mix_out, ggu_out, gd_out, gusum_out, table_out,
    *rest,
):
    scratch, other, rest = rest[:4], rest[4:8], rest[8:]
    x_ref, cotp_ref, line_ref, wqkv, wout, qs, ks, vs, ot_ref, lse_ref, att_ref, rest = *rest[:11], rest[11:]
    h1_ref, dn2_ref, ggu_ref, gd_ref, gusum, rest = *rest[:5], rest[5:]
    small_ref, recv_gu, rest = *rest[:2], rest[2:]
    mid_x, mid_c, mid_o, down, tables, table, pieces, gate_w, up_w, gu, normed, rest = *rest[:11], rest[11:]
    n1s, n2s, cots, qkv, vt, att, parts, summed, wgu, wgu_t, wd, wd_t, us, dabs, *sems = rest
    copies = Copies(sems)
    chip, line, core, side, over, far = spots()
    total, heads = qkv.shape[0], wo_ref.shape[0]
    hidden, lanes = wd_ref.shape[0], wd.shape[0]
    chunk, width = x_ref.shape[1], x_ref.shape[2]
    rows = PLANE * chunk
    ranks = PLANE * CORES
    share = hidden // PLANE
    stores = []

    def store(source, target):
        stores.append(copies.keep(source, target))

    loads = [copies.keep(wg_ref, gate_w), copies.keep(wu_ref, up_w)]
    for c in range(CORES):
        column = pl.ds(pl.multiple_of((CORES * chip + c) * heads, heads), heads)
        for n, w in enumerate((wq_ref, wk_ref, wv_ref)):
            loads.append(copies.keep(w.at[:, column], pieces.at[c, :, n * heads : (n + 1) * heads]))
    copies.greet()
    small_ref[...] = jnp.zeros_like(small_ref)
    small_ref[0:1] = gain1_ref[...].astype(F32)
    small_ref[1:2] = gain2_ref[...].astype(F32)
    small_ref[TABLE_ROW : TABLE_ROW + 1, 0 : place_ref.shape[1]] = place_ref[...].astype(F32)
    copies.welcome()
    early = copies.branch()
    tokens = inward_stream(early, tok_ref, mid_x, x_ref)
    next(tokens)
    out_part = quarter_columns(wo_ref, chip)
    out_sent = [early.send(out_part, mid_o.at[line], q) for q in line_partners()[: PLANE - 1]]
    out_kept = copies.keep(out_part, mid_o.at[line])
    mine = CORES * line + core
    small = [early.send(small_ref, line_ref.at[mine], q) for q in line_partners()]
    small += [early.send(small_ref, tables.at[chip], q) for q in plane_partners()]
    local = [copies.keep(small_ref, line_ref.at[mine]), copies.keep(small_ref, tables.at[chip])]
    finished(loads)
    next(tokens)
    cotangents = inward_stream(early, cot_ref, mid_c, cotp_ref)
    next(cotangents)
    gu[...] = jnp.zeros_like(gu)
    for k in range(PLANE):
        @pl.when(chip == k)
        def _():
            for c in range(CORES):
                for z in range(PLANE):
                    begin, at = (CORES * z + c) * hidden + k * share, z * share
                    gu[c, :, at : at + share] = gate_w[:, begin : begin + share]
                    gu[c, :, lanes + at : lanes + at + share] = up_w[:, begin : begin + share]
    wd[hidden:lanes] = jnp.zeros((lanes - hidden, width), BF16)
    arrived(out_sent)
    out_kept.wait()
    out_rows = to_ranks_stream(early, mid_o, wout)
    next(out_rows)
    arrived(small)
    finished(local)
    load = [copies.keep(tables.at[line], table), copies.keep(tables.at[line], table_out)]
    store(line_ref, line_out)
    gain = gains_of(line_ref, 0)
    next(tokens)
    projections = columns_relay(copies, pieces, wqkv, pl.ds(0, 3 * heads))
    for n in range(PLANE):
        unit, ignored = unit_rows(x_ref[n].astype(F32))
        normed[n * chunk : (n + 1) * chunk] = (unit * gain).astype(BF16)
    gathering = copies.branch()
    gather = gather_stream(gathering, normed, n1s)
    next(gather)
    finished(load)
    next(gather)
    projections.hop(1)
    next(gather)
    projections.hop(2)
    next(gather)
    next(gather)
    next(cotangents)

    def slot_rows(slot):
        return pl.ds(pl.multiple_of(slot * rows, rows), rows)

    def project(slot):
        qkv[slot_rows(slot), :] = matmul(n1s[slot], wqkv[...].reshape(width, 3 * heads)).astype(BF16)

    next(gather)
    projections.hop(3)
    next(gather)()
    each_slot("own", project)
    each_slot("near", project)
    next(gather)
    each_slot("far", project)
    for source, target in ((n1s, n1_out), (x_ref, x_out), (wqkv, wqkv_out)):
        store(source, target)

    for n, ref in enumerate((qs, ks, vs)):
        scale = jnp.bfloat16(SCALE) if n == 0 else None
        in_place_order(table, qkv, slice(n * heads, (n + 1) * heads), ref, scale)
    next(cotangents)
    gather_cot = gather_stream(copies, cotp_ref.reshape(rows, width), cots)
    next(gather_cot)
    gate_up = columns_relay(copies, gu, wgu, pl.ds(0, 2 * lanes))
    down_part = wd_ref.at[pl.ds(pl.multiple_of(chip * share, 8), share)]
    down_rows = Relay(copies, lambda core: down_part, lambda z, core: down.at[z], False)
    for start in range(0, total, CONT):
        part = slice(start, start + CONT)
        vt[:, part] = vs[part, :].astype(F32).T.astype(BF16)
    for source, target in ((qs, q_out), (ks, k_out), (vs, v_out), (cotp_ref, cot_out)):
        store(source, target)
    for number in range(total // CONT):
        attend_block(number, total // 2, qs, ks, vt, att, ot_ref, lse_ref)
        if number == 5:
            next(gather_cot)
            next(gather_cot)
            next(gather_cot)
            gate_up.hop(1)
    in_gathered_order(table, att, att_ref, slice(0, heads))
    next(out_rows)

    def spread(slot):
        parts[slot] = matmul(att_ref[slot_rows(slot), :], wout[...]).astype(BF16)

    scattering = copies.branch()
    scatter = Scatter(scattering, parts, summed, scratch)
    each_slot("far", spread)
    scatter.share(0)
    each_slot("near", spread)
    scatter.share(1, 2)
    scatter.far()
    each_slot("own", spread)
    scatter.share(3)
    scatter.side()
    scatter.over()
    next(gather_cot)
    down_rows.hop(1)
    next(gather_cot)
    next(gather_cot)()
    gate_up.hop(2)
    down_rows.hop(2)
    for source, target in ((wout, wo_out), (ot_ref, ot_out), (lse_ref, lse_out), (att_ref, att_out)):
        store(source, target)
    scatter.cross()
    next(gather_cot)
    gate_up.hop(3)
    for s in range(ranks):
        wgu_t[:, s * heads : (s + 1) * heads] = wgu[s].T
    down_rows.hop(3)
    for z in range(PLANE):
        wd[z * share : (z + 1) * share] = down[z]
    wd_t[...] = wd[...].T
    early.finish()
    gathering.finish()
    gain = gains_of(line_ref, 1)
    scatter.end()
    for n in range(PLANE):
        part = slice(n * chunk, (n + 1) * chunk)
        hidden_rows = x_ref[n].astype(F32) + summed[part]
        h1_ref[part] = hidden_rows
        unit, ignored = unit_rows(hidden_rows)
        normed[part] = (unit * gain).astype(BF16)
    gather = gather_stream(copies, normed, n2s)
    next(gather)
    store(h1_ref, h1_out)
    next(gather)
    scattering.finish()
    finished(stores)
    stores.clear()

    def feed_rows(slot, at):
        block, cot = n2s[slot, at, :], cots[slot, at, :]
        both = matmul(block, wgu[...].reshape(width, 2 * lanes))
        gate, upper = both[:, :lanes], both[:, lanes:]
        bend = jnp.tanh(0.7978845608028654 * (gate + 0.044715 * gate * gate * gate))
        half = 0.5 * (1.0 + bend)
        active = gate * half
        slope = half + (0.5 * 0.7978845608028654) * gate * (1.0 - bend * bend) * (
            1.0 + 3 * 0.044715 * gate * gate
        )
        mixed = (active * upper).astype(BF16)
        us[slot, at, :] = mixed
        parts[slot, at, :] = matmul(mixed, wd[...]).astype(BF16)
        du = matmul(cot, wd_t[...])
        dabs[slot, at, 0:lanes] = (du * upper * slope).astype(BF16)
        dabs[slot, at, lanes:] = (du * active).astype(BF16)
        n1s[slot, at, :] = matmul(dabs[slot, at, :], wgu_t[...]).astype(BF16)

    def feed(slot):
        feed_rows(slot, pl.ds(0, rows))

    def feed_halves(which, between):
        count, slot_of = chip_slots("near")
        half = rows // 2

        @pl.loop(0, count)
        def _(n):
            @pl.when(n == count - 1)
            def _():
                between()

            number = 1 - lax.div(n, CORES) if which == 0 else lax.div(n, CORES)
            feed_rows(slot_of(n), pl.ds(pl.multiple_of(number * half, half), half))

    scatter = Scatter(copies, n1s, dn2_ref, other)
    each_slot("own", feed)
    scatter.share(3)
    next(gather)
    next(gather)
    feed_halves(0, lambda: None)
    next(gather)
    next(gather)
    feed_halves(1, next(gather))
    scatter.share(1, 2)
    next(gather)
    scatter.side()
    scatter.over()
    scatter.share_between(0, chip_slots("far")[1], feed)
    scatter.far()
    store(parts, mix_out)

    def by_rows(s):
        columns = pl.ds(pl.multiple_of(s * heads, heads), heads)
        grad = jnp.zeros((heads, 2 * lanes), F32)
        for slot in range(ranks):
            grad = grad + inner(n2s[slot, :, columns], dabs[slot])
        ggu_ref[s] = grad.astype(BF16)

    pl.loop(0, ranks)(by_rows)
    columns = column_grads_stream(copies, ggu_ref, recv_gu, gusum, pl.ds(0, EARLY))
    next(columns)
    store(ggu_ref, ggu_out)
    scatter.cross()
    grad = jnp.zeros((lanes, width), F32)
    for slot in range(ranks):
        grad = grad + inner(us[slot], cots[slot])
    for z in range(PLANE):
        for h in range(2):
            block = grad[z * share : (z + 1) * share, h * (width // 2) : (h + 1) * (width // 2)]
            gd_ref[z, h] = block.astype(BF16)
    store(gd_ref, gd_out)
    scatter.end()
    store(dn2_ref, dn2_out)
    next(columns)
    store(gusum, gusum_out)
    for relay in (projections, gate_up, down_rows):
        relay.finish()
    copies.finish()
    finished(stores)


def front(tokens, cotangent, gain1, gain2, places, w_query, w_key, w_value, w_out, w_gate, w_up, w_down):
    rows, width = tokens.shape
    heads, hidden = w_out.shape[0], w_down.shape[0]
    lanes = -(-hidden // 128) * 128
    ranks = PLANE * CORES
    total = ranks * rows
    small = (8, heads)
    chunks, blocks = (PLANE, rows // PLANE, width), (ranks, rows, width)
    low = lambda *shape: jax.ShapeDtypeStruct(shape, BF16)
    wide = lambda *shape: jax.ShapeDtypeStruct(shape, F32)
    held = [
        low(*chunks), low(*chunks), wide(ranks, *small), low(ranks, heads, 3 * heads),
        low(heads, width), low(total, heads), low(total, heads), low(total, heads), low(heads, total),
        wide(2, total), low(total, heads), wide(rows, width), wide(rows, width),
    ]
    grads = [low(ranks, heads, 2 * lanes), low(PLANE, 2, hidden // PLANE, width // 2), low(CORES, heads, EARLY)]
    shapes = [low(*blocks)] + held + [low(*blocks)] + grads + [wide(*small)]
    scratch = scatter_scratch(rows, width) * 2
    scratch += [pltpu.VMEM(a.shape, a.dtype) for a in held + grads]
    held = lambda *shape: pltpu.VMEM(shape, BF16)
    scratch += [pltpu.VMEM(small, F32), held(CORES, PLANE, heads, EARLY)]
    scratch += [held(*chunks), held(*chunks), held(PLANE, heads, width // PLANE), held(PLANE, hidden // PLANE, width)]
    scratch += [pltpu.VMEM((PLANE,) + small, F32), pltpu.SMEM(small, F32)]
    scratch += [held(CORES, heads, 3 * heads), held(*w_gate.shape), held(*w_up.shape), held(CORES, heads, 2 * lanes)]
    scratch += [held(rows, width), held(*blocks), held(*blocks), held(*blocks), held(total, 3 * heads)]
    scratch += [held(heads, total), held(total, heads), held(*blocks), pltpu.VMEM((rows, width), F32)]
    scratch += [held(ranks, heads, 2 * lanes), held(2 * lanes, width), held(lanes, width), held(width, lanes)]
    scratch += [held(ranks, rows, lanes), held(ranks, rows, 2 * lanes)]
    return comm_call(
        front_kernel, "front", 1, tuple(shapes), [ANY] * 2 + [IN_VMEM] * 3 + [ANY] * 7, (ANY,) * len(shapes),
        scratch, FRONT_SEMS[0], FRONT_SEMS[1],
    )(tokens, cotangent, gain1, gain2, places, w_query, w_key, w_value, w_out, w_gate, w_up, w_down)


def attend_back_block(number, prompt, qs, ks, vs, gs, kt, ot_ref, lse_ref, dqs, dks, dvs):
    start = number * CONT
    own = slice(start, start + CONT)
    query, grad = qs[own, :], gs[own, :]
    product = grad.astype(F32).T * ot_ref[:, own].astype(F32)
    outs = []
    for head in range(2):
        rows = slice(head * HEAD, (head + 1) * HEAD)
        delta = jnp.sum(product[rows], axis=0, keepdims=True)
        lse = lse_ref[head : head + 1, own]
        keep = head_mask(CONT, head)
        query_head = jnp.where(keep, query, jnp.zeros_like(query))
        grad_head = jnp.where(keep, grad, jnp.zeros_like(grad))
        dq = None
        for keys in [own] + ([slice(0, min(start, prompt))] if start else []):
            prob = jnp.exp(dot_nt(ks[keys, :], query_head) - lse)
            if keys == own:
                prob = jnp.where(causal_mask(), prob, 0.0)
            dprob = dot_nt(vs[keys, :], grad_head)
            dscore = (prob * (dprob - delta)).astype(BF16)
            dvs[keys, :] += matmul(prob.astype(BF16), grad_head)
            dks[keys, :] += matmul(dscore, query_head)
            term = matmul(kt[rows, keys], dscore)
            dq = term if dq is None else dq + term
        outs.append(dq)
    dqs[own, :] = (jnp.concatenate(outs, axis=0) * SCALE).T.astype(BF16)


def rear_kernel(
    table, summed_in, h1_in, cot_in, x_in, line_in, n1_in, mix_in, wqkv_in, wo_in,
    q_in, k_in, v_in, ot_in, lse_in, att_in, gu_ref, down_ref, gusum_in,
    out_ref, grad_ref, gains_ref, gate_end, up_end, q_end, k_end, v_end, wo_all, wd_end,
    *rest,
):
    scratch, other, rest = rest[:4], rest[4:8], rest[8:]
    summed_ref, h1_ref, cot_ref, x_ref, line_ref, wqkv_ref, wo_ref, rest = *rest[:7], rest[7:]
    qs, ks, vs, ot_ref, lse_ref, att_ref, rest = *rest[:6], rest[6:]
    gate_out, up_out, q_out, k_out, v_out, wd_out, rest = *rest[:6], rest[6:]
    n1s, mix, parts, gas, datt, gs, kt, dqs, dks, dvs, dqkv, w_t, rest = *rest[:12], rest[12:]
    dh1, summed, mixed, low, low_tok, low_out, rest = *rest[:6], rest[6:]
    recv_gu, sum_gu, gu_all, gqkv, recv_qkv, sum_qkv, qkv_all, gwo, rest = *rest[:8], rest[8:]
    mid_wo, recv_wo, sum_wo, recv_wd, sum_wd, down_all, own, recv_gain, sum_gain, plane, *sems = rest
    copies = Copies(sems)
    total, heads = att_ref.shape
    ranks = PLANE * CORES
    chunk, width = x_ref.shape[1], x_ref.shape[2]
    rows = PLANE * chunk
    share = down_ref.shape[2]
    hidden = PLANE * share
    lanes = gu_ref.shape[2] // 2

    def load(*pairs):
        return [copies.keep(source, target) for source, target in pairs]

    first = load((summed_in, summed_ref), (h1_in, h1_ref), (cot_in, cot_ref), (line_in, line_ref))
    second_load = load((k_in, ks), (wqkv_in, wqkv_ref), (wo_in, wo_ref))
    third = load((mix_in, mix))
    fourth = load((q_in, qs), (v_in, vs), (ot_in, ot_ref), (lse_in, lse_ref), (x_in, x_ref))
    fifth = load((n1_in, n1s), (att_in, att_ref), (gusum_in, sum_gu.at[:, :, pl.ds(0, EARLY)]))
    stores = []
    copies.greet(crossing=True)
    finished(first)
    gain = gains_of(line_ref, 1)
    gain2_sum = jnp.zeros((1, width), F32)
    for n in range(PLANE):
        part = slice(n * chunk, (n + 1) * chunk)
        back, by_gain = norm_back(summed_ref[part], h1_ref[part], gain)
        grad = cot_ref[n].astype(F32) + back
        gain2_sum = gain2_sum + by_gain
        dh1[part] = grad
        low[part] = grad.astype(BF16)
    copies.welcome()
    gather = gather_stream(copies, low, gas)
    next(gather)
    gate_up = column_grads_stream(copies, gu_ref, recv_gu, sum_gu, pl.ds(EARLY, 2 * lanes - EARLY))
    next(gate_up)
    down = sum_stream(copies, down_ref, recv_wd, sum_wd)
    next(down)
    finished(second_load)
    for start in range(0, total, CONT):
        part = slice(start, start + CONT)
        kt[:, part] = ks[part, :].astype(F32).T.astype(BF16)
    for s in range(ranks):
        w_t[:, s * heads : (s + 1) * heads] = wqkv_ref[s].T
    dks[...] = jnp.zeros_like(dks)
    dvs[...] = jnp.zeros_like(dvs)

    def slot_rows(slot):
        return pl.ds(pl.multiple_of(slot * rows, rows), rows)

    def attended_grad(slot):
        datt[slot_rows(slot), :] = outer(gas[slot], wo_ref[...]).astype(BF16)

    next(gather)
    finished(third)
    mixing = copies.branch()
    second = Scatter(mixing, mix, mixed, other)
    second.share(0, 1, 2, 3)
    each_slot("own", attended_grad)
    next(gather)
    next(gather)
    next(gather)
    next(gather)
    each_slot("near", attended_grad)
    next(gather)()
    second.far()
    second.side()
    second.over()
    next(gather)
    each_slot("far", attended_grad)
    finished(fourth)
    finished(fifth)
    grad = jnp.zeros((heads, width), F32)
    for slot in range(ranks):
        grad = grad + inner(att_ref[slot * rows : (slot + 1) * rows, :], gas[slot])
    gwo[...] = grad.astype(BF16)
    out_w = row_grads_stream(copies, gwo, mid_wo, recv_wo, sum_wo, wo_all)
    next(out_w)
    in_place_order(table, datt, slice(0, heads), gs)
    for number in range(total // CONT):
        attend_back_block(number, total // 2, qs, ks, vs, gs, kt, ot_ref, lse_ref, dqs, dks, dvs)
        if number == 3:
            second.cross()
        if number == 4:
            next(gate_up)
            gather_gu = gather_stream(copies, sum_gu, gu_all, twin=False)
            next(gather_gu)
        if number == 6:
            next(out_w)
    ks_low, vs_low = gs, datt
    for start in range(0, total, CONT):
        part = slice(start, start + CONT)
        ks_low[part, :] = dks[part, :].astype(BF16)
        vs_low[part, :] = dvs[part, :].astype(BF16)
    for n, ref in enumerate((dqs, ks_low, vs_low)):
        in_gathered_order(table, ref, dqkv, slice(n * heads, (n + 1) * heads))

    def spread(slot):
        parts[slot] = matmul(dqkv[slot_rows(slot), :], w_t[...]).astype(BF16)

    scatter = Scatter(copies, parts, summed, scratch)
    each_slot("far", spread)
    scatter.share(0)
    each_slot("near", spread)
    scatter.share(1, 2)
    scatter.far()
    each_slot("own", spread)
    scatter.share(3)
    scatter.side()
    scatter.over()
    next(gather_gu)
    next(gather_gu)
    second.end()
    for n in range(PLANE):
        part = slice(n * chunk, (n + 1) * chunk)
        low_out[n] = (h1_ref[part] + mixed[part]).astype(BF16)
    output = Outward(copies, low_out, out_ref)

    def by_rows(s):
        columns = pl.ds(pl.multiple_of(s * heads, heads), heads)
        grad = jnp.zeros((heads, 3 * heads), F32)
        for slot in range(ranks):
            grad = grad + inner(n1s[slot, :, columns], dqkv[slot * rows : (slot + 1) * rows, :])
        gqkv[s] = grad.astype(BF16)

    pl.loop(0, ranks)(by_rows)
    qkv = column_grads_stream(copies, gqkv, recv_qkv, sum_qkv, pl.ds(0, 3 * heads))
    next(qkv)
    scatter.cross()
    next(down)
    gather_down = gather_stream(copies, sum_wd, down_all, twin=False)
    next(gather_down)
    next(out_w)
    drain(gather_gu)

    def format_gate(chip, c, z):
        begin, at = (CORES * z + c) * hidden + chip * share, z * share
        gate_out[:, begin : begin + share] = gu_all[chip, c, :, at : at + share]
        up_out[:, begin : begin + share] = gu_all[chip, c, :, lanes + at : lanes + at + share]

    for chip in range(PLANE):
        for c in range(CORES):
            for z in range(PLANE):
                format_gate(chip, c, z)
    stores += load((gate_out, gate_end), (up_out, up_end))
    scatter.end()
    gain = gains_of(line_ref, 0)
    gain1_sum = jnp.zeros((1, width), F32)
    for n in range(PLANE):
        part = slice(n * chunk, (n + 1) * chunk)
        back, by_gain = norm_back(summed[part], x_ref[n].astype(F32), gain)
        gain1_sum = gain1_sum + by_gain
        low_tok[n] = (dh1[part] + back).astype(BF16)
    tokens = Outward(copies, low_tok, grad_ref)
    own[...] = jnp.zeros_like(own)
    for s in range(ranks):
        part = slice(s * heads, (s + 1) * heads)
        own[s, 0:1] = gain1_sum[:, part]
        own[s, 1:2] = gain2_sum[:, part]
    gains = gain_grads_stream(copies, own, recv_gain, sum_gain, plane, gains_ref)
    next(gains)
    next(gather_down)
    next(gather_down)
    next(qkv)
    gather_qkv = gather_stream(copies, sum_qkv, qkv_all, twin=False)
    next(gather_qkv)
    next(gather_qkv)
    next(gather_qkv)
    drain(gather_down)
    for chip in range(PLANE):
        for h in range(2):
            wd_out[chip * share : (chip + 1) * share, h * (width // 2) : (h + 1) * (width // 2)] = down_all[chip, h]
    stores += load((wd_out, wd_end))
    next(gather_qkv)
    next(gather_qkv)
    next(gains)
    drain(gather_qkv)
    for chip in range(PLANE):
        for c in range(CORES):
            begin = (CORES * chip + c) * heads
            for n, ref in enumerate((q_out, k_out, v_out)):
                ref[:, begin : begin + heads] = qkv_all[chip, c, :, n * heads : (n + 1) * heads]
    stores += load((q_out, q_end), (k_out, k_end), (v_out, v_end))
    next(out_w)
    next(gains)
    output.wait()
    tokens.wait()
    copies.finish()
    finished(stores)


def rear(table, summed, h1, cot, x, lines, n1, mixed, w_qkv, w_o, qs, ks, vs, ot, lse, att, gate_up_grad, down_grad, gate_up_sum, ff):
    ranks = PLANE * CORES
    rows, width = h1.shape
    total, heads = att.shape
    hidden = PLANE * down_grad.shape[2]
    quarter = width // PLANE
    small = lines.shape[1:]
    low = lambda *shape: jax.ShapeDtypeStruct(shape, BF16)
    shapes = (
        low(rows, width), low(rows, width), jax.ShapeDtypeStruct(small, F32),
        low(heads, ff), low(heads, ff), low(heads, width), low(heads, width), low(heads, width),
        low(heads, width), low(hidden, width),
    )
    held = lambda *shape: pltpu.VMEM(shape, BF16)
    wide = lambda *shape: pltpu.VMEM(shape, F32)
    scratch = scatter_scratch(rows, width) * 2
    scratch += [pltpu.VMEM(a.shape, a.dtype) for a in (summed, h1, cot, x, lines, w_qkv, w_o, qs, ks, vs, ot, lse, att)]
    scratch += [held(*shapes[n].shape) for n in (3, 4, 5, 6, 7, 9)]
    scratch += [held(*n1.shape)] * 4 + [held(total, heads)] * 2 + [held(heads, total), held(total, heads)]
    scratch += [wide(total, heads)] * 2 + [held(total, 3 * heads), held(3 * heads, width)]
    scratch += [wide(rows, width)] * 3 + [held(rows, width)] + [held(*x.shape)] * 2
    for grad in (gate_up_grad, w_qkv):
        piece = (CORES,) + grad.shape[1:]
        if grad is w_qkv:
            scratch += [held(*grad.shape)]
        columns = grad.shape[2] - (0 if grad is w_qkv else EARLY)
        scratch += [held(CORES, PLANE, grad.shape[1], columns), held(*piece), held(PLANE, *piece)]
    scratch += [held(heads, width)]
    scratch += [held(PLANE, heads, quarter)] * 2 + [held(heads, quarter)]
    scratch += [held(*down_grad.shape), held(*down_grad.shape[1:]), held(*down_grad.shape)]
    scratch += [wide(*lines.shape)] * 2 + [wide(*small), wide(PLANE, *small)]
    return comm_call(
        rear_kernel, "rear", 2, shapes,
        [pl.BlockSpec(memory_space=pltpu.SMEM)] + [ANY] * 18,
        (ANY, ANY, IN_VMEM) + (ANY,) * 7,
        scratch, REAR_SEMS[0], REAR_SEMS[1],
    )(
        table, summed, h1, cot, x, lines, n1, mixed, w_qkv, w_o, qs, ks, vs, ot, lse, att,
        gate_up_grad, down_grad, gate_up_sum,
    )


def finish_kernel(*refs):
    count = (len(refs) - 1) // 4
    inputs, outputs, held, stage = (refs[n * count : (n + 1) * count] for n in range(4))
    sems = refs[-1]
    loads, stores = [], []
    for n, (source, buffer) in enumerate(zip(inputs, held)):
        loads.append(pltpu.make_async_copy(source, buffer, sems.at[0, n]))
        loads[-1].start()
    for n, (target, buffer, wide) in enumerate(zip(outputs, held, stage)):
        loads[n].wait()
        if buffer.shape != target.shape:
            wide[...] = buffer[n - len(inputs) + 2 : n - len(inputs) + 3, :]
            buffer = wide
        elif buffer.dtype != target.dtype:
            wide[...] = buffer[...].astype(F32)
            buffer = wide
        stores.append(pltpu.make_async_copy(buffer, target, sems.at[1, n]))
        stores[-1].start()
    for copy in stores:
        copy.wait()


def finish(tokens, grads, gains):
    inputs = list(tokens) + list(grads) + [gains] * 2
    shapes = [jax.ShapeDtypeStruct(a.shape, a.dtype) for a in tokens]
    shapes += [jax.ShapeDtypeStruct(a.shape, F32) for a in grads]
    shapes += [jax.ShapeDtypeStruct((1, gains.shape[1]), F32)] * 2
    held = [pltpu.VMEM(a.shape, a.dtype) for a in inputs]
    stage = [pltpu.VMEM((8, 128), F32)] * len(tokens) + [pltpu.VMEM(a.shape, F32) for a in shapes[len(tokens) :]]
    return pl.pallas_call(
        finish_kernel,
        out_shape=tuple(shapes),
        in_specs=[ANY] * len(inputs),
        out_specs=(ANY,) * len(inputs),
        scratch_shapes=held + stage + [pltpu.SemaphoreType.DMA((2, len(inputs)))],
        compiler_params=pltpu.CompilerParams(vmem_limit_bytes=60 << 20),
        name="finish",
    )(*inputs)


def plane_local(
    tokens,
    cotangent,
    block_table,
    norm1_gain,
    w_query,
    w_key,
    w_value,
    w_out,
    norm2_gain,
    w_gate,
    w_up,
    w_down,
):
    (
        n1, x, cot, gains, w_qkv, w_o, qs, ks, vs, ot, lse, att, h1, dn2, mixed, g_gu, g_down, gu_sum, table
    ) = front(
        tokens[0], cotangent[0], norm1_gain[None], norm2_gain[None], block_table,
        w_query, w_key, w_value, w_out, w_gate, w_up, w_down,
    )
    output, tokens_grad, gain_grads, *grads = rear(
        table, dn2, h1, cot, x, gains, n1, mixed, w_qkv, w_o, qs, ks, vs, ot, lse, att, g_gu, g_down, gu_sum,
        w_gate.shape[1],
    )
    output, tokens_grad, gate, up, query, key, value, out, down, gain1, gain2 = finish(
        (output, tokens_grad), grads, gain_grads
    )
    return (
        output[None], tokens_grad[None],
        gain1[0], query, key, value, out, gain2[0], gate, up, down,
    )


def plane_solution(mesh):
    split = Mesh(mesh.devices.reshape(PLANE, PLANE, CORES), ("group", "z", "core"))
    ctx = ("z", "core")
    token, weight = P("group", ctx, None), P(ctx, None)
    in_specs = (token, token, P("group", None), P(ctx)) + (weight,) * 4 + (P(ctx),) + (weight,) * 3
    out_specs = (token, token, P(ctx)) + (weight,) * 4 + (P(ctx),) + (weight,) * 3
    return jax.shard_map(
        plane_local, mesh=split, in_specs=in_specs, out_specs=out_specs, check_vma=False
    )


def family_solution(mesh):
    in_specs = (
        P("group", "ctx", None),
        P("group", "ctx", None),
        P("group", None),
        P("ctx"),
        P("ctx", None),
        P("ctx", None),
        P("ctx", None),
        P("ctx", None),
        P("ctx"),
        P("ctx", None),
        P("ctx", None),
        P("ctx", None),
    )
    out_specs = (
        P("group", "ctx", None),
        P("group", "ctx", None),
        P("ctx"),
        P("ctx", None),
        P("ctx", None),
        P("ctx", None),
        P("ctx", None),
        P("ctx"),
        P("ctx", None),
        P("ctx", None),
        P("ctx", None),
    )
    return jax.shard_map(local, mesh=mesh, in_specs=in_specs, out_specs=out_specs, check_vma=False)


def solution(mesh):
    groups, ranks = mesh.shape["group"], mesh.shape["ctx"]
    if groups == PLANE and ranks == 2 * PLANE:
        return plane_solution(mesh)
    return family_solution(mesh)
```

```python
import jax
import jax.numpy as jnp
from jax import lax
from jax.experimental import pallas as pl
from jax.experimental.pallas import tpu as pltpu
from jax.sharding import Mesh
from jax.sharding import PartitionSpec as P

HEADS = 16
HEAD = 64
BLK = 128
KEYBLK = 512
PROMPT_MAX = 2048
CONT = 256


EPS = 1e-06
SCALE = 0.125


def rms_scale(hidden, gain):
    return hidden * lax.rsqrt(jnp.mean(hidden * hidden, axis=-1, keepdims=True) + EPS) * gain


def gated(gate, upper):
    return jax.nn.gelu(gate, approximate=True) * upper


def matmul(left, right):
    return jnp.dot(left, right, preferred_element_type=jnp.float32)


def inner(left, right):
    return lax.dot_general(
        left, right, (((0,), (0,)), ((), ())), preferred_element_type=jnp.float32
    )


def outer(left, right):
    return lax.dot_general(
        left, right, (((1,), (1,)), ((), ())), preferred_element_type=jnp.float32
    )


def family_index(table):
    offsets = jnp.arange(BLK, dtype=jnp.int32)
    return (table[:, None] * BLK + offsets[None, :]).reshape(-1)


def segment_of(index, prompt_len):
    return jnp.where(index < prompt_len, 0, 1 + (index - prompt_len) // CONT)


def allowed(query_index, key_index, prompt_len):
    query_seg = segment_of(query_index, prompt_len)
    key_seg = segment_of(key_index, prompt_len)
    same = (query_seg[:, None] == key_seg[None, :]) & (key_index[None, :] <= query_index[:, None])
    prompt = (key_seg[None, :] == 0) & (query_seg[:, None] > 0)
    return same | prompt


def head_split(block):
    return block.reshape(block.shape[0], HEADS, HEAD)


def scores_of(query_heads, key_block, query_index, key_index, prompt_len):
    score = (
        jnp.einsum(
            "qhd,khd->hqk", query_heads, head_split(key_block), preferred_element_type=jnp.float32
        )
        * SCALE
    )
    return (score, allowed(query_index, key_index, prompt_len))


def attend_stats(queries, keys, query_index, key_index, prompt_len):
    query_heads = head_split(queries)

    def step(carry, number):
        best, total = carry
        start = number * KEYBLK
        key_block = lax.dynamic_slice_in_dim(keys, start, KEYBLK, 0)
        block_index = lax.dynamic_slice_in_dim(key_index, start, KEYBLK, 0)
        score, keep = scores_of(query_heads, key_block, query_index, block_index, prompt_len)
        score = jnp.where(keep[None], score, -1e30)
        larger = jnp.maximum(best, jnp.max(score, axis=-1))
        terms = jnp.where(keep[None], jnp.exp(score - larger[:, :, None]), 0.0)
        total = total * jnp.exp(best - larger) + jnp.sum(terms, axis=-1)
        return ((larger, total), None)

    start_best = jnp.full((HEADS, queries.shape[0]), -1e30, jnp.float32)
    (best, total), ignored = lax.scan(
        step, (start_best, jnp.zeros_like(start_best)), jnp.arange(keys.shape[0] // KEYBLK)
    )
    return best + jnp.log(total)


def attend_values(queries, keys, values, lse, query_index, key_index, prompt_len):
    query_heads = head_split(queries)

    def step(acc, number):
        start = number * KEYBLK
        key_block = lax.dynamic_slice_in_dim(keys, start, KEYBLK, 0)
        value_block = lax.dynamic_slice_in_dim(values, start, KEYBLK, 0)
        block_index = lax.dynamic_slice_in_dim(key_index, start, KEYBLK, 0)
        score, keep = scores_of(query_heads, key_block, query_index, block_index, prompt_len)
        prob = jnp.where(keep[None], jnp.exp(score - lse[:, :, None]), 0.0).astype(jnp.bfloat16)
        return (
            acc
            + jnp.einsum(
                "hqk,khd->qhd", prob, head_split(value_block), preferred_element_type=jnp.float32
            ),
            None,
        )

    start_acc = jnp.zeros((queries.shape[0], HEADS, HEAD), jnp.float32)
    acc, ignored = lax.scan(step, start_acc, jnp.arange(keys.shape[0] // KEYBLK))
    return acc.reshape(queries.shape[0], HEADS * HEAD)


def block_grads(query_heads, grad_heads, key_block, value_block, lse, delta, keep):
    key_heads = head_split(key_block)
    value_heads = head_split(value_block)
    score = (
        jnp.einsum("qhd,khd->hqk", query_heads, key_heads, preferred_element_type=jnp.float32)
        * SCALE
    )
    prob = jnp.where(keep[None], jnp.exp(score - lse[:, :, None]), 0.0)
    dvalue = jnp.einsum(
        "hqk,qhd->khd", prob.astype(jnp.bfloat16), grad_heads, preferred_element_type=jnp.float32
    )
    dprob = jnp.einsum("qhd,khd->hqk", grad_heads, value_heads, preferred_element_type=jnp.float32)
    dscore = (prob * (dprob - delta[:, :, None])).astype(jnp.bfloat16)
    dquery = (
        jnp.einsum("hqk,khd->qhd", dscore, key_heads, preferred_element_type=jnp.float32) * SCALE
    )
    dkey = (
        jnp.einsum("hqk,qhd->khd", dscore, query_heads, preferred_element_type=jnp.float32) * SCALE
    )
    return (dquery, dkey, dvalue)


def local(
    tokens,
    cotangent,
    block_table,
    norm1_gain,
    w_query,
    w_key,
    w_value,
    w_out,
    norm2_gain,
    w_gate,
    w_up,
    w_down,
):
    row_count = tokens.shape[1]
    width = tokens.shape[2]
    every_index = family_index(block_table[0])
    prompt_len = min(PROMPT_MAX, every_index.shape[0] // 2)
    own_index = lax.dynamic_slice_in_dim(
        every_index, lax.axis_index("ctx") * row_count, row_count, 0
    )
    gain1, wq_full, wk_full, wv_full, wo_full = (
        lax.all_gather(norm1_gain, "ctx", axis=0, tiled=True),
        lax.all_gather(w_query, "ctx", axis=0, tiled=True),
        lax.all_gather(w_key, "ctx", axis=0, tiled=True),
        lax.all_gather(w_value, "ctx", axis=0, tiled=True),
        lax.all_gather(w_out, "ctx", axis=0, tiled=True),
    )
    inputs = tokens[0].astype(jnp.float32)
    normed1, norm1_pull = jax.vjp(rms_scale, inputs, gain1.astype(jnp.float32))
    first_low = normed1.astype(jnp.bfloat16)
    queries = matmul(first_low, wq_full).astype(jnp.bfloat16)
    keys_own = matmul(first_low, wk_full).astype(jnp.bfloat16)
    values_own = matmul(first_low, wv_full).astype(jnp.bfloat16)
    keys_all, values_all = (
        lax.all_gather(keys_own, "ctx", axis=0, tiled=True),
        lax.all_gather(values_own, "ctx", axis=0, tiled=True),
    )
    lse = attend_stats(queries, keys_all, own_index, every_index, prompt_len)
    attended_wide = attend_values(
        queries, keys_all, values_all, lse, own_index, every_index, prompt_len
    )
    attended = attended_wide.astype(jnp.bfloat16)
    hidden = inputs + matmul(attended, wo_full)
    gain2, wg_full, wu_full, wd_full = (
        lax.all_gather(norm2_gain, "ctx", axis=0, tiled=True),
        lax.all_gather(w_gate, "ctx", axis=0, tiled=True),
        lax.all_gather(w_up, "ctx", axis=0, tiled=True),
        lax.all_gather(w_down, "ctx", axis=0, tiled=True),
    )
    normed2, norm2_pull = jax.vjp(rms_scale, hidden, gain2.astype(jnp.float32))
    second_low = normed2.astype(jnp.bfloat16)
    gate = matmul(second_low, wg_full)
    upper = matmul(second_low, wu_full)
    mixed_wide, gate_pull = jax.vjp(gated, gate, upper)
    mixed = mixed_wide.astype(jnp.bfloat16)
    result = hidden + matmul(mixed, wd_full)
    output = result.astype(jnp.bfloat16)[None]
    grad_low = cotangent[0]
    grad_down = inner(mixed, grad_low)
    dmixed = outer(grad_low, wd_full)
    dgate, dupper = gate_pull(dmixed)
    dgate_low = dgate.astype(jnp.bfloat16)
    dupper_low = dupper.astype(jnp.bfloat16)
    grad_gate = inner(second_low, dgate_low)
    grad_up = inner(second_low, dupper_low)
    dnormed2 = outer(dgate_low, wg_full) + outer(dupper_low, wu_full)
    dhidden_norm, grad_gain2 = norm2_pull(dnormed2)
    dhidden = grad_low.astype(jnp.float32) + dhidden_norm
    attn_low = dhidden.astype(jnp.bfloat16)
    grad_out_w = inner(attended, attn_low)
    dattended = outer(attn_low, wo_full).astype(jnp.bfloat16)
    delta = jnp.sum(
        (dattended.astype(jnp.float32) * attended_wide).reshape(row_count, HEADS, HEAD), axis=-1
    ).T
    query_heads = head_split(queries)
    grad_heads = head_split(dattended)

    def key_step(carry, number):
        start = number * KEYBLK
        key_block = lax.dynamic_slice_in_dim(keys_all, start, KEYBLK, 0)
        value_block = lax.dynamic_slice_in_dim(values_all, start, KEYBLK, 0)
        block_index = lax.dynamic_slice_in_dim(every_index, start, KEYBLK, 0)
        keep = allowed(own_index, block_index, prompt_len)
        dquery, dkey, dvalue = block_grads(
            query_heads, grad_heads, key_block, value_block, lse, delta, keep
        )
        joined = jnp.concatenate(
            [dkey.reshape(KEYBLK, width), dvalue.reshape(KEYBLK, width)], axis=1
        )
        return (carry + dquery, joined)

    start_query = jnp.zeros((row_count, HEADS, HEAD), jnp.float32)
    query_sum, key_terms = lax.scan(
        key_step, start_query, jnp.arange(every_index.shape[0] // KEYBLK)
    )
    summed = lax.psum_scatter(
        key_terms.reshape(every_index.shape[0], 2 * width).astype(jnp.bfloat16),
        "ctx",
        scatter_dimension=0,
        tiled=True,
    ).astype(jnp.float32)
    query_grad = query_sum.reshape(row_count, width)
    key_grad = summed[:, :width]
    value_grad = summed[:, width:]
    query_low = query_grad.astype(jnp.bfloat16)
    key_low = key_grad.astype(jnp.bfloat16)
    value_low = value_grad.astype(jnp.bfloat16)
    grad_query = inner(first_low, query_low)
    grad_key = inner(first_low, key_low)
    grad_value = inner(first_low, value_low)
    dnormed1 = outer(query_low, wq_full) + outer(key_low, wk_full) + outer(value_low, wv_full)
    dinput_norm, grad_gain1 = norm1_pull(dnormed1)
    tokens_grad = (dhidden + dinput_norm).astype(jnp.bfloat16)[None]
    shards = (
        lax.psum_scatter(
            grad_gain1.astype(jnp.bfloat16), "ctx", scatter_dimension=0, tiled=True
        ).astype(jnp.float32),
        lax.psum_scatter(
            grad_query.astype(jnp.bfloat16), "ctx", scatter_dimension=0, tiled=True
        ).astype(jnp.float32),
        lax.psum_scatter(
            grad_key.astype(jnp.bfloat16), "ctx", scatter_dimension=0, tiled=True
        ).astype(jnp.float32),
        lax.psum_scatter(
            grad_value.astype(jnp.bfloat16), "ctx", scatter_dimension=0, tiled=True
        ).astype(jnp.float32),
        lax.psum_scatter(
            grad_out_w.astype(jnp.bfloat16), "ctx", scatter_dimension=0, tiled=True
        ).astype(jnp.float32),
        lax.psum_scatter(
            grad_gain2.astype(jnp.bfloat16), "ctx", scatter_dimension=0, tiled=True
        ).astype(jnp.float32),
        lax.psum_scatter(
            grad_gate.astype(jnp.bfloat16), "ctx", scatter_dimension=0, tiled=True
        ).astype(jnp.float32),
        lax.psum_scatter(
            grad_up.astype(jnp.bfloat16), "ctx", scatter_dimension=0, tiled=True
        ).astype(jnp.float32),
        lax.psum_scatter(
            grad_down.astype(jnp.bfloat16), "ctx", scatter_dimension=0, tiled=True
        ).astype(jnp.float32),
    )
    shards = (
        lax.psum(shards[0].astype(jnp.bfloat16), "group").astype(jnp.float32),
        lax.psum(shards[1].astype(jnp.bfloat16), "group").astype(jnp.float32),
        lax.psum(shards[2].astype(jnp.bfloat16), "group").astype(jnp.float32),
        lax.psum(shards[3].astype(jnp.bfloat16), "group").astype(jnp.float32),
        lax.psum(shards[4].astype(jnp.bfloat16), "group").astype(jnp.float32),
        lax.psum(shards[5].astype(jnp.bfloat16), "group").astype(jnp.float32),
        lax.psum(shards[6].astype(jnp.bfloat16), "group").astype(jnp.float32),
        lax.psum(shards[7].astype(jnp.bfloat16), "group").astype(jnp.float32),
        lax.psum(shards[8].astype(jnp.bfloat16), "group").astype(jnp.float32),
    )
    return (
        output,
        tokens_grad,
        shards[0],
        shards[1],
        shards[2],
        shards[3],
        shards[4],
        shards[5],
        shards[6],
        shards[7],
        shards[8],
    )


PLANE = 4
CORES = 2
TP = ("group", "core")
F32 = jnp.float32
BF16 = jnp.bfloat16


def dot_nt(left, right):
    return lax.dot_general(left, right, (((1,), (1,)), ((), ())), preferred_element_type=F32)


def head_mask(rows, head):
    lane = lax.broadcasted_iota(jnp.int32, (rows, 2 * HEAD), 1)
    return (lane >= head * HEAD) & (lane < (head + 1) * HEAD)


def causal_mask():
    key = lax.broadcasted_iota(jnp.int32, (CONT, CONT), 0)
    query = lax.broadcasted_iota(jnp.int32, (CONT, CONT), 1)
    return key <= query


MESH = pl.DeviceIdType.MESH
EARLY = 256
FRONT_SEMS = (126, 137)
REAR_SEMS = (114, 104)


def spots():
    chip, line, core = lax.axis_index("group"), lax.axis_index("z"), lax.axis_index("core")
    side = chip + 1 - 2 * lax.rem(chip, 2)
    over = lax.rem(chip + 2, PLANE)
    far = PLANE - 1 - chip
    return chip, line, core, side, over, far


def plane_partners():
    chip, line, core, side, over, far = spots()
    return [(q, line, core) for q in (far, side, over)]


def line_partners():
    chip, line, core, side, over, far = spots()
    lines = [lax.rem(line + d, PLANE) for d in range(1, PLANE)]
    same = [(chip, z, core) for z in lines]
    return same + [(chip, z, 1 - core) for z in lines] + [(chip, line, 1 - core)]


class Kept:
    def __init__(self, copies, copy, held):
        self.copies, self.copy, self.held = copies, copy, held
        copy.start()

    def wait(self):
        self.copy.wait()
        self.copies.root().free.extend(self.held)


class Copies:
    def __init__(self, sems, parent=None):
        self.sems, self.parent = sems, parent
        self.counts, self.free, self.started, self.branches = [0, 0], [], [], []

    def branch(self):
        self.branches.append(Copies(self.sems, self))
        return self.branches[-1]

    def number(self, side=0):
        if self.parent is not None:
            return self.parent.number(side)
        self.counts[side] += 1
        return self.counts[side] - 1

    def root(self):
        return self if self.parent is None else self.parent.root()

    def left(self, held=None):
        free = self.root().free
        number = free.pop() if held is not None and free else self.number(0)
        if held is not None:
            held.append(number)
        return self.sems[0].at[number]

    def greet(self, crossing=False):
        barrier = pltpu.get_barrier_semaphore()
        partners = plane_partners() + line_partners()
        chip, line, core, side, over, far = spots()
        if crossing:
            partners += [(line, lax.rem(line + d, PLANE), core) for d in range(1, PLANE)]
            partners += [(lax.rem(chip + d, PLANE), chip, core) for d in range(1, PLANE)]

        def signal(partner):
            pl.semaphore_signal(barrier, inc=1, device_id=partner, device_id_type=MESH)

        for partner in partners:
            signal(partner)
        if crossing:
            @pl.when(chip != line)
            def _():
                signal((line, line, core))
                signal((chip, chip, core))

        self.crossing, self.expected = crossing, len(partners)

    def welcome(self):
        barrier = pltpu.get_barrier_semaphore()
        if not self.crossing:
            pl.semaphore_wait(barrier, self.expected)
            return
        away = lax.axis_index("group") != lax.axis_index("z")

        @pl.when(away)
        def _():
            pl.semaphore_wait(barrier, self.expected + 2)

        @pl.when(jnp.logical_not(away))
        def _():
            pl.semaphore_wait(barrier, self.expected)

    def send(self, source, target, partner, start=True):
        held = []
        copy = pltpu.make_async_remote_copy(
            src_ref=source,
            dst_ref=target,
            send_sem=self.left(held),
            recv_sem=self.sems[1].at[self.number(1)],
            device_id=partner,
            device_id_type=MESH,
        )
        if start:
            copy.start()
        self.started.append((copy, held))
        return copy

    def keep(self, source, target):
        held = []
        return Kept(self, pltpu.make_async_copy(source, target, self.left(held)), held)

    def finish(self):
        for copy, held in self.started:
            copy.wait_send()
            self.root().free.extend(held)
        self.started = []
        for branch in self.branches:
            branch.finish()


def arrived(copies):
    for copy in copies:
        copy.wait_recv()


def finished(copies):
    for copy in copies:
        copy.wait()


def gather_stream(copies, own_ref, out_ref, twin=True):
    chip, line, core, side, over, far = spots()
    half = own_ref.shape[0] // 2
    to_far, to_side, to_over = plane_partners()
    to_twin = (chip, line, 1 - core)

    def slot_of(q):
        return CORES * q + core if twin else q

    def part(slot, number):
        return out_ref.at[slot, pl.ds(number * half, half)]

    def own(number):
        return own_ref.at[pl.ds(number * half, half)]

    def on(slot, number, partner):
        return copies.send(part(slot, number), part(slot, number), partner)

    def share(slot, number):
        return [on(slot, number, to_twin)] if twin else []

    mine, slot_side, slot_over, slot_far = map(slot_of, (chip, side, over, far))
    sides, overs = [None, None], [None, None]
    overs[0] = copies.send(own(0), part(mine, 0), to_over)
    sides[1] = copies.send(own(1), part(mine, 1), to_side)
    sides[0] = copies.send(own(0), part(mine, 0), to_side)
    overs[1] = copies.send(own(1), part(mine, 1), to_over)
    twins = [copies.send(own(h), part(mine, h), to_twin) for h in range(2)] if twin else []
    local = copies.keep(own_ref, out_ref.at[mine])
    yield
    local.wait()
    arrived(twins)
    yield
    overs[0].wait_recv()
    far0 = on(slot_over, 0, to_side)
    twins = share(slot_over, 0)
    sides[1].wait_recv()
    far1 = on(slot_side, 1, to_over)
    twins += share(slot_side, 1)
    yield
    arrived(twins)
    yield
    sides[0].wait_recv()
    twins = share(slot_side, 0)
    overs[1].wait_recv()
    twins += share(slot_over, 1)
    yield
    arrived(twins)
    yield
    twins = [
        copies.send(part(slot_far, h), part(slot_far, h), to_twin, start=False)
        for h in range(2 if twin else 0)
    ]

    def pass_on():
        for number, copy in enumerate((far0, far1)):
            copy.wait_recv()
            if twin:
                twins[number].start()

    yield pass_on
    arrived(twins)
    yield


class Scatter:
    def __init__(self, copies, part_ref, out_ref, scratch):
        self.copies, self.part_ref, self.out_ref = copies, part_ref, out_ref
        self.twin, self.from_side, self.from_over, self.go = scratch
        chip, line, self.core, side, over, far = spots()
        self.half = out_ref.shape[0] // 2
        ignored, self.to_side, self.to_over = plane_partners()
        self.to_twin = (chip, line, 1 - self.core)
        self.chips = (far, side, over, chip)
        self.twins = [None] * 4

    def share(self, *numbers, start=True):
        for n in numbers:
            self.twins[n] = []
            for h in range(2):
                rows = pl.ds(h * self.half, self.half)
                source = self.part_ref.at[CORES * self.chips[n] + 1 - self.core, rows]
                self.twins[n].append(self.copies.send(source, self.twin.at[n, rows], self.to_twin, start))

    def share_between(self, n, slot_of, body):
        self.share(n, start=False)

        @pl.loop(0, CORES)
        def _(number):
            @pl.when(number == 1)
            def _():
                for copy in self.twins[n]:
                    copy.start()

            body(slot_of(number))

    def _pair(self, n, h):
        part = slice(h * self.half, (h + 1) * self.half)
        self.twins[n][h].wait_recv()
        own = self.part_ref[CORES * self.chips[n] + self.core, part]
        return own.astype(F32) + self.twin[n, part].astype(F32)

    def _send(self, n, h, value, target, partner):
        self.go[n, h * self.half : (h + 1) * self.half] = value.astype(BF16)
        return self.copies.send(self.go.at[n, pl.ds(h * self.half, self.half)], target, partner)

    def far(self):
        self.far0 = self._send(0, 0, self._pair(0, 0), self.from_side.at[0], self.to_side)
        self.far1 = self._send(0, 1, self._pair(0, 1), self.from_over.at[0], self.to_over)

    def side(self):
        self.side0 = self._send(1, 0, self._pair(1, 0), self.from_side.at[1], self.to_side)

    def over(self):
        self.over1 = self._send(2, 1, self._pair(2, 1), self.from_over.at[2], self.to_over)

    def cross(self):
        value = self._pair(2, 0)
        self.far0.wait_recv()
        value = value + self.from_side[0].astype(F32)
        self.over0 = self._send(2, 0, value, self.from_over.at[1], self.to_over)
        value = self._pair(1, 1)
        self.far1.wait_recv()
        value = value + self.from_over[0].astype(F32)
        self.side1 = self._send(1, 1, value, self.from_side.at[2], self.to_side)

    def end(self):
        first, second = self._pair(3, 0), self._pair(3, 1)
        self.side0.wait_recv()
        first = first + self.from_side[1].astype(F32)
        self.over1.wait_recv()
        second = second + self.from_over[2].astype(F32)
        self.over0.wait_recv()
        self.out_ref[0 : self.half] = first + self.from_over[1].astype(F32)
        self.side1.wait_recv()
        self.out_ref[self.half :] = second + self.from_side[2].astype(F32)


def drain(gather):
    for step in gather:
        if step is not None:
            step()


def scatter_scratch(rows, width):
    return [
        pltpu.VMEM((PLANE, rows, width), BF16),
        pltpu.VMEM((3, rows // 2, width), BF16),
        pltpu.VMEM((3, rows // 2, width), BF16),
        pltpu.VMEM((3, rows, width), BF16),
    ]


def inward_stream(copies, own_ref, mid, out_ref):
    chip, line, core, side, over, far = spots()
    chunk = own_ref.shape[0] // PLANE
    half = chunk // 2
    sent, moved, local = [[], []], [], []
    for h in range(2):
        part = pl.ds(h * half, half)
        for q in plane_partners():
            rows = own_ref.at[pl.ds(q[0] * chunk + h * half, half)]
            sent[h].append(copies.send(rows, mid.at[chip, part], q))
    local = [copies.keep(own_ref.at[pl.ds(chip * chunk, chunk)], mid.at[chip])]
    yield
    finished(local)
    for h in range(2):
        part = pl.ds(h * half, half)
        arrived(sent[h])
        for q in line_partners()[: PLANE - 1]:
            moved.append(copies.send(mid.at[q[1], part], out_ref.at[line, part], q))
    local = copies.keep(mid.at[line], out_ref.at[line])
    yield
    arrived(moved)
    local.wait()
    yield


class Outward:
    def __init__(self, copies, own_ref, out_ref):
        self.chip, self.line, self.core = (lax.axis_index(name) for name in ("group", "z", "core"))
        self.copies, self.chunk, self.out_ref = copies, own_ref.shape[1], out_ref
        self.arrive = [copies.number(1) for ignored in range(PLANE)]
        self.sends, self.away = [], self.chip != self.line
        for d in range(PLANE):
            z = lax.rem(self.line + d, PLANE)
            copy = self._copy(own_ref.at[z], self.chip, z, copies.left())
            self.sends.append(copy)
            if d:
                copy.start()
        self.local = pltpu.make_async_copy(
            own_ref.at[self.line], self._rows(self.chip), copies.left()
        )

        @pl.when(self.away)
        def _():
            self.sends[0].start()

        @pl.when(self.chip == self.line)
        def _():
            self.local.start()

    def _rows(self, chip):
        return self.out_ref.at[pl.ds(pl.multiple_of(chip * self.chunk, self.chunk), self.chunk)]

    def _copy(self, source, chip, z, left):
        return pltpu.make_async_remote_copy(
            src_ref=source,
            dst_ref=self._rows(chip),
            send_sem=left,
            recv_sem=self.copies.sems[1].at[self.arrive[0] + chip],
            device_id=(self.line, z, self.core),
            device_id_type=MESH,
        )

    def wait(self):
        for chip in range(PLANE):
            copy = self._copy(self._rows(chip), chip, self.line, self.copies.sems[0].at[0])

            @pl.when((chip != self.chip) | self.away)
            def _():
                copy.wait_recv()

        @pl.when(self.chip == self.line)
        def _():
            self.local.wait()

        @pl.when(self.away)
        def _():
            self.sends[0].wait_send()

        for copy in self.sends[1:]:
            copy.wait_send()


def columns_stream(copies, piece_ref, out_ref, lanes):
    chip, line, core, side, over, far = spots()
    mine = out_ref.at[CORES * line + core, :, lanes]
    sent = [copies.send(piece_ref.at[q[2], :, lanes], mine, q) for q in line_partners()]
    local = copies.keep(piece_ref.at[core, :, lanes], mine)
    yield
    arrived(sent)
    local.wait()
    yield


class Relay:
    def __init__(self, copies, piece, slot, both=True):
        self.line, self.core = lax.axis_index("z"), lax.axis_index("core")
        self.copies, self.slot, self.both = copies, slot, both
        self.cores = range(CORES) if both else (self.core,)
        self.twin = None
        count = PLANE * CORES if both else PLANE
        self.arrive = [copies.number(1) for ignored in range(count)]
        self.sends = []
        mine = slot(self.line, self.core)
        if both:
            self.twin = self._copy(piece(1 - self.core), mine, self.line, self.core, self.line, 1 - self.core, copies.left())
            self.twin.start()
        self.local = copies.keep(piece(self.core), mine)
        for step in (1, -1):
            for core in self.cores:
                copy = self._copy(piece(core), mine, self.line, self.core, self.line + step, core, copies.left())
                self._start(self._inside(self.line + step), copy)

    def _inside(self, z):
        return (z >= 0) & (z < PLANE)

    def _sem(self, z, core):
        number = CORES * z + core if self.both else z
        return self.copies.sems[1].at[self.arrive[0] + number]

    def _copy(self, source, target, z, core, to, to_core, left=None):
        return pltpu.make_async_remote_copy(
            src_ref=source,
            dst_ref=target,
            send_sem=self.copies.sems[0].at[0] if left is None else left,
            recv_sem=self._sem(z, core),
            device_id=(lax.axis_index("group"), to, to_core),
            device_id_type=MESH,
        )

    def _start(self, when, copy):
        @pl.when(when)
        def _():
            copy.start()

        self.sends.append((when, copy))

    def hop(self, distance):
        if distance == 1:
            self.local.wait()
            if self.both:
                self._copy(*[self.slot(self.line, 1 - self.core)] * 2, self.line, 1 - self.core, self.line, self.core).wait_recv()
        for step in (1, -1):
            z = self.line - step * distance
            there, on = self._inside(z), self._inside(z) & self._inside(self.line + step)
            for core in self.cores:
                slot = self.slot(jnp.clip(z, 0, PLANE - 1), core)
                left = self.copies.left() if distance < PLANE - 1 else None
                copy = self._copy(slot, slot, jnp.clip(z, 0, PLANE - 1), core, self.line + step, self.core, left)

                @pl.when(there)
                def _():
                    copy.wait_recv()

                if distance < PLANE - 1:
                    self._start(on, copy)

    def finish(self):
        if self.both:
            self.twin.wait_send()
        for when, copy in self.sends:
            @pl.when(when)
            def _():
                copy.wait_send()


def columns_relay(copies, piece_ref, out_ref, lanes):
    return Relay(
        copies,
        lambda core: piece_ref.at[core, :, lanes],
        lambda z, core: out_ref.at[CORES * z + core, :, lanes],
    )


def sum_stream(copies, grad_ref, recv, sum_ref):
    chip, line, core, side, over, far = spots()
    sent = [
        copies.send(grad_ref.at[q[1]], recv.at[line], q) for q in line_partners()[: PLANE - 1]
    ]
    local = copies.keep(grad_ref.at[line], recv.at[line])
    yield
    arrived(sent)
    local.wait()
    total = recv[0].astype(F32)
    for family in range(1, PLANE):
        total = total + recv[family].astype(F32)
    sum_ref[...] = total.astype(BF16)
    yield


def quarter_columns(ref, number):
    width = ref.shape[1] // PLANE
    return ref.at[:, pl.ds(pl.multiple_of(number * width, width), width)]


def to_ranks_stream(copies, mid, out_ref):
    chip, line, core, side, over, far = spots()
    target = quarter_columns(out_ref, chip)
    sent = [copies.send(mid.at[q[0]], target, q) for q in plane_partners()]
    local = copies.keep(mid.at[chip], target)
    yield
    arrived(sent)
    local.wait()
    yield


def unit_rows(value):
    inverse = lax.rsqrt(jnp.mean(value * value, axis=-1, keepdims=True) + EPS)
    return value * inverse, inverse


def comm_call(kernel, name, number, out_shape, in_specs, out_specs, scratch, sends, arrivals, vmem_mib=60):
    return pl.pallas_call(
        kernel,
        out_shape=out_shape,
        in_specs=in_specs,
        out_specs=out_specs,
        scratch_shapes=scratch + [pltpu.SemaphoreType.DMA((sends,)), pltpu.SemaphoreType.DMA((arrivals,))],
        compiler_params=pltpu.CompilerParams(
            collective_id=number, has_side_effects=True, vmem_limit_bytes=vmem_mib << 20
        ),
        name=name,
    )


ANY = pl.BlockSpec(memory_space=pl.ANY)
IN_VMEM = pl.BlockSpec(memory_space=pltpu.VMEM)


def gains_of(line_ref, row):
    return jnp.concatenate([line_ref[s, row : row + 1, :] for s in range(line_ref.shape[0])], axis=1)


def column_grads_stream(copies, grad_ref, recv, sum_ref, lanes):
    chip, line, core, side, over, far = spots()
    sent = [
        copies.send(grad_ref.at[CORES * q[1] + q[2], :, lanes], recv.at[core, line], q)
        for q in line_partners()
    ]
    local = copies.keep(grad_ref.at[CORES * line + core, :, lanes], recv.at[core, line])
    yield
    arrived(sent)
    local.wait()
    for number in range(CORES):
        total = recv[number, 0].astype(F32)
        for family in range(1, PLANE):
            total = total + recv[number, family].astype(F32)
        sum_ref[number, :, lanes] = total.astype(BF16)
    yield


def row_grads_stream(copies, grad_ref, mid, recv, summed, out_ref):
    chip, line, core, side, over, far = spots()
    width = out_ref.shape[1] // PLANE

    def quarter(q):
        return pl.ds(pl.multiple_of(q * width, width), width)

    sent = [copies.send(grad_ref.at[:, quarter(q[0])], mid.at[chip], q) for q in plane_partners()]
    local = copies.keep(grad_ref.at[:, quarter(chip)], mid.at[chip])
    yield
    local.wait()
    arrived(sent)
    sent = [copies.send(mid.at[q[1]], recv.at[line], q) for q in line_partners()[: PLANE - 1]]
    local = copies.keep(mid.at[line], recv.at[line])
    yield
    arrived(sent)
    local.wait()
    total = recv[0].astype(F32)
    for family in range(1, PLANE):
        total = total + recv[family].astype(F32)
    summed[...] = total.astype(BF16)
    sent = [copies.send(summed, out_ref.at[:, quarter(chip)], q) for q in plane_partners()]
    local = copies.keep(summed, out_ref.at[:, quarter(chip)])
    yield
    arrived(sent)
    local.wait()
    yield


def gain_grads_stream(copies, own, recv, summed, plane, out_ref):
    chip, line, core, side, over, far = spots()
    mine = CORES * line + core
    sent = [copies.send(own.at[CORES * q[1] + q[2]], recv.at[mine], q) for q in line_partners()]
    local = copies.keep(own.at[mine], recv.at[mine])
    yield
    arrived(sent)
    local.wait()
    summed[...] = jnp.sum(recv[...], axis=0)
    sent = [copies.send(summed, plane.at[chip], q) for q in plane_partners()]
    local = copies.keep(summed, plane.at[chip])
    yield
    arrived(sent)
    local.wait()
    out_ref[...] = jnp.sum(plane[...], axis=0)
    yield


def norm_back(grad, value, gain):
    unit, inverse = unit_rows(value)
    scaled = grad * gain
    back = inverse * (scaled - unit * jnp.mean(scaled * unit, axis=-1, keepdims=True))
    return back, jnp.sum(grad * unit, axis=0, keepdims=True)


TABLE_ROW = 2


def chunk_row(stored, part, chunk):
    plane, core, line = 2 * (stored % 2) + part, (stored // 2) % 2, stored // 4
    return ((plane * CORES + core) * PLANE + line) * chunk


def chosen(blocks, flags):
    value = blocks[0]
    for block, flag in zip(blocks[1:], flags[1:]):
        value = jnp.where(flag, block, value)
    return value


def in_place_order(table_ref, source, lanes, target, scale=None):
    chunk = BLK // 2
    blocks = source.shape[0] // BLK
    for place in range(blocks):
        flags = [table_ref[TABLE_ROW, stored] == float(place) for stored in range(blocks)]
        for part in range(2):
            rows = [chunk_row(stored, part, chunk) for stored in range(blocks)]
            block = chosen([source[row : row + chunk, lanes] for row in rows], flags)
            row = place * BLK + part * chunk
            target[row : row + chunk, :] = block if scale is None else block * scale


def in_gathered_order(table_ref, source, target, lanes):
    chunk = BLK // 2
    blocks = source.shape[0] // BLK
    for stored in range(blocks):
        flags = [table_ref[TABLE_ROW, stored] == float(place) for place in range(blocks)]
        for part in range(2):
            rows = [place * BLK + part * chunk for place in range(blocks)]
            block = chosen([source[row : row + chunk, :] for row in rows], flags)
            row = chunk_row(stored, part, chunk)
            target[row : row + chunk, lanes] = block


def attend_block(number, prompt, qs, ks, vt, att, ot_ref, lse_ref):
    start = number * CONT
    before = min(start, prompt)
    own_rows = slice(start, start + CONT)
    query = qs[own_rows, :]
    outs = []
    for head in range(2):
        masked = jnp.where(head_mask(CONT, head), query, jnp.zeros_like(query))
        own = dot_nt(ks[own_rows, :], masked)
        own = jnp.where(causal_mask(), own, -1e30)
        best = jnp.max(own, axis=0, keepdims=True)
        if before:
            past = dot_nt(ks[0:before, :], masked)
            best = jnp.maximum(best, jnp.max(past, axis=0, keepdims=True))
        terms = jnp.exp(own - best)
        total_terms = jnp.sum(terms, axis=0, keepdims=True)
        rows = slice(head * HEAD, (head + 1) * HEAD)
        out = matmul(vt[rows, own_rows], terms.astype(BF16))
        if before:
            terms = jnp.exp(past - best)
            total_terms = total_terms + jnp.sum(terms, axis=0, keepdims=True)
            out = out + matmul(vt[rows, 0:before], terms.astype(BF16))
        outs.append(out / total_terms)
        lse_ref[head : head + 1, own_rows] = best + jnp.log(total_terms)
    joined = jnp.concatenate(outs, axis=0)
    ot_ref[:, own_rows] = joined.astype(BF16)
    att[own_rows, :] = joined.T.astype(BF16)


def chip_slots(group):
    chip, line, core, side, over, far = spots()
    if group == "near":
        return 2 * CORES, lambda n: CORES * (side + lax.div(n, CORES) * (over - side)) + lax.rem(n, CORES)
    q = {"own": chip, "far": far}[group]
    return CORES, lambda n: CORES * q + lax.rem(core + 1 + n, CORES)


def each_slot(group, body):
    count, slot_of = chip_slots(group)

    @pl.loop(0, count)
    def _(n):
        body(slot_of(n))


def front_kernel(
    tok_ref, cot_ref, gain1_ref, gain2_ref, place_ref, wq_ref, wk_ref, wv_ref, wo_ref, wg_ref, wu_ref, wd_ref,
    n1_out, x_out, cot_out, line_out, wqkv_out, wo_out, q_out, k_out, v_out, ot_out, lse_out, att_out,
    h1_out, dn2_out, mix_out, ggu_out, gd_out, gusum_out, table_out,
    *rest,
):
    scratch, other, rest = rest[:4], rest[4:8], rest[8:]
    x_ref, cotp_ref, line_ref, wqkv, wout, qs, ks, vs, ot_ref, lse_ref, att_ref, rest = *rest[:11], rest[11:]
    h1_ref, dn2_ref, ggu_ref, gd_ref, gusum, rest = *rest[:5], rest[5:]
    small_ref, recv_gu, rest = *rest[:2], rest[2:]
    mid_x, mid_c, mid_o, down, tables, table, pieces, gate_w, up_w, gu, normed, rest = *rest[:11], rest[11:]
    n1s, n2s, cots, qkv, vt, att, parts, summed, wgu, wgu_t, wd, wd_t, us, dabs, *sems = rest
    copies = Copies(sems)
    chip, line, core, side, over, far = spots()
    total, heads = qkv.shape[0], wo_ref.shape[0]
    hidden, lanes = wd_ref.shape[0], wd.shape[0]
    chunk, width = x_ref.shape[1], x_ref.shape[2]
    rows = PLANE * chunk
    ranks = PLANE * CORES
    share = hidden // PLANE
    stores = []

    def store(source, target):
        stores.append(copies.keep(source, target))

    loads = [copies.keep(wg_ref, gate_w), copies.keep(wu_ref, up_w)]
    for c in range(CORES):
        column = pl.ds(pl.multiple_of((CORES * chip + c) * heads, heads), heads)
        for n, w in enumerate((wq_ref, wk_ref, wv_ref)):
            loads.append(copies.keep(w.at[:, column], pieces.at[c, :, n * heads : (n + 1) * heads]))
    copies.greet()
    small_ref[...] = jnp.zeros_like(small_ref)
    small_ref[0:1] = gain1_ref[...].astype(F32)
    small_ref[1:2] = gain2_ref[...].astype(F32)
    small_ref[TABLE_ROW : TABLE_ROW + 1, 0 : place_ref.shape[1]] = place_ref[...].astype(F32)
    copies.welcome()
    early = copies.branch()
    tokens = inward_stream(early, tok_ref, mid_x, x_ref)
    next(tokens)
    out_part = quarter_columns(wo_ref, chip)
    out_sent = [early.send(out_part, mid_o.at[line], q) for q in line_partners()[: PLANE - 1]]
    out_kept = copies.keep(out_part, mid_o.at[line])
    mine = CORES * line + core
    small = [early.send(small_ref, line_ref.at[mine], q) for q in line_partners()]
    small += [early.send(small_ref, tables.at[chip], q) for q in plane_partners()]
    local = [copies.keep(small_ref, line_ref.at[mine]), copies.keep(small_ref, tables.at[chip])]
    finished(loads)
    next(tokens)
    cotangents = inward_stream(early, cot_ref, mid_c, cotp_ref)
    next(cotangents)
    gu[...] = jnp.zeros_like(gu)
    for k in range(PLANE):
        @pl.when(chip == k)
        def _():
            for c in range(CORES):
                for z in range(PLANE):
                    begin, at = (CORES * z + c) * hidden + k * share, z * share
                    gu[c, :, at : at + share] = gate_w[:, begin : begin + share]
                    gu[c, :, lanes + at : lanes + at + share] = up_w[:, begin : begin + share]
    wd[hidden:lanes] = jnp.zeros((lanes - hidden, width), BF16)
    arrived(out_sent)
    out_kept.wait()
    out_rows = to_ranks_stream(early, mid_o, wout)
    next(out_rows)
    arrived(small)
    finished(local)
    load = [copies.keep(tables.at[line], table), copies.keep(tables.at[line], table_out)]
    store(line_ref, line_out)
    gain = gains_of(line_ref, 0)
    next(tokens)
    projections = columns_relay(copies, pieces, wqkv, pl.ds(0, 3 * heads))
    for n in range(PLANE):
        unit, ignored = unit_rows(x_ref[n].astype(F32))
        normed[n * chunk : (n + 1) * chunk] = (unit * gain).astype(BF16)
    gathering = copies.branch()
    gather = gather_stream(gathering, normed, n1s)
    next(gather)
    finished(load)
    next(gather)
    projections.hop(1)
    next(gather)
    projections.hop(2)
    next(gather)
    next(gather)
    next(cotangents)

    def slot_rows(slot):
        return pl.ds(pl.multiple_of(slot * rows, rows), rows)

    def project(slot):
        qkv[slot_rows(slot), :] = matmul(n1s[slot], wqkv[...].reshape(width, 3 * heads)).astype(BF16)

    next(gather)
    projections.hop(3)
    next(gather)()
    each_slot("own", project)
    each_slot("near", project)
    next(gather)
    each_slot("far", project)
    for source, target in ((n1s, n1_out), (x_ref, x_out), (wqkv, wqkv_out)):
        store(source, target)

    for n, ref in enumerate((qs, ks, vs)):
        scale = jnp.bfloat16(SCALE) if n == 0 else None
        in_place_order(table, qkv, slice(n * heads, (n + 1) * heads), ref, scale)
    next(cotangents)
    gather_cot = gather_stream(copies, cotp_ref.reshape(rows, width), cots)
    next(gather_cot)
    gate_up = columns_relay(copies, gu, wgu, pl.ds(0, 2 * lanes))
    down_part = wd_ref.at[pl.ds(pl.multiple_of(chip * share, 8), share)]
    down_rows = Relay(copies, lambda core: down_part, lambda z, core: down.at[z], False)
    for start in range(0, total, CONT):
        part = slice(start, start + CONT)
        vt[:, part] = vs[part, :].astype(F32).T.astype(BF16)
    for source, target in ((qs, q_out), (ks, k_out), (vs, v_out), (cotp_ref, cot_out)):
        store(source, target)
    for number in range(total // CONT):
        attend_block(number, total // 2, qs, ks, vt, att, ot_ref, lse_ref)
        if number == 5:
            next(gather_cot)
            next(gather_cot)
            next(gather_cot)
            gate_up.hop(1)
    in_gathered_order(table, att, att_ref, slice(0, heads))
    next(out_rows)

    def spread(slot):
        parts[slot] = matmul(att_ref[slot_rows(slot), :], wout[...]).astype(BF16)

    scattering = copies.branch()
    scatter = Scatter(scattering, parts, summed, scratch)
    each_slot("far", spread)
    scatter.share(0)
    each_slot("near", spread)
    scatter.share(1, 2)
    scatter.far()
    each_slot("own", spread)
    scatter.share(3)
    scatter.side()
    scatter.over()
    next(gather_cot)
    down_rows.hop(1)
    next(gather_cot)
    next(gather_cot)()
    gate_up.hop(2)
    down_rows.hop(2)
    for source, target in ((wout, wo_out), (ot_ref, ot_out), (lse_ref, lse_out), (att_ref, att_out)):
        store(source, target)
    scatter.cross()
    next(gather_cot)
    gate_up.hop(3)
    for s in range(ranks):
        wgu_t[:, s * heads : (s + 1) * heads] = wgu[s].T
    down_rows.hop(3)
    for z in range(PLANE):
        wd[z * share : (z + 1) * share] = down[z]
    wd_t[...] = wd[...].T
    early.finish()
    gathering.finish()
    gain = gains_of(line_ref, 1)
    scatter.end()
    for n in range(PLANE):
        part = slice(n * chunk, (n + 1) * chunk)
        hidden_rows = x_ref[n].astype(F32) + summed[part]
        h1_ref[part] = hidden_rows
        unit, ignored = unit_rows(hidden_rows)
        normed[part] = (unit * gain).astype(BF16)
    gather = gather_stream(copies, normed, n2s)
    next(gather)
    store(h1_ref, h1_out)
    next(gather)
    scattering.finish()
    finished(stores)
    stores.clear()

    def feed_rows(slot, at):
        block, cot = n2s[slot, at, :], cots[slot, at, :]
        both = matmul(block, wgu[...].reshape(width, 2 * lanes))
        gate, upper = both[:, :lanes], both[:, lanes:]
        bend = jnp.tanh(0.7978845608028654 * (gate + 0.044715 * gate * gate * gate))
        half = 0.5 * (1.0 + bend)
        active = gate * half
        slope = half + (0.5 * 0.7978845608028654) * gate * (1.0 - bend * bend) * (
            1.0 + 3 * 0.044715 * gate * gate
        )
        mixed = (active * upper).astype(BF16)
        us[slot, at, :] = mixed
        parts[slot, at, :] = matmul(mixed, wd[...]).astype(BF16)
        du = matmul(cot, wd_t[...])
        dabs[slot, at, 0:lanes] = (du * upper * slope).astype(BF16)
        dabs[slot, at, lanes:] = (du * active).astype(BF16)
        n1s[slot, at, :] = matmul(dabs[slot, at, :], wgu_t[...]).astype(BF16)

    def feed(slot):
        feed_rows(slot, pl.ds(0, rows))

    def feed_halves(which, between):
        count, slot_of = chip_slots("near")
        half = rows // 2

        @pl.loop(0, count)
        def _(n):
            @pl.when(n == count - 1)
            def _():
                between()

            number = 1 - lax.div(n, CORES) if which == 0 else lax.div(n, CORES)
            feed_rows(slot_of(n), pl.ds(pl.multiple_of(number * half, half), half))

    scatter = Scatter(copies, n1s, dn2_ref, other)
    each_slot("own", feed)
    scatter.share(3)
    next(gather)
    next(gather)
    feed_halves(0, lambda: None)
    next(gather)
    next(gather)
    feed_halves(1, next(gather))
    scatter.share(1, 2)
    next(gather)
    scatter.side()
    scatter.over()
    scatter.share_between(0, chip_slots("far")[1], feed)
    scatter.far()
    store(parts, mix_out)

    def by_rows(begin, size):
        @pl.loop(0, ranks)
        def _(s):
            columns = pl.ds(pl.multiple_of(s * heads, heads), heads)
            grad = jnp.zeros((heads, size), F32)
            for slot in range(ranks):
                grad = grad + inner(n2s[slot, :, columns], dabs[slot, :, begin : begin + size])
            ggu_ref[s, :, begin : begin + size] = grad.astype(BF16)

    by_rows(0, EARLY)
    columns = column_grads_stream(copies, ggu_ref, recv_gu, gusum, pl.ds(0, EARLY))
    next(columns)
    by_rows(EARLY, 2 * lanes - EARLY)
    store(ggu_ref, ggu_out)
    scatter.cross()
    grad = jnp.zeros((lanes, width), F32)
    for slot in range(ranks):
        grad = grad + inner(us[slot], cots[slot])
    for z in range(PLANE):
        for h in range(2):
            block = grad[z * share : (z + 1) * share, h * (width // 2) : (h + 1) * (width // 2)]
            gd_ref[z, h] = block.astype(BF16)
    store(gd_ref, gd_out)
    scatter.end()
    store(dn2_ref, dn2_out)
    next(columns)
    store(gusum, gusum_out)
    for relay in (projections, gate_up, down_rows):
        relay.finish()
    copies.finish()
    finished(stores)


def front(tokens, cotangent, gain1, gain2, places, w_query, w_key, w_value, w_out, w_gate, w_up, w_down):
    rows, width = tokens.shape
    heads, hidden = w_out.shape[0], w_down.shape[0]
    lanes = -(-hidden // 128) * 128
    ranks = PLANE * CORES
    total = ranks * rows
    small = (8, heads)
    chunks, blocks = (PLANE, rows // PLANE, width), (ranks, rows, width)
    low = lambda *shape: jax.ShapeDtypeStruct(shape, BF16)
    wide = lambda *shape: jax.ShapeDtypeStruct(shape, F32)
    held = [
        low(*chunks), low(*chunks), wide(ranks, *small), low(ranks, heads, 3 * heads),
        low(heads, width), low(total, heads), low(total, heads), low(total, heads), low(heads, total),
        wide(2, total), low(total, heads), wide(rows, width), wide(rows, width),
    ]
    grads = [low(ranks, heads, 2 * lanes), low(PLANE, 2, hidden // PLANE, width // 2), low(CORES, heads, EARLY)]
    shapes = [low(*blocks)] + held + [low(*blocks)] + grads + [wide(*small)]
    scratch = scatter_scratch(rows, width) * 2
    scratch += [pltpu.VMEM(a.shape, a.dtype) for a in held + grads]
    held = lambda *shape: pltpu.VMEM(shape, BF16)
    scratch += [pltpu.VMEM(small, F32), held(CORES, PLANE, heads, EARLY)]
    scratch += [held(*chunks), held(*chunks), held(PLANE, heads, width // PLANE), held(PLANE, hidden // PLANE, width)]
    scratch += [pltpu.VMEM((PLANE,) + small, F32), pltpu.SMEM(small, F32)]
    scratch += [held(CORES, heads, 3 * heads), held(*w_gate.shape), held(*w_up.shape), held(CORES, heads, 2 * lanes)]
    scratch += [held(rows, width), held(*blocks), held(*blocks), held(*blocks), held(total, 3 * heads)]
    scratch += [held(heads, total), held(total, heads), held(*blocks), pltpu.VMEM((rows, width), F32)]
    scratch += [held(ranks, heads, 2 * lanes), held(2 * lanes, width), held(lanes, width), held(width, lanes)]
    scratch += [held(ranks, rows, lanes), held(ranks, rows, 2 * lanes)]
    return comm_call(
        front_kernel, "front", 1, tuple(shapes), [ANY] * 2 + [IN_VMEM] * 3 + [ANY] * 7, (ANY,) * len(shapes),
        scratch, FRONT_SEMS[0], FRONT_SEMS[1],
    )(tokens, cotangent, gain1, gain2, places, w_query, w_key, w_value, w_out, w_gate, w_up, w_down)


def attend_back_block(number, prompt, qs, ks, vs, gs, kt, ot_ref, lse_ref, dqs, dks, dvs):
    start = number * CONT
    own = slice(start, start + CONT)
    query, grad = qs[own, :], gs[own, :]
    product = grad.astype(F32).T * ot_ref[:, own].astype(F32)
    outs = []
    for head in range(2):
        rows = slice(head * HEAD, (head + 1) * HEAD)
        delta = jnp.sum(product[rows], axis=0, keepdims=True)
        lse = lse_ref[head : head + 1, own]
        keep = head_mask(CONT, head)
        query_head = jnp.where(keep, query, jnp.zeros_like(query))
        grad_head = jnp.where(keep, grad, jnp.zeros_like(grad))
        dq = None
        for keys in [own] + ([slice(0, min(start, prompt))] if start else []):
            prob = jnp.exp(dot_nt(ks[keys, :], query_head) - lse)
            if keys == own:
                prob = jnp.where(causal_mask(), prob, 0.0)
            dprob = dot_nt(vs[keys, :], grad_head)
            dscore = (prob * (dprob - delta)).astype(BF16)
            dvs[keys, :] += matmul(prob.astype(BF16), grad_head)
            dks[keys, :] += matmul(dscore, query_head)
            term = matmul(kt[rows, keys], dscore)
            dq = term if dq is None else dq + term
        outs.append(dq)
    dqs[own, :] = (jnp.concatenate(outs, axis=0) * SCALE).T.astype(BF16)


def rear_kernel(
    table, summed_in, h1_in, cot_in, x_in, line_in, n1_in, mix_in, wqkv_in, wo_in,
    q_in, k_in, v_in, ot_in, lse_in, att_in, gu_ref, down_ref, gusum_in,
    out_ref, grad_ref, gains_ref, gate_end, up_end, q_end, k_end, v_end, wo_all, wd_end,
    *rest,
):
    scratch, other, rest = rest[:4], rest[4:8], rest[8:]
    summed_ref, h1_ref, cot_ref, x_ref, line_ref, wqkv_ref, wo_ref, rest = *rest[:7], rest[7:]
    qs, ks, vs, ot_ref, lse_ref, att_ref, rest = *rest[:6], rest[6:]
    gate_out, up_out, q_out, k_out, v_out, wd_out, rest = *rest[:6], rest[6:]
    n1s, mix, parts, gas, datt, gs, kt, dqs, dks, dvs, dqkv, w_t, rest = *rest[:12], rest[12:]
    dh1, summed, mixed, low, low_tok, low_out, rest = *rest[:6], rest[6:]
    recv_gu, sum_gu, gu_all, gqkv, recv_qkv, sum_qkv, qkv_all, gwo, rest = *rest[:8], rest[8:]
    mid_wo, recv_wo, sum_wo, recv_wd, sum_wd, down_all, own, recv_gain, sum_gain, plane, *sems = rest
    copies = Copies(sems)
    total, heads = att_ref.shape
    ranks = PLANE * CORES
    chunk, width = x_ref.shape[1], x_ref.shape[2]
    rows = PLANE * chunk
    share = down_ref.shape[2]
    hidden = PLANE * share
    lanes = gu_ref.shape[2] // 2

    def load(*pairs):
        return [copies.keep(source, target) for source, target in pairs]

    first = load((summed_in, summed_ref), (h1_in, h1_ref), (cot_in, cot_ref), (line_in, line_ref))
    second_load = load((k_in, ks), (wqkv_in, wqkv_ref), (wo_in, wo_ref))
    third = load((mix_in, mix))
    fourth = load((q_in, qs), (v_in, vs), (ot_in, ot_ref), (lse_in, lse_ref), (x_in, x_ref))
    fifth = load((n1_in, n1s), (att_in, att_ref), (gusum_in, sum_gu.at[:, :, pl.ds(0, EARLY)]))
    stores = []
    copies.greet(crossing=True)
    finished(first)
    gain = gains_of(line_ref, 1)
    gain2_sum = jnp.zeros((1, width), F32)
    for n in range(PLANE):
        part = slice(n * chunk, (n + 1) * chunk)
        back, by_gain = norm_back(summed_ref[part], h1_ref[part], gain)
        grad = cot_ref[n].astype(F32) + back
        gain2_sum = gain2_sum + by_gain
        dh1[part] = grad
        low[part] = grad.astype(BF16)
    copies.welcome()
    gather = gather_stream(copies, low, gas)
    next(gather)
    gate_up = column_grads_stream(copies, gu_ref, recv_gu, sum_gu, pl.ds(EARLY, 2 * lanes - EARLY))
    next(gate_up)
    down = sum_stream(copies, down_ref, recv_wd, sum_wd)
    next(down)
    finished(second_load)
    for start in range(0, total, CONT):
        part = slice(start, start + CONT)
        kt[:, part] = ks[part, :].astype(F32).T.astype(BF16)
    for s in range(ranks):
        w_t[:, s * heads : (s + 1) * heads] = wqkv_ref[s].T
    dks[...] = jnp.zeros_like(dks)
    dvs[...] = jnp.zeros_like(dvs)

    def slot_rows(slot):
        return pl.ds(pl.multiple_of(slot * rows, rows), rows)

    def attended_grad(slot):
        datt[slot_rows(slot), :] = outer(gas[slot], wo_ref[...]).astype(BF16)

    next(gather)
    finished(third)
    mixing = copies.branch()
    second = Scatter(mixing, mix, mixed, other)
    second.share(0, 1, 2, 3)
    each_slot("own", attended_grad)
    next(gather)
    next(gather)
    next(gather)
    next(gather)
    each_slot("near", attended_grad)
    next(gather)()
    second.far()
    second.side()
    second.over()
    next(gather)
    each_slot("far", attended_grad)
    finished(fourth)
    finished(fifth)
    grad = jnp.zeros((heads, width), F32)
    for slot in range(ranks):
        grad = grad + inner(att_ref[slot * rows : (slot + 1) * rows, :], gas[slot])
    gwo[...] = grad.astype(BF16)
    out_w = row_grads_stream(copies, gwo, mid_wo, recv_wo, sum_wo, wo_all)
    next(out_w)
    in_place_order(table, datt, slice(0, heads), gs)
    for number in range(total // CONT):
        attend_back_block(number, total // 2, qs, ks, vs, gs, kt, ot_ref, lse_ref, dqs, dks, dvs)
        if number == 3:
            second.cross()
        if number == 6:
            next(gate_up)
            gather_gu = gather_stream(copies, sum_gu, gu_all, twin=False)
            next(gather_gu)
            next(out_w)
    ks_low, vs_low = gs, datt
    for start in range(0, total, CONT):
        part = slice(start, start + CONT)
        ks_low[part, :] = dks[part, :].astype(BF16)
        vs_low[part, :] = dvs[part, :].astype(BF16)
    for n, ref in enumerate((dqs, ks_low, vs_low)):
        in_gathered_order(table, ref, dqkv, slice(n * heads, (n + 1) * heads))

    def spread(slot):
        parts[slot] = matmul(dqkv[slot_rows(slot), :], w_t[...]).astype(BF16)

    scatter = Scatter(copies, parts, summed, scratch)
    each_slot("far", spread)
    scatter.share(0)
    each_slot("near", spread)
    scatter.share(1, 2)
    scatter.far()
    each_slot("own", spread)
    scatter.share(3)
    scatter.side()
    scatter.over()
    next(gather_gu)
    next(gather_gu)
    second.end()
    for n in range(PLANE):
        part = slice(n * chunk, (n + 1) * chunk)
        low_out[n] = (h1_ref[part] + mixed[part]).astype(BF16)
    output = Outward(copies, low_out, out_ref)

    def by_rows(s):
        columns = pl.ds(pl.multiple_of(s * heads, heads), heads)
        grad = jnp.zeros((heads, 3 * heads), F32)
        for slot in range(ranks):
            grad = grad + inner(n1s[slot, :, columns], dqkv[slot * rows : (slot + 1) * rows, :])
        gqkv[s] = grad.astype(BF16)

    pl.loop(0, ranks)(by_rows)
    qkv = column_grads_stream(copies, gqkv, recv_qkv, sum_qkv, pl.ds(0, 3 * heads))
    next(qkv)
    scatter.cross()
    next(down)
    gather_down = gather_stream(copies, sum_wd, down_all, twin=False)
    next(gather_down)
    next(out_w)
    drain(gather_gu)

    def format_gate(chip, c, z):
        begin, at = (CORES * z + c) * hidden + chip * share, z * share
        gate_out[:, begin : begin + share] = gu_all[chip, c, :, at : at + share]
        up_out[:, begin : begin + share] = gu_all[chip, c, :, lanes + at : lanes + at + share]

    for chip in range(PLANE):
        for c in range(CORES):
            for z in range(PLANE):
                format_gate(chip, c, z)
    stores += load((gate_out, gate_end), (up_out, up_end))
    scatter.end()
    gain = gains_of(line_ref, 0)
    gain1_sum = jnp.zeros((1, width), F32)
    for n in range(PLANE):
        part = slice(n * chunk, (n + 1) * chunk)
        back, by_gain = norm_back(summed[part], x_ref[n].astype(F32), gain)
        gain1_sum = gain1_sum + by_gain
        low_tok[n] = (dh1[part] + back).astype(BF16)
    tokens = Outward(copies, low_tok, grad_ref)
    own[...] = jnp.zeros_like(own)
    for s in range(ranks):
        part = slice(s * heads, (s + 1) * heads)
        own[s, 0:1] = gain1_sum[:, part]
        own[s, 1:2] = gain2_sum[:, part]
    gains = gain_grads_stream(copies, own, recv_gain, sum_gain, plane, gains_ref)
    next(gains)
    next(gather_down)
    next(gather_down)
    next(qkv)
    gather_qkv = gather_stream(copies, sum_qkv, qkv_all, twin=False)
    next(gather_qkv)
    next(gather_qkv)
    next(gather_qkv)
    drain(gather_down)
    for chip in range(PLANE):
        for h in range(2):
            wd_out[chip * share : (chip + 1) * share, h * (width // 2) : (h + 1) * (width // 2)] = down_all[chip, h]
    stores += load((wd_out, wd_end))
    next(gather_qkv)
    next(gather_qkv)
    next(gains)
    drain(gather_qkv)
    for chip in range(PLANE):
        for c in range(CORES):
            begin = (CORES * chip + c) * heads
            for n, ref in enumerate((q_out, k_out, v_out)):
                ref[:, begin : begin + heads] = qkv_all[chip, c, :, n * heads : (n + 1) * heads]
    stores += load((q_out, q_end), (k_out, k_end), (v_out, v_end))
    next(out_w)
    next(gains)
    output.wait()
    tokens.wait()
    copies.finish()
    finished(stores)


def rear(table, summed, h1, cot, x, lines, n1, mixed, w_qkv, w_o, qs, ks, vs, ot, lse, att, gate_up_grad, down_grad, gate_up_sum, ff):
    ranks = PLANE * CORES
    rows, width = h1.shape
    total, heads = att.shape
    hidden = PLANE * down_grad.shape[2]
    quarter = width // PLANE
    small = lines.shape[1:]
    low = lambda *shape: jax.ShapeDtypeStruct(shape, BF16)
    shapes = (
        low(rows, width), low(rows, width), jax.ShapeDtypeStruct(small, F32),
        low(heads, ff), low(heads, ff), low(heads, width), low(heads, width), low(heads, width),
        low(heads, width), low(hidden, width),
    )
    held = lambda *shape: pltpu.VMEM(shape, BF16)
    wide = lambda *shape: pltpu.VMEM(shape, F32)
    scratch = scatter_scratch(rows, width) * 2
    scratch += [pltpu.VMEM(a.shape, a.dtype) for a in (summed, h1, cot, x, lines, w_qkv, w_o, qs, ks, vs, ot, lse, att)]
    scratch += [held(*shapes[n].shape) for n in (3, 4, 5, 6, 7, 9)]
    scratch += [held(*n1.shape)] * 4 + [held(total, heads)] * 2 + [held(heads, total), held(total, heads)]
    scratch += [wide(total, heads)] * 2 + [held(total, 3 * heads), held(3 * heads, width)]
    scratch += [wide(rows, width)] * 3 + [held(rows, width)] + [held(*x.shape)] * 2
    for grad in (gate_up_grad, w_qkv):
        piece = (CORES,) + grad.shape[1:]
        if grad is w_qkv:
            scratch += [held(*grad.shape)]
        columns = grad.shape[2] - (0 if grad is w_qkv else EARLY)
        scratch += [held(CORES, PLANE, grad.shape[1], columns), held(*piece), held(PLANE, *piece)]
    scratch += [held(heads, width)]
    scratch += [held(PLANE, heads, quarter)] * 2 + [held(heads, quarter)]
    scratch += [held(*down_grad.shape), held(*down_grad.shape[1:]), held(*down_grad.shape)]
    scratch += [wide(*lines.shape)] * 2 + [wide(*small), wide(PLANE, *small)]
    return comm_call(
        rear_kernel, "rear", 2, shapes,
        [pl.BlockSpec(memory_space=pltpu.SMEM)] + [ANY] * 18,
        (ANY, ANY, IN_VMEM) + (ANY,) * 7,
        scratch, REAR_SEMS[0], REAR_SEMS[1],
    )(
        table, summed, h1, cot, x, lines, n1, mixed, w_qkv, w_o, qs, ks, vs, ot, lse, att,
        gate_up_grad, down_grad, gate_up_sum,
    )


def finish_kernel(*refs):
    count = (len(refs) - 1) // 4
    inputs, outputs, held, stage = (refs[n * count : (n + 1) * count] for n in range(4))
    sems = refs[-1]
    loads, stores = [], []
    for n, (source, buffer) in enumerate(zip(inputs, held)):
        loads.append(pltpu.make_async_copy(source, buffer, sems.at[0, n]))
        loads[-1].start()
    for n, (target, buffer, wide) in enumerate(zip(outputs, held, stage)):
        loads[n].wait()
        if buffer.shape != target.shape:
            wide[...] = buffer[n - len(inputs) + 2 : n - len(inputs) + 3, :]
            buffer = wide
        elif buffer.dtype != target.dtype:
            wide[...] = buffer[...].astype(F32)
            buffer = wide
        stores.append(pltpu.make_async_copy(buffer, target, sems.at[1, n]))
        stores[-1].start()
    for copy in stores:
        copy.wait()


def finish(tokens, grads, gains):
    inputs = list(tokens) + list(grads) + [gains] * 2
    shapes = [jax.ShapeDtypeStruct(a.shape, a.dtype) for a in tokens]
    shapes += [jax.ShapeDtypeStruct(a.shape, F32) for a in grads]
    shapes += [jax.ShapeDtypeStruct((1, gains.shape[1]), F32)] * 2
    held = [pltpu.VMEM(a.shape, a.dtype) for a in inputs]
    stage = [pltpu.VMEM((8, 128), F32)] * len(tokens) + [pltpu.VMEM(a.shape, F32) for a in shapes[len(tokens) :]]
    return pl.pallas_call(
        finish_kernel,
        out_shape=tuple(shapes),
        in_specs=[ANY] * len(inputs),
        out_specs=(ANY,) * len(inputs),
        scratch_shapes=held + stage + [pltpu.SemaphoreType.DMA((2, len(inputs)))],
        compiler_params=pltpu.CompilerParams(vmem_limit_bytes=60 << 20),
        name="finish",
    )(*inputs)


def plane_local(
    tokens,
    cotangent,
    block_table,
    norm1_gain,
    w_query,
    w_key,
    w_value,
    w_out,
    norm2_gain,
    w_gate,
    w_up,
    w_down,
):
    (
        n1, x, cot, gains, w_qkv, w_o, qs, ks, vs, ot, lse, att, h1, dn2, mixed, g_gu, g_down, gu_sum, table
    ) = front(
        tokens[0], cotangent[0], norm1_gain[None], norm2_gain[None], block_table,
        w_query, w_key, w_value, w_out, w_gate, w_up, w_down,
    )
    output, tokens_grad, gain_grads, *grads = rear(
        table, dn2, h1, cot, x, gains, n1, mixed, w_qkv, w_o, qs, ks, vs, ot, lse, att, g_gu, g_down, gu_sum,
        w_gate.shape[1],
    )
    output, tokens_grad, gate, up, query, key, value, out, down, gain1, gain2 = finish(
        (output, tokens_grad), grads, gain_grads
    )
    return (
        output[None], tokens_grad[None],
        gain1[0], query, key, value, out, gain2[0], gate, up, down,
    )


def plane_solution(mesh):
    split = Mesh(mesh.devices.reshape(PLANE, PLANE, CORES), ("group", "z", "core"))
    ctx = ("z", "core")
    token, weight = P("group", ctx, None), P(ctx, None)
    in_specs = (token, token, P("group", None), P(ctx)) + (weight,) * 4 + (P(ctx),) + (weight,) * 3
    out_specs = (token, token, P(ctx)) + (weight,) * 4 + (P(ctx),) + (weight,) * 3
    return jax.shard_map(
        plane_local, mesh=split, in_specs=in_specs, out_specs=out_specs, check_vma=False
    )


def family_solution(mesh):
    in_specs = (
        P("group", "ctx", None),
        P("group", "ctx", None),
        P("group", None),
        P("ctx"),
        P("ctx", None),
        P("ctx", None),
        P("ctx", None),
        P("ctx", None),
        P("ctx"),
        P("ctx", None),
        P("ctx", None),
        P("ctx", None),
    )
    out_specs = (
        P("group", "ctx", None),
        P("group", "ctx", None),
        P("ctx"),
        P("ctx", None),
        P("ctx", None),
        P("ctx", None),
        P("ctx", None),
        P("ctx"),
        P("ctx", None),
        P("ctx", None),
        P("ctx", None),
    )
    return jax.shard_map(local, mesh=mesh, in_specs=in_specs, out_specs=out_specs, check_vma=False)


def solution(mesh):
    groups, ranks = mesh.shape["group"], mesh.shape["ctx"]
    if groups == PLANE and ranks == 2 * PLANE:
        return plane_solution(mesh)
    return family_solution(mesh)
```
